128 devices in a mesh: layer: 16 (over x, z_lo, core), dp: 8 (over z_hi, y).
Axes of the slice: x: 4, y: 4, z: 4 (z_hi: 2, z_lo: 2; z = z_hi * 2 + z_lo), core: 2. Of those that a mesh axis runs over, the one named last changes fastest.
Arguments:
- resid_in: bfloat16 [4, 256, 3584], P(None, 'dp'), may hold values from -6 to 6
- resid_out: bfloat16 [4, 256, 3584], P(None, ('layer', 'dp')), may hold values from -4 to 4
- encoder: bfloat16 [2, 3584, 32768], P(None, None, ('layer', 'dp')), may hold values from -0.09375 to 0.09375
- enc_bias: float32 [2, 32768], P(None, ('layer', 'dp')), may hold values from -3 to 3
- decoder: bfloat16 [5, 32768, 3584], P(None, ('layer', 'dp')), may hold values from -0.046875 to 0.046875
- active: int32 [4, 8, 32], replicated, may hold values from 0 to 127, all different within a row
Outputs:
- recon: bfloat16 [4, 256, 3584], P(None, ('layer', 'dp'))
- grad_encoder: bfloat16 [2, 3584, 32768], P(None, None, ('layer', 'dp'))
- grad_bias: float32 [2, 32768], P(None, ('layer', 'dp'))
- grad_decoder: bfloat16 [5, 32768, 3584], P(None, ('layer', 'dp'))
The draws below stay inside these ranges and needn't reach their ends.
Inputs may be any that keep to these rules, and one draw needn't show every extreme that they name: Row active[l, n] lists 32 different blocks of layer l, active for tokens n * 32 to (n + 1) * 32 - 1; every block number appears in at least one row of active, counting the rows of all layers together (not necessarily in a row of every layer).
All inputs are finite; a program needn't handle non-finite values.
Results may differ from the reference program's by a relative error of at most 0.0059.
Values may be sent and summed in bfloat16 or wider, within the bound.
No kernel may reach another device: no remote copies, remote signals or barrier semaphores. Data moves between devices by JAX's collectives and lax.ppermute only.
A program may use at most 128 MiB of HBM per device.

```python
import jax
import jax.numpy as jnp
from jax import lax

D = 3584
FEAT = 16384
BLOCK = 128
LAYERS = 4
PAIRS = 5
TOK_DEV = 32
TILES = 8
TOKENS = 256
ACTIVE = 32


def levels(stream_key, extent, cuts, low, top_value):
    def one(axis_at, parts):
        steps = jax.random.uniform(jax.random.fold_in(jax.random.fold_in(stream_key, 6), axis_at), (parts,), jnp.float32, low / len(cuts), top_value / len(cuts))
        return jnp.repeat(jnp.exp(steps), extent[axis_at] // parts).reshape((-1,) + (1,) * (len(extent) - axis_at - 1))

    loudness = one(*cuts[0])
    for cut in cuts[1:]:
        loudness = loudness * one(*cut)
    return loudness


def distinct(own_key, rows, number_of, top, lift):
    ranking = jax.random.permutation(jax.random.fold_in(own_key, 1), number_of)
    boost = ranking
    for power in range(3):
        boost = boost * boost // number_of
    boost = boost * lift // number_of
    tickets = jax.random.randint(jax.random.fold_in(own_key, 2), (rows, number_of), 0, 4096) + boost
    sure = jax.random.permutation(jax.random.fold_in(own_key, 3), rows)[jnp.arange(number_of) % rows]
    tickets = jnp.where(jnp.arange(rows)[:, None] == sure[None, :], 1 << 14, tickets)
    merit = tickets * number_of + jnp.arange(number_of)
    return lax.top_k(merit.astype(jnp.int32), top)[1].astype(jnp.int32)


def noise(rng, dims, scale, most, shards=(), kind=jnp.bfloat16):
    values = jax.random.normal(rng, dims, jnp.float32) * scale
    if len(shards) > 0:
        values = levels(rng, dims, shards, -0.22, 0.18) * values
    return jnp.clip(values, min=-most, max=most).astype(kind)


def setup_inputs(seed: int = 0) -> dict:
    arg_keys = jax.random.split(jax.random.key(seed), 7)
    resid_in = noise(arg_keys[0], (LAYERS, TOKENS, D), 1.0, 6.0, ((1, 8),))
    resid_out = noise(arg_keys[1], (LAYERS, TOKENS, D), 0.5, 4.0, ((1, 128),))
    encoder = noise(arg_keys[2], (2, D, 2 * FEAT), D ** -0.5, 0.09375, ((2, 128),))
    enc_bias = noise(arg_keys[3], (2, 2 * FEAT), 0.5, 3.0, ((1, 128),), jnp.float32)
    decoder = noise(arg_keys[4], (PAIRS, 2 * FEAT, D), FEAT ** -0.5, 0.046875, ((1, 128),))
    active = distinct(arg_keys[5], LAYERS * TILES, FEAT // BLOCK, ACTIVE, 4096).reshape((LAYERS, TILES, ACTIVE))
    return {"resid_in": resid_in, "resid_out": resid_out, "encoder": encoder, "enc_bias": enc_bias, "decoder": decoder, "active": active}


def pair_map(fold_side, pair_slot):
    if pair_slot >= LAYERS - fold_side:
        return 1, pair_slot - 1
    return 0, fold_side + pair_slot


def reference(resid_in, resid_out, encoder, enc_bias, decoder, active):
    block_ids = jnp.arange(FEAT // BLOCK, dtype=jnp.int32)
    decoded = jnp.zeros((LAYERS, TOKENS, D), jnp.float32)
    saved = []
    for fold_side in range(2):
        low_col = fold_side * FEAT
        high_col = low_col + FEAT
        layer_ids = [fold_side, LAYERS - 1 - fold_side]
        side_state = []
        for source_slot in range(2):
            layer_id = layer_ids[source_slot]
            inputs = resid_in[layer_id]
            pre_acts = jnp.dot(inputs, encoder[source_slot][:, low_col:high_col], preferred_element_type=jnp.float32) + enc_bias[source_slot, low_col:high_col]
            listed_hit = jnp.any(active[layer_id][:, :, None] == block_ids[None, None, :], axis=1).astype(jnp.float32)
            block_keep = jnp.repeat(jnp.repeat(listed_hit, TOK_DEV, axis=0), BLOCK, axis=1)
            positive = jnp.maximum(pre_acts, 0.0)
            feature_codes = (block_keep * positive * positive).astype(jnp.bfloat16)
            side_state.append((inputs, block_keep, positive, feature_codes))
        for pair_slot in range(PAIRS):
            source_slot, target_layer = pair_map(fold_side, pair_slot)
            decoded = decoded.at[target_layer].add(jnp.dot(side_state[source_slot][3], decoder[pair_slot][low_col:high_col], preferred_element_type=jnp.float32))
        saved.append(side_state)
    recon = decoded.astype(jnp.bfloat16)
    errors_all = (decoded - resid_out.astype(jnp.float32)).astype(jnp.bfloat16)
    enc_parts = []
    bias_parts = []
    dec_parts = []
    for fold_side in range(2):
        low_col = fold_side * FEAT
        high_col = low_col + FEAT
        back_codes = [jnp.zeros((TOKENS, FEAT), jnp.float32), jnp.zeros((TOKENS, FEAT), jnp.float32)]
        dec_side = []
        for pair_slot in range(PAIRS):
            source_slot, target_layer = pair_map(fold_side, pair_slot)
            codes_here = saved[fold_side][source_slot][3]
            dec_side.append(jnp.dot(codes_here.T, errors_all[target_layer], preferred_element_type=jnp.float32).astype(jnp.bfloat16))
            back_codes[source_slot] = back_codes[source_slot] + jnp.dot(errors_all[target_layer], decoder[pair_slot][low_col:high_col].T, preferred_element_type=jnp.float32)
        dec_parts.append(jnp.stack(dec_side))
        enc_side = []
        bias_side = []
        for source_slot in range(2):
            state = saved[fold_side][source_slot]
            back_pre = (back_codes[source_slot] * state[1] * (2.0 * state[2])).astype(jnp.bfloat16)
            enc_side.append(jnp.dot(state[0].T, back_pre, preferred_element_type=jnp.float32).astype(jnp.bfloat16))
            bias_side.append(jnp.sum(back_pre.astype(jnp.float32), axis=0))
        enc_parts.append(jnp.stack(enc_side))
        bias_parts.append(jnp.stack(bias_side))
    grad_encoder = jnp.concatenate(enc_parts, axis=2)
    grad_bias = jnp.concatenate(bias_parts, axis=1)
    grad_decoder = jnp.concatenate(dec_parts, axis=1)
    return recon, grad_encoder, grad_bias, grad_decoder
```

```python
import functools

import jax
import jax.numpy as jnp
from jax import lax
from jax.experimental import pallas as pl
from jax.experimental.pallas import tpu as pltpu
from jax.sharding import Mesh
from jax.sharding import PartitionSpec as P

FEAT = 16384
BLOCK = 128
LAYERS = 4
D = 3584
W = 256
HALF = 128
TILES = 8
HROW = 16
PAIRS = 5
GRID_AXES = ("y", "x", "zl", "zh")
DP = ("zh", "y")
ALL = ("x", "zl", "core", "zh", "y")
BF = jnp.bfloat16
F32 = jnp.float32
SWAP = [(0, 1), (1, 0)]

SLOT = ((0, 0, 0, 0, 1), (0, 0, 0, 1, 1))
TARGET = ((0, 1, 2, 3, 3), (1, 2, 3, 2, 3))
FIRST = (((0, 1), (1, 1), (2, 1), (3, 1)), ((0, 0), (0, 1), (1, 1), (2, 1)))
SECOND = (((4, 0), (4, 0), (4, 0), (4, 1)), ((3, 0), (3, 0), (3, 1), (4, 1)))


def _tables(side):
    rows = []
    for s in range(2):
        rows.append(
            [p for p, _ in FIRST[s]]
            + [v for _, v in FIRST[s]]
            + [p for p, _ in SECOND[s]]
            + [v for _, v in SECOND[s]]
            + list(SLOT[s])
            + list(TARGET[s])
        )
    return jnp.where(side == 0, jnp.array(rows[0], jnp.int32), jnp.array(rows[1], jnp.int32))


T_FIRST, T_FV, T_SECOND, T_SV, T_SLOT, T_TARGET = 0, 4, 8, 12, 16, 21


def _rows(ref):
    v = ref[...]
    return v.reshape(TILES * HROW, v.shape[-1])


def _encode_kernel(own_ref, oth_ref, enc_ref, bias_ref, keep_ref, codes_ref, slope_ref, acc_ref):
    c = pl.program_id(1)
    x = jnp.concatenate([_rows(own_ref), _rows(oth_ref)], axis=0)
    part = jnp.dot(x, enc_ref[0], preferred_element_type=F32)

    @pl.when(c == 0)
    def _():
        acc_ref[...] = part

    @pl.when(c > 0)
    def _():
        acc_ref[...] += part

    @pl.when(c == pl.num_programs(1) - 1)
    def _():
        positive = jnp.maximum(acc_ref[...] + bias_ref[0], 0.0)
        keep = jnp.broadcast_to(keep_ref[0][:, None, :], (TILES, HROW, W)).reshape(HALF, W)
        keep = jnp.concatenate([keep, keep], axis=0)
        kept = keep * positive
        codes_ref[0] = (kept * positive).astype(BF)
        slope_ref[0] = 2.0 * kept


def _encode(own, oth, encoder, bias, keep):
    chunk = 896
    xspec = pl.BlockSpec((TILES, None, HROW, chunk), lambda k, c: (0, k, 0, c))
    return pl.pallas_call(
        _encode_kernel,
        grid=(2, D // chunk),
        in_specs=[
            xspec,
            xspec,
            pl.BlockSpec((1, chunk, W), lambda k, c: (k, c, 0)),
            pl.BlockSpec((1, 1, W), lambda k, c: (k, 0, 0)),
            pl.BlockSpec((1, TILES, W), lambda k, c: (k, 0, 0)),
        ],
        out_specs=[
            pl.BlockSpec((1, 2 * HALF, W), lambda k, c: (k, 0, 0)),
            pl.BlockSpec((1, 2 * HALF, W), lambda k, c: (k, 0, 0)),
        ],
        out_shape=[
            jax.ShapeDtypeStruct((2, 2 * HALF, W), BF),
            jax.ShapeDtypeStruct((2, 2 * HALF, W), F32),
        ],
        scratch_shapes=[pltpu.VMEM((2 * HALF, W), F32)],
        compiler_params=pltpu.CompilerParams(vmem_limit_bytes=16 << 20),
        cost_estimate=pl.CostEstimate(
            flops=2 * 2 * 256 * D * W, bytes_accessed=2 * D * W * 2 + 2 * 256 * D * 2, transcendentals=0
        ),
        name="encode",
    )(own, oth, encoder, bias[:, None, :], keep)


def _decode_kernel(tab_ref, codes_ref, first_ref, second_ref, own_ref, oth_ref, acc_ref):
    t = pl.program_id(1)
    has_first = tab_ref[T_FV + t] > 0
    has_second = tab_ref[T_SV + t] > 0

    @pl.when(has_first)
    def _():
        acc_ref[...] = jnp.dot(codes_ref[0], first_ref[0], preferred_element_type=F32)

    @pl.when(jnp.logical_not(has_first))
    def _():
        acc_ref[...] = jnp.zeros_like(acc_ref)

    @pl.when(has_second)
    def _():
        acc_ref[...] += jnp.dot(codes_ref[1], second_ref[0], preferred_element_type=F32)

    own_ref[0] = acc_ref[:HALF]
    oth_ref[0] = acc_ref[HALF:].astype(BF)


def _decode(tables, codes, decoder):
    chunk = 1792
    out = pl.BlockSpec((1, HALF, chunk), lambda c, t, tab: (t, 0, c))
    return pl.pallas_call(
        _decode_kernel,
        grid_spec=pltpu.PrefetchScalarGridSpec(
            num_scalar_prefetch=1,
            grid=(D // chunk, LAYERS),
            in_specs=[
                pl.BlockSpec((2, 2 * HALF, W), lambda c, t, tab: (0, 0, 0)),
                pl.BlockSpec((1, W, chunk), lambda c, t, tab: (tab[T_FIRST + t], 0, c)),
                pl.BlockSpec((1, W, chunk), lambda c, t, tab: (tab[T_SECOND + t], 0, c)),
            ],
            out_specs=[out, out],
            scratch_shapes=[pltpu.VMEM((2 * HALF, chunk), F32)],
        ),
        out_shape=[
            jax.ShapeDtypeStruct((LAYERS, HALF, D), F32),
            jax.ShapeDtypeStruct((LAYERS, HALF, D), BF),
        ],
        compiler_params=pltpu.CompilerParams(vmem_limit_bytes=20 << 20),
        cost_estimate=pl.CostEstimate(
            flops=2 * PAIRS * 256 * D * W, bytes_accessed=PAIRS * W * D * 2 + 4 * 128 * D * 6, transcendentals=0
        ),
        name="decode",
    )(tables, codes, decoder, decoder)


def _backward_kernel(
    tab_ref, codes_ref, slope_ref, own_ref, oth_ref, dec_ref, grad_ref, pre_ref, bias_ref, back_ref
):
    p = pl.program_id(0)
    c = pl.program_id(1)
    slot = tab_ref[T_SLOT + p]

    @pl.when(jnp.logical_and(p == 0, c == 0))
    def _():
        back_ref[...] = jnp.zeros_like(back_ref)

    err = jnp.concatenate([own_ref[0], oth_ref[0]], axis=0)
    grad_ref[0] = lax.dot_general(
        codes_ref[slot], err, (((0,), (0,)), ((), ())), preferred_element_type=F32
    ).astype(BF)
    back_ref[slot] += lax.dot_general(
        err, dec_ref[0], (((1,), (1,)), ((), ())), preferred_element_type=F32
    )

    @pl.when(jnp.logical_and(p == pl.num_programs(0) - 1, c == pl.num_programs(1) - 1))
    def _():
        for k in range(2):
            pre = (back_ref[k] * slope_ref[k]).astype(BF)
            pre_ref[k] = pre
            bias_ref[k] = jnp.sum(pre.astype(F32), axis=0, keepdims=True)


def _backward(tables, codes, slope, own, oth, decoder):
    chunk = 1792
    whole = lambda p, c, tab: (0, 0, 0)
    err = pl.BlockSpec((1, HALF, chunk), lambda p, c, tab: (tab[T_TARGET + p], 0, c))
    return pl.pallas_call(
        _backward_kernel,
        grid_spec=pltpu.PrefetchScalarGridSpec(
            num_scalar_prefetch=1,
            grid=(PAIRS, D // chunk),
            in_specs=[
                pl.BlockSpec((2, 2 * HALF, W), whole),
                pl.BlockSpec((2, 2 * HALF, W), whole),
                err,
                err,
                pl.BlockSpec((1, W, chunk), lambda p, c, tab: (p, 0, c)),
            ],
            out_specs=[
                pl.BlockSpec((1, W, chunk), lambda p, c, tab: (p, 0, c)),
                pl.BlockSpec((2, 2 * HALF, W), whole),
                pl.BlockSpec((2, 1, W), whole),
            ],
            scratch_shapes=[pltpu.VMEM((2, 2 * HALF, W), F32)],
        ),
        out_shape=[
            jax.ShapeDtypeStruct((PAIRS, W, D), BF),
            jax.ShapeDtypeStruct((2, 2 * HALF, W), BF),
            jax.ShapeDtypeStruct((2, 1, W), F32),
        ],
        compiler_params=pltpu.CompilerParams(vmem_limit_bytes=20 << 20),
        cost_estimate=pl.CostEstimate(
            flops=4 * PAIRS * 256 * D * W, bytes_accessed=2 * PAIRS * W * D * 2 + 4 * 256 * D * 2, transcendentals=0
        ),
        name="backward",
    )(tables, codes, slope, own, oth, decoder)


def _grad_encoder_kernel(own_ref, oth_ref, pre_ref, out_ref):
    x = jnp.concatenate([_rows(own_ref), _rows(oth_ref)], axis=0)
    out_ref[0] = lax.dot_general(
        x, pre_ref[0], (((0,), (0,)), ((), ())), preferred_element_type=F32
    ).astype(BF)


def _grad_encoder(own, oth, pre):
    chunk = 896
    xspec = pl.BlockSpec((TILES, None, HROW, chunk), lambda k, c: (0, k, 0, c))
    return pl.pallas_call(
        _grad_encoder_kernel,
        grid=(2, D // chunk),
        in_specs=[xspec, xspec, pl.BlockSpec((1, 2 * HALF, W), lambda k, c: (k, 0, 0))],
        out_specs=pl.BlockSpec((1, chunk, W), lambda k, c: (k, c, 0)),
        out_shape=jax.ShapeDtypeStruct((2, D, W), BF),
        compiler_params=pltpu.CompilerParams(vmem_limit_bytes=16 << 20),
        cost_estimate=pl.CostEstimate(
            flops=2 * 2 * 256 * D * W, bytes_accessed=2 * D * W * 2 + 2 * 256 * D * 2, transcendentals=0
        ),
        name="grad_encoder",
    )(own, oth, pre)


def per_device(resid_in, resid_out, encoder, enc_bias, decoder, active):
    x, zl, core = lax.axis_index("x"), lax.axis_index("zl"), lax.axis_index("core")
    zh, y = lax.axis_index("zh"), lax.axis_index("y")
    rank = (((x * 2 + zl) * 2 + core) * 2 + zh) * 4 + y
    side = x // 2
    tables = _tables(side)
    mine = jnp.stack(
        [
            lax.dynamic_slice(resid_in, (layer, core * HROW, 0), (1, HROW, D))[0]
            for layer in (side, LAYERS - 1 - side)
        ]
    )
    own = lax.all_to_all(jnp.broadcast_to(mine[None], (TILES, 2, HROW, D)), DP, 0, 0)
    oth = lax.ppermute(own, "core", SWAP)
    block_ids = (rank * W - side * FEAT) // BLOCK + jnp.arange(W // BLOCK, dtype=jnp.int32)
    listed = jnp.where(side == 0, active[jnp.array([0, 3])], active[jnp.array([1, 2])])
    hit = jnp.any(listed[:, :, :, None] == block_ids, axis=2).astype(F32)
    keep = jnp.repeat(hit, BLOCK, axis=2)
    codes, slope = _encode(own, oth, encoder, enc_bias, keep)
    part_own, part_oth = _decode(tables, codes, decoder)
    part = (part_own + lax.ppermute(part_oth, "core", SWAP).astype(F32)).astype(BF)
    pieces = lax.all_to_all(part.reshape(64, 8, D), GRID_AXES, 0, 0)
    summed = jnp.sum(pieces.astype(F32), axis=0)
    target = lax.all_to_all(resid_out, "y", 0, 0).reshape(8, D)
    errors = (summed - target.astype(F32)).astype(BF)
    recon = lax.all_to_all(summed.astype(BF).reshape(4, 2, D), "y", 0, 0)
    err_own = lax.all_to_all(jnp.broadcast_to(errors[None], (64, 8, D)), GRID_AXES, 0, 0)
    err_own = err_own.reshape(LAYERS, HALF, D)
    err_oth = lax.ppermute(err_own, "core", SWAP)
    grad_decoder, pre, grad_bias = _backward(tables, codes, slope, err_own, err_oth, decoder)
    grad_encoder = _grad_encoder(own, oth, pre)
    return recon, grad_encoder, grad_bias[:, 0, :], grad_decoder


def solution(mesh):
    fine = Mesh(mesh.devices.reshape(4, 2, 2, 2, 4), ALL)
    in_specs = (
        P(None, DP, None),
        P(None, ALL, None),
        P(None, None, ALL),
        P(None, ALL),
        P(None, ALL, None),
        P(),
    )
    out_specs = (P(None, ALL, None), P(None, None, ALL), P(None, ALL), P(None, ALL, None))
    return jax.shard_map(
        per_device, mesh=fine, in_specs=in_specs, out_specs=out_specs, check_vma=False
    )
```

```python
import jax
import jax.numpy as jnp
from jax import lax
from jax.experimental import pallas as pl
from jax.experimental.pallas import tpu as pltpu
from jax.sharding import Mesh
from jax.sharding import PartitionSpec as P

FEAT = 16384
BLOCK = 128
LAYERS = 4
D = 3584
W = 256
HALF = 128
TILES = 8
HROW = 16
PAIRS = 5
GRID_AXES = ("y", "x", "zl", "zh")
DP = ("zh", "y")
ALL = ("x", "zl", "core", "zh", "y")
BF = jnp.bfloat16
F32 = jnp.float32
SWAP = [(0, 1), (1, 0)]

SLOT = ((0, 0, 0, 0, 1), (0, 0, 0, 1, 1))
TARGET = ((0, 1, 2, 3, 3), (1, 2, 3, 2, 3))
FIRST = (((0, 1), (1, 1), (2, 1), (3, 1)), ((0, 0), (0, 1), (1, 1), (2, 1)))
SECOND = (((4, 0), (4, 0), (4, 0), (4, 1)), ((3, 0), (3, 0), (3, 1), (4, 1)))


def _tables(side):
    rows = []
    for s in range(2):
        rows.append(
            [p for p, _ in FIRST[s]]
            + [v for _, v in FIRST[s]]
            + [p for p, _ in SECOND[s]]
            + [v for _, v in SECOND[s]]
            + list(SLOT[s])
            + list(TARGET[s])
        )
    return jnp.where(side == 0, jnp.array(rows[0], jnp.int32), jnp.array(rows[1], jnp.int32))


T_FIRST, T_FV, T_SECOND, T_SV, T_SLOT, T_TARGET = 0, 4, 8, 12, 16, 21


def _tokens(own_ref, oth_ref, k):
    own = own_ref[:, k].reshape(HALF, D)
    oth = oth_ref[:, k].reshape(HALF, D)
    return own, oth


VMEM = pltpu.MemorySpace.VMEM
WHOLE = pl.BlockSpec(memory_space=VMEM)
CHUNK = 512


def _encode_kernel(own_ref, oth_ref, enc_ref, bias_ref, keep_ref, codes_ref, turned_ref, slope_ref):
    k = pl.program_id(0)
    x = jnp.concatenate(_tokens(own_ref, oth_ref, k), axis=0)
    pre = jnp.dot(x, enc_ref[0], preferred_element_type=F32) + bias_ref[0]
    positive = jnp.maximum(pre, 0.0)
    keep = jnp.broadcast_to(keep_ref[0][:, None, :], (TILES, HROW, W)).reshape(HALF, W)
    keep = jnp.concatenate([keep, keep], axis=0)
    kept = keep * positive
    codes = kept * positive
    codes_ref[0] = codes.astype(BF)
    turned_ref[0] = codes.T.astype(BF)
    slope_ref[0] = 2.0 * kept


def _encode(own, oth, encoder, bias, keep):
    out = pl.BlockSpec((1, 2 * HALF, W), lambda k: (k, 0, 0))
    return pl.pallas_call(
        _encode_kernel,
        grid=(2,),
        in_specs=[
            WHOLE,
            WHOLE,
            pl.BlockSpec((1, D, W), lambda k: (k, 0, 0)),
            pl.BlockSpec((1, 1, W), lambda k: (k, 0, 0)),
            pl.BlockSpec((1, TILES, W), lambda k: (k, 0, 0)),
        ],
        out_specs=[out, out, out],
        out_shape=[
            jax.ShapeDtypeStruct((2, 2 * HALF, W), BF),
            jax.ShapeDtypeStruct((2, W, 2 * HALF), BF),
            jax.ShapeDtypeStruct((2, 2 * HALF, W), F32),
        ],
        compiler_params=pltpu.CompilerParams(vmem_limit_bytes=24 << 20),
        cost_estimate=pl.CostEstimate(
            flops=2 * 2 * 256 * D * W, bytes_accessed=2 * D * W * 2, transcendentals=0
        ),
        name="encode",
    )(own, oth, encoder, bias[:, None, :], keep)


def _decode_kernel(tab_ref, codes_ref, first_ref, second_ref, own_ref, oth_ref):
    t = pl.program_id(0)
    has_first = tab_ref[T_FV + t] > 0
    has_second = tab_ref[T_SV + t] > 0

    def write(cols, value):
        own_ref[0, :, cols] = value[:HALF].astype(BF)
        oth_ref[0, :, cols] = value[HALF:].astype(BF)

    def sweep(part):
        for c in range(D // CHUNK):
            cols = slice(c * CHUNK, (c + 1) * CHUNK)
            write(cols, part(cols))

    def first(cols):
        return jnp.dot(codes_ref[0], first_ref[0, :, cols], preferred_element_type=F32)

    def both(cols):
        return first(cols) + jnp.dot(codes_ref[1], second_ref[0, :, cols], preferred_element_type=F32)

    @pl.when(has_second)
    def _():
        sweep(both)

    @pl.when(jnp.logical_and(has_first, jnp.logical_not(has_second)))
    def _():
        sweep(first)

    @pl.when(jnp.logical_not(has_first))
    def _():
        own_ref[...] = jnp.zeros_like(own_ref)
        oth_ref[...] = jnp.zeros_like(oth_ref)


def _decode(tables, codes, decoder):
    out = pl.BlockSpec((1, HALF, D), lambda t, tab: (t, 0, 0))
    return pl.pallas_call(
        _decode_kernel,
        grid_spec=pltpu.PrefetchScalarGridSpec(
            num_scalar_prefetch=1,
            grid=(LAYERS,),
            in_specs=[
                pl.BlockSpec((2, 2 * HALF, W), lambda t, tab: (0, 0, 0)),
                pl.BlockSpec((1, W, D), lambda t, tab: (tab[T_FIRST + t], 0, 0)),
                pl.BlockSpec((1, W, D), lambda t, tab: (tab[T_SECOND + t], 0, 0)),
            ],
            out_specs=[out, out],
        ),
        out_shape=[
            jax.ShapeDtypeStruct((LAYERS, HALF, D), BF),
            jax.ShapeDtypeStruct((LAYERS, HALF, D), BF),
        ],
        compiler_params=pltpu.CompilerParams(vmem_limit_bytes=24 << 20),
        cost_estimate=pl.CostEstimate(
            flops=2 * PAIRS * 256 * D * W, bytes_accessed=PAIRS * W * D * 2 + 4 * 128 * D * 4, transcendentals=0
        ),
        name="decode",
    )(tables, codes, decoder, decoder)


def _turn_kernel(own_ref, oth_ref, out_ref):
    k = pl.program_id(0)
    own, oth = _tokens(own_ref, oth_ref, k)
    for c in range(D // CHUNK):
        cols = slice(c * CHUNK, (c + 1) * CHUNK)
        out_ref[0, cols, :HALF] = own[:, cols].T
        out_ref[0, cols, HALF:] = oth[:, cols].T


def _turn(own, oth):
    return pl.pallas_call(
        _turn_kernel,
        grid=(2,),
        in_specs=[WHOLE, WHOLE],
        out_specs=pl.BlockSpec((1, D, 2 * HALF), lambda k: (k, 0, 0)),
        out_shape=jax.ShapeDtypeStruct((2, D, 2 * HALF), BF),
        compiler_params=pltpu.CompilerParams(vmem_limit_bytes=20 << 20),
        cost_estimate=pl.CostEstimate(flops=2 * 256 * D * 300, bytes_accessed=4 * 256 * D * 2, transcendentals=0),
        name="turn",
    )(own, oth)


def _backward_kernel(
    tab_ref, turned_ref, slope_ref, own_ref, oth_ref, xt_ref, dec_ref, grad_ref, genc_ref, bias_ref, back_ref, pre_ref
):
    p = pl.program_id(0)

    @pl.when(p == 0)
    def _():
        back_ref[...] = jnp.zeros_like(back_ref)

    @pl.when(p < PAIRS)
    def _():
        pair = jnp.minimum(p, PAIRS - 1)
        slot = tab_ref[T_SLOT + pair]
        target = tab_ref[T_TARGET + pair]
        err = jnp.concatenate([own_ref[target], oth_ref[target]], axis=0)
        back_ref[slot] += lax.dot_general(
            err, dec_ref[0], (((1,), (1,)), ((), ())), preferred_element_type=F32
        )
        turned = turned_ref[slot]
        for c in range(D // CHUNK):
            cols = slice(c * CHUNK, (c + 1) * CHUNK)
            grad_ref[0, :, cols] = jnp.dot(
                turned, err[:, cols], preferred_element_type=F32
            ).astype(BF)

    @pl.when(p == PAIRS)
    def _():
        for k in range(2):
            pre = (back_ref[k] * slope_ref[k]).astype(BF)
            pre_ref[k] = pre
            bias_ref[k] = jnp.sum(pre.astype(F32), axis=0, keepdims=True)

    @pl.when(p >= PAIRS)
    def _():
        k = jnp.maximum(p - PAIRS, 0)
        genc_ref[0] = jnp.dot(xt_ref[0], pre_ref[k], preferred_element_type=F32).astype(BF)


def _backward(tables, turned, slope, own, oth, xt, decoder):
    pair = lambda p, tab: (jnp.minimum(p, PAIRS - 1), 0, 0)
    enc = lambda p, tab: (jnp.maximum(p - PAIRS, 0), 0, 0)
    return pl.pallas_call(
        _backward_kernel,
        grid_spec=pltpu.PrefetchScalarGridSpec(
            num_scalar_prefetch=1,
            grid=(PAIRS + 2,),
            in_specs=[WHOLE, WHOLE, WHOLE, WHOLE, pl.BlockSpec((1, D, 2 * HALF), enc), pl.BlockSpec((1, W, D), pair)],
            out_specs=[
                pl.BlockSpec((1, W, D), pair),
                pl.BlockSpec((1, D, W), enc),
                pl.BlockSpec((2, 1, W), lambda p, tab: (0, 0, 0)),
            ],
            scratch_shapes=[pltpu.VMEM((2, 2 * HALF, W), F32), pltpu.VMEM((2, 2 * HALF, W), BF)],
        ),
        out_shape=[
            jax.ShapeDtypeStruct((PAIRS, W, D), BF),
            jax.ShapeDtypeStruct((2, D, W), BF),
            jax.ShapeDtypeStruct((2, 1, W), F32),
        ],
        compiler_params=pltpu.CompilerParams(vmem_limit_bytes=32 << 20),
        cost_estimate=pl.CostEstimate(
            flops=4 * PAIRS * 256 * D * W + 4 * 256 * D * W,
            bytes_accessed=2 * PAIRS * W * D * 2 + 2 * D * W * 2,
            transcendentals=0,
        ),
        name="backward",
    )(tables, turned, slope, own, oth, xt, decoder)


def _hbm(x):
    return pltpu.with_memory_space_constraint(x, pltpu.MemorySpace.HBM)


def _vmem(x):
    return pltpu.with_memory_space_constraint(x, VMEM)


def per_device(resid_in, resid_out, encoder, enc_bias, decoder, active):
    x, zl, core = lax.axis_index("x"), lax.axis_index("zl"), lax.axis_index("core")
    zh, y = lax.axis_index("zh"), lax.axis_index("y")
    rank = (((x * 2 + zl) * 2 + core) * 2 + zh) * 4 + y
    side = x // 2
    tables = _tables(side)
    mine = jnp.stack(
        [
            lax.dynamic_slice(resid_in, (layer, core * HROW, 0), (1, HROW, D))[0]
            for layer in (side, LAYERS - 1 - side)
        ]
    )
    own = lax.all_to_all(jnp.broadcast_to(mine[None], (TILES, 2, HROW, D)), DP, 0, 0)
    oth = lax.ppermute(own, "core", SWAP)
    block_ids = (rank * W - side * FEAT) // BLOCK + jnp.arange(W // BLOCK, dtype=jnp.int32)
    listed = jnp.where(side == 0, active[jnp.array([0, 3])], active[jnp.array([1, 2])])
    hit = jnp.any(listed[:, :, :, None] == block_ids, axis=2).astype(F32)
    keep = jnp.repeat(hit, BLOCK, axis=2)
    codes, turned, slope = _encode(own, oth, _hbm(encoder), enc_bias, keep)
    part_own, part_oth = _decode(tables, codes, _hbm(decoder))
    swapped = lax.ppermute(part_oth, "core", SWAP)
    part = (part_own.astype(F32) + swapped.astype(F32)).astype(BF)
    pieces = lax.all_to_all(part.reshape(64, 8, D), GRID_AXES, 0, 0)
    summed = jnp.sum(pieces.astype(F32), axis=0)
    target = lax.all_to_all(resid_out, "y", 0, 0).reshape(8, D)
    errors = (summed - target.astype(F32)).astype(BF)
    xt = _turn(own, oth)
    errors, xt = lax.optimization_barrier((errors, xt))
    recon = lax.all_to_all(summed.astype(BF).reshape(4, 2, D), "y", 0, 0)
    err_own = lax.all_to_all(jnp.broadcast_to(errors[None], (64, 8, D)), GRID_AXES, 0, 0)
    err_own = err_own.reshape(LAYERS, HALF, D)
    err_oth = lax.ppermute(err_own, "core", SWAP)
    grad_decoder, grad_encoder, grad_bias = _backward(
        tables, turned, slope, _vmem(err_own), _vmem(err_oth), _hbm(xt), _hbm(decoder)
    )
    return recon, grad_encoder, grad_bias[:, 0, :], grad_decoder


def solution(mesh):
    fine = Mesh(mesh.devices.reshape(4, 2, 2, 2, 4), ALL)
    in_specs = (
        P(None, DP, None),
        P(None, ALL, None),
        P(None, None, ALL),
        P(None, ALL),
        P(None, ALL, None),
        P(),
    )
    out_specs = (P(None, ALL, None), P(None, None, ALL), P(None, ALL), P(None, ALL, None))
    return jax.shard_map(
        per_device, mesh=fine, in_specs=in_specs, out_specs=out_specs, check_vma=False
    )
```

```python
import jax
import jax.numpy as jnp
from jax import lax
from jax.experimental import pallas as pl
from jax.experimental.pallas import tpu as pltpu
from jax.sharding import Mesh
from jax.sharding import PartitionSpec as P

FEAT = 16384
BLOCK = 128
LAYERS = 4
D = 3584
W = 256
HALF = 128
TILES = 8
HROW = 16
PAIRS = 5
GRID_AXES = ("y", "x", "zl", "zh")
DP = ("zh", "y")
ALL = ("x", "zl", "core", "zh", "y")
BF = jnp.bfloat16
F32 = jnp.float32
SWAP = [(0, 1), (1, 0)]

SLOT = ((0, 0, 0, 0, 1), (0, 0, 0, 1, 1))
TARGET = ((0, 1, 2, 3, 3), (1, 2, 3, 2, 3))
FIRST = (((0, 1), (1, 1), (2, 1), (3, 1)), ((0, 0), (0, 1), (1, 1), (2, 1)))
SECOND = (((4, 0), (4, 0), (4, 0), (4, 1)), ((3, 0), (3, 0), (3, 1), (4, 1)))


def _tables(side):
    rows = []
    for s in range(2):
        rows.append(
            [p for p, _ in FIRST[s]]
            + [v for _, v in FIRST[s]]
            + [p for p, _ in SECOND[s]]
            + [v for _, v in SECOND[s]]
            + list(SLOT[s])
            + list(TARGET[s])
        )
    return jnp.where(side == 0, jnp.array(rows[0], jnp.int32), jnp.array(rows[1], jnp.int32))


T_FIRST, T_FV, T_SECOND, T_SV, T_SLOT, T_TARGET = 0, 4, 8, 12, 16, 21


VMEM = pltpu.MemorySpace.VMEM
HBM = pltpu.MemorySpace.HBM
WHOLE = pl.BlockSpec(memory_space=VMEM)
CHUNK = 512
CHUNKS = [slice(c, c + CHUNK) for c in range(0, D, CHUNK)]


def _hbm(x):
    return pltpu.with_memory_space_constraint(x, HBM)


def _vmem(x):
    return pltpu.with_memory_space_constraint(x, VMEM)


def _params(mib):
    return pltpu.CompilerParams(vmem_limit_bytes=mib << 20)


def _tokens(own_ref, oth_ref, k):
    return own_ref[:, k].reshape(HALF, D), oth_ref[:, k].reshape(HALF, D)


def _forward_kernel(
    tab_ref, own_ref, oth_ref, enc_hbm, dec_hbm, bias_ref, keep_ref,
    part_own_ref, part_oth_ref, turned_ref, slope_ref, dec_ref, enc_ref, codes_ref, enc_sem, dec_sem,
):
    enc_copies = [
        pltpu.make_async_copy(enc_hbm.at[k], enc_ref.at[k], enc_sem.at[k]) for k in range(2)
    ]
    dec_copies = [
        pltpu.make_async_copy(dec_hbm.at[p], dec_ref.at[p], dec_sem.at[p]) for p in range(PAIRS)
    ]
    for copy in enc_copies + dec_copies:
        copy.start()
    for k in range(2):
        x = jnp.concatenate(_tokens(own_ref, oth_ref, k), axis=0)
        enc_copies[k].wait()
        pre = jnp.dot(x, enc_ref[k], preferred_element_type=F32) + bias_ref[k : k + 1]
        positive = jnp.maximum(pre, 0.0)
        keep = jnp.broadcast_to(keep_ref[k][:, None, :], (TILES, HROW, W)).reshape(HALF, W)
        keep = jnp.concatenate([keep, keep], axis=0)
        kept = keep * positive
        codes = kept * positive
        codes_ref[k] = codes.astype(BF)
        turned_ref[k] = codes.T.astype(BF)
        slope_ref[k] = 2.0 * kept

    def sweep(t, part):
        for cols in CHUNKS:
            value = part(cols).astype(BF)
            part_own_ref[t, :, cols] = value[:HALF]
            part_oth_ref[t, :, cols] = value[HALF:]

    needed = ((0,), (1,), (2, 3), (4,))
    for t in range(LAYERS):
        for p in needed[t]:
            dec_copies[p].wait()
        has_first = tab_ref[T_FV + t] > 0
        has_second = tab_ref[T_SV + t] > 0
        one = tab_ref[T_FIRST + t]
        two = tab_ref[T_SECOND + t]

        def first(cols, one=one):
            return jnp.dot(codes_ref[0], dec_ref[one, :, cols], preferred_element_type=F32)

        def both(cols, first=first, two=two):
            return first(cols) + jnp.dot(
                codes_ref[1], dec_ref[two, :, cols], preferred_element_type=F32
            )

        @pl.when(has_second)
        def _():
            sweep(t, both)

        @pl.when(jnp.logical_and(has_first, jnp.logical_not(has_second)))
        def _():
            sweep(t, first)

        @pl.when(jnp.logical_not(has_first))
        def _():
            part_own_ref[t] = jnp.zeros((HALF, D), BF)
            part_oth_ref[t] = jnp.zeros((HALF, D), BF)


def _forward(tables, own, oth, encoder, decoder, bias, keep):
    smem = pl.BlockSpec(memory_space=pltpu.MemorySpace.SMEM)
    hbm = pl.BlockSpec(memory_space=HBM)
    return pl.pallas_call(
        _forward_kernel,
        in_specs=[smem, WHOLE, WHOLE, hbm, hbm, WHOLE, WHOLE],
        out_specs=[WHOLE] * 5,
        out_shape=[
            jax.ShapeDtypeStruct((LAYERS, HALF, D), BF),
            jax.ShapeDtypeStruct((LAYERS, HALF, D), BF),
            jax.ShapeDtypeStruct((2, W, 2 * HALF), BF),
            jax.ShapeDtypeStruct((2, 2 * HALF, W), F32),
            jax.ShapeDtypeStruct((PAIRS, W, D), BF),
        ],
        scratch_shapes=[
            pltpu.VMEM((2, D, W), BF),
            pltpu.VMEM((2, 2 * HALF, W), BF),
            pltpu.SemaphoreType.DMA((2,)),
            pltpu.SemaphoreType.DMA((PAIRS,)),
        ],
        compiler_params=_params(18),
        cost_estimate=pl.CostEstimate(
            flops=2 * (PAIRS + 2) * 256 * D * W,
            bytes_accessed=(2 * D * W + PAIRS * W * D) * 2,
            transcendentals=0,
        ),
        name="forward",
    )(tables, own, oth, encoder, decoder, bias, keep)


def _join_kernel(own_ref, got_ref, out_ref):
    out_ref[...] = (own_ref[...].astype(F32) + got_ref[...].astype(F32)).astype(BF)


def _join(own, got):
    return pl.pallas_call(
        _join_kernel,
        grid=(LAYERS,),
        in_specs=[pl.BlockSpec((1, HALF, D), lambda t: (t, 0, 0))] * 2,
        out_specs=pl.BlockSpec((1, HALF, D), lambda t: (t, 0, 0)),
        out_shape=jax.ShapeDtypeStruct((LAYERS, HALF, D), BF),
        compiler_params=_params(8),
        cost_estimate=pl.CostEstimate(
            flops=4 * HALF * D, bytes_accessed=3 * 4 * HALF * D * 2, transcendentals=0
        ),
        name="join",
    )(own, got)


def _settle_kernel(pieces_ref, target_ref, errors_ref, recon_ref, rows_ref):
    summed = lax.fori_loop(
        0, 64, lambda i, acc: acc + pieces_ref[i].astype(F32), jnp.zeros((8, D), F32), unroll=8
    )
    for j in range(4):
        rows_ref[2 * j : 2 * j + 2] = target_ref[j].astype(F32)
    errors = (summed - rows_ref[...]).astype(BF)
    rows_ref[...] = summed
    for j in range(4):
        recon_ref[j] = rows_ref[2 * j : 2 * j + 2].astype(BF)

    def spread(i, carry):
        errors_ref[i] = errors
        return carry

    lax.fori_loop(0, 64, spread, 0, unroll=8)


def _settle(pieces, target):
    return pl.pallas_call(
        _settle_kernel,
        in_specs=[WHOLE, WHOLE],
        out_specs=[WHOLE, WHOLE],
        out_shape=[
            jax.ShapeDtypeStruct((64, 8, D), BF),
            jax.ShapeDtypeStruct((4, 2, D), BF),
        ],
        scratch_shapes=[pltpu.VMEM((8, D), F32)],
        compiler_params=_params(4),
        cost_estimate=pl.CostEstimate(
            flops=64 * 8 * D, bytes_accessed=2 * 64 * 8 * D * 2, transcendentals=0
        ),
        name="settle",
    )(pieces, target)


def _backward_kernel(
    tab_ref, turned_ref, slope_ref, own_ref, oth_ref, x_own_ref, x_oth_ref, dec_ref, grad_ref, genc_ref, bias_ref, back_ref, pre_ref
):
    p = pl.program_id(0)

    @pl.when(p == 0)
    def _():
        back_ref[...] = jnp.zeros_like(back_ref)

    @pl.when(p < PAIRS)
    def _():
        pair = jnp.minimum(p, PAIRS - 1)
        slot = tab_ref[T_SLOT + pair]
        target = tab_ref[T_TARGET + pair]
        err = jnp.concatenate([own_ref[target], oth_ref[target]], axis=0)
        back_ref[slot] += lax.dot_general(
            err, dec_ref[pair], (((1,), (1,)), ((), ())), preferred_element_type=F32
        )
        turned = turned_ref[slot]
        for cols in CHUNKS:
            err = jnp.concatenate([own_ref[target, :, cols], oth_ref[target, :, cols]], axis=0)
            grad_ref[0, :, cols] = jnp.dot(turned, err, preferred_element_type=F32).astype(BF)

    @pl.when(p == PAIRS)
    def _():
        for k in range(2):
            pre = (back_ref[k] * slope_ref[k]).astype(BF)
            pre_ref[k] = pre
            bias_ref[k : k + 1] = jnp.sum(pre.astype(F32), axis=0, keepdims=True)

    @pl.when(p >= PAIRS)
    def _():
        k = jnp.maximum(p - PAIRS, 0)
        own, oth = _tokens(x_own_ref, x_oth_ref, k)
        for rows in CHUNKS:
            x = jnp.concatenate([own[:, rows], oth[:, rows]], axis=0)
            genc_ref[0, rows] = lax.dot_general(
                x, pre_ref[k], (((0,), (0,)), ((), ())), preferred_element_type=F32
            ).astype(BF)


def _backward(tables, turned, slope, own, oth, x_own, x_oth, decoder):
    pair = lambda p, tab: (jnp.minimum(p, PAIRS - 1), 0, 0)
    enc = lambda p, tab: (jnp.maximum(p - PAIRS, 0), 0, 0)
    return pl.pallas_call(
        _backward_kernel,
        grid_spec=pltpu.PrefetchScalarGridSpec(
            num_scalar_prefetch=1,
            grid=(PAIRS + 2,),
            in_specs=[WHOLE] * 7,
            out_specs=[
                pl.BlockSpec((1, W, D), pair),
                pl.BlockSpec((1, D, W), enc),
                pl.BlockSpec((2, W), lambda p, tab: (0, 0)),
            ],
            scratch_shapes=[pltpu.VMEM((2, 2 * HALF, W), F32), pltpu.VMEM((2, 2 * HALF, W), BF)],
        ),
        out_shape=[
            jax.ShapeDtypeStruct((PAIRS, W, D), BF),
            jax.ShapeDtypeStruct((2, D, W), BF),
            jax.ShapeDtypeStruct((2, W), F32),
        ],
        compiler_params=_params(18),
        cost_estimate=pl.CostEstimate(
            flops=4 * PAIRS * 256 * D * W + 4 * 256 * D * W,
            bytes_accessed=PAIRS * W * D * 2 + 2 * D * W * 2,
            transcendentals=0,
        ),
        name="backward",
    )(tables, turned, slope, own, oth, x_own, x_oth, decoder)


def per_device(resid_in, resid_out, encoder, enc_bias, decoder, active):
    x, zl, core = lax.axis_index("x"), lax.axis_index("zl"), lax.axis_index("core")
    zh, y = lax.axis_index("zh"), lax.axis_index("y")
    rank = (((x * 2 + zl) * 2 + core) * 2 + zh) * 4 + y
    side = x // 2
    tables = _tables(side)
    block_ids = (rank * W - side * FEAT) // BLOCK + jnp.arange(W // BLOCK, dtype=jnp.int32)
    outer = jnp.concatenate([active[:1], active[3:]], axis=0)
    listed = jnp.where(side == 0, outer, active[1:3])
    hit = jnp.any(listed[:, :, :, None] == block_ids, axis=2).astype(F32)
    keep = jnp.repeat(hit, BLOCK, axis=2)
    mine = jnp.stack(
        [
            lax.dynamic_slice(resid_in, (layer, core * HROW, 0), (1, HROW, D))[0]
            for layer in (side, LAYERS - 1 - side)
        ]
    )
    mine, tables, keep = lax.optimization_barrier((mine, tables, keep))
    own = lax.all_to_all(jnp.broadcast_to(mine[None], (TILES, 2, HROW, D)), DP, 0, 0)
    oth = lax.ppermute(own, "core", SWAP)
    part_own, part_oth, turned, slope, dec = _forward(
        tables, own, oth, _hbm(encoder), _hbm(decoder), enc_bias, keep
    )
    swapped = lax.ppermute(part_oth, "core", SWAP)
    resid_out, part_own = lax.optimization_barrier((resid_out, part_own))
    target = lax.all_to_all(resid_out, "y", 0, 0)
    swapped, target = lax.optimization_barrier((swapped, target))
    part = _join(part_own, swapped)
    pieces = lax.all_to_all(part.reshape(64, 8, D), GRID_AXES, 0, 0)
    errors, recon = _settle(pieces, target)
    err_own = lax.all_to_all(errors, GRID_AXES, 0, 0).reshape(LAYERS, HALF, D)
    err_oth = lax.ppermute(err_own, "core", SWAP)
    recon, err_own = lax.optimization_barrier((recon, err_own))
    recon = lax.all_to_all(recon, "y", 0, 0)
    err_oth, recon = lax.optimization_barrier((err_oth, recon))
    grad_decoder, grad_encoder, grad_bias = _backward(
        tables, turned, slope, err_own, err_oth, own, oth, dec
    )
    return recon, grad_encoder, grad_bias, grad_decoder


def solution(mesh):
    fine = Mesh(mesh.devices.reshape(4, 2, 2, 2, 4), ALL)
    in_specs = (
        P(None, DP, None),
        P(None, ALL, None),
        P(None, None, ALL),
        P(None, ALL),
        P(None, ALL, None),
        P(),
    )
    out_specs = (P(None, ALL, None), P(None, None, ALL), P(None, ALL), P(None, ALL, None))
    return jax.shard_map(
        per_device, mesh=fine, in_specs=in_specs, out_specs=out_specs, check_vma=False
    )
```

```python
import jax
import jax.numpy as jnp
from jax import lax
from jax.experimental import pallas as pl
from jax.experimental.pallas import tpu as pltpu
from jax.sharding import Mesh
from jax.sharding import PartitionSpec as P

FEAT = 16384
BLOCK = 128
LAYERS = 4
D = 3584
W = 256
HALF = 128
TILES = 8
HROW = 16
PAIRS = 5
GRID_AXES = ("y", "x", "zl", "zh")
DP = ("zh", "y")
ALL = ("x", "zl", "core", "zh", "y")
BF = jnp.bfloat16
F32 = jnp.float32
SWAP = [(0, 1), (1, 0)]

VMEM = pltpu.MemorySpace.VMEM
HBM = pltpu.MemorySpace.HBM
WHOLE = pl.BlockSpec(memory_space=VMEM)
CHUNK = 512
CHUNKS = [slice(c, c + CHUNK) for c in range(0, D, CHUNK)]


def _hbm(x):
    return pltpu.with_memory_space_constraint(x, HBM)


def _vmem(x):
    return pltpu.with_memory_space_constraint(x, VMEM)


def _params(mib):
    return pltpu.CompilerParams(vmem_limit_bytes=mib << 20)


def _tokens(own_ref, oth_ref, k):
    return own_ref[:, k].reshape(HALF, D), oth_ref[:, k].reshape(HALF, D)


def _side():
    return lax.axis_index("x") // 2


def _prepare_kernel(in_hbm, out_ref, spread_ref, *rest):
    piece_refs, sem = rest[:4], rest[4]
    side, core, y = _side(), lax.axis_index("core"), lax.axis_index("y")
    copies = []
    for k, layer in enumerate((side, LAYERS - 1 - side)):
        for i in range(TILES):
            copies.append(
                pltpu.make_async_copy(
                    in_hbm.at[layer, pl.ds(pl.multiple_of(core * HROW, HROW), HROW)],
                    spread_ref.at[i, k],
                    sem.at[k * TILES + i],
                )
            )
    for copy in copies:
        copy.start()
    for j in range(4):
        piece_refs[j][...] = out_ref[lax.rem(y + j, 4)]
    for copy in copies:
        copy.wait()


def _prepare(resid_in, resid_out):
    return pl.pallas_call(
        _prepare_kernel,
        in_specs=[pl.BlockSpec(memory_space=HBM), WHOLE],
        out_specs=[WHOLE] * 5,
        out_shape=[jax.ShapeDtypeStruct((TILES, 2, HROW, D), BF)]
        + [jax.ShapeDtypeStruct((2, D), BF)] * 4,
        scratch_shapes=[pltpu.SemaphoreType.DMA((2 * TILES,))],
        compiler_params=_params(2),
        name="prepare",
    )(_hbm(resid_in), resid_out)


def _decode(t, side, codes_ref, dec_ref, own_ref, oth_ref, at):
    has_first = t >= side
    has_second = t + 1 >= LAYERS - side
    one = jnp.maximum(t - side, 0)

    def sweep(part):
        for cols in CHUNKS:
            value = part(cols).astype(BF)
            own_ref[at, :, cols] = value[:HALF]
            oth_ref[at, :, cols] = value[HALF:]

    def first(cols):
        return jnp.dot(codes_ref[0], dec_ref[one, :, cols], preferred_element_type=F32)

    def both(cols):
        return first(cols) + jnp.dot(
            codes_ref[1], dec_ref[t + 1, :, cols], preferred_element_type=F32
        )

    @pl.when(has_second)
    def _():
        sweep(both)

    @pl.when(jnp.logical_and(has_first, jnp.logical_not(has_second)))
    def _():
        sweep(first)

    @pl.when(jnp.logical_not(has_first))
    def _():
        own_ref[at] = jnp.zeros((HALF, D), BF)
        oth_ref[at] = jnp.zeros((HALF, D), BF)


def _forward_kernel(
    own_ref, oth_ref, enc_hbm, dec_hbm, bias_ref, active_ref,
    part_own_ref, part_oth_ref, codes_ref, turned_ref, slope_ref, dec_ref, enc_ref, enc_sem, dec_sem,
):
    enc_copies = [
        pltpu.make_async_copy(enc_hbm.at[k], enc_ref.at[k], enc_sem.at[k]) for k in range(2)
    ]
    dec_copies = [
        pltpu.make_async_copy(dec_hbm.at[p], dec_ref.at[p], dec_sem.at[p]) for p in range(PAIRS)
    ]
    for copy in enc_copies + dec_copies[::-1]:
        copy.start()
    x, zl, core = lax.axis_index("x"), lax.axis_index("zl"), lax.axis_index("core")
    zh, y = lax.axis_index("zh"), lax.axis_index("y")
    side = _side()
    rank = (((x * 2 + zl) * 2 + core) * 2 + zh) * 4 + y
    block = rank * (W // BLOCK) - side * (FEAT // BLOCK)
    for k, layer in enumerate((side, LAYERS - 1 - side)):
        rows = jnp.concatenate(_tokens(own_ref, oth_ref, k), axis=0)
        listed = active_ref[layer]
        keep = [
            jnp.broadcast_to(
                jnp.max((listed == block + b).astype(F32), axis=1, keepdims=True), (TILES, BLOCK)
            )
            for b in range(W // BLOCK)
        ]
        keep = jnp.concatenate(keep, axis=1)
        keep = jnp.broadcast_to(keep[:, None, :], (TILES, HROW, W)).reshape(HALF, W)
        keep = jnp.concatenate([keep, keep], axis=0)
        enc_copies[k].wait()
        pre = jnp.dot(rows, enc_ref[k], preferred_element_type=F32) + bias_ref[k : k + 1]
        positive = jnp.maximum(pre, 0.0)
        kept = keep * positive
        codes = kept * positive
        codes_ref[k] = codes.astype(BF)
        turned_ref[k] = codes.T.astype(BF)
        slope_ref[k] = 2.0 * kept
    for p in (4, 3, 2):
        dec_copies[p].wait()
    _decode(3, side, codes_ref, dec_ref, part_own_ref, part_oth_ref, 1)
    dec_copies[1].wait()
    _decode(2, side, codes_ref, dec_ref, part_own_ref, part_oth_ref, 0)
    dec_copies[0].wait()


def _forward(own, oth, encoder, decoder, bias, active):
    hbm = pl.BlockSpec(memory_space=HBM)
    return pl.pallas_call(
        _forward_kernel,
        in_specs=[WHOLE, WHOLE, hbm, hbm, WHOLE, WHOLE],
        out_specs=[WHOLE] * 6,
        out_shape=[
            jax.ShapeDtypeStruct((2, HALF, D), BF),
            jax.ShapeDtypeStruct((2, HALF, D), BF),
            jax.ShapeDtypeStruct((2, 2 * HALF, W), BF),
            jax.ShapeDtypeStruct((2, W, 2 * HALF), BF),
            jax.ShapeDtypeStruct((2, 2 * HALF, W), F32),
            jax.ShapeDtypeStruct((PAIRS, W, D), BF),
        ],
        scratch_shapes=[
            pltpu.VMEM((2, D, W), BF),
            pltpu.SemaphoreType.DMA((2,)),
            pltpu.SemaphoreType.DMA((PAIRS,)),
        ],
        compiler_params=_params(10),
        cost_estimate=pl.CostEstimate(
            flops=2 * 5 * 256 * D * W,
            bytes_accessed=(2 * D * W + PAIRS * W * D) * 2,
            transcendentals=0,
        ),
        name="forward",
    )(own, oth, _hbm(encoder), _hbm(decoder), bias, active)


def _forward_low_kernel(codes_ref, dec_ref, part_own_ref, part_oth_ref):
    for t in (1, 0):
        _decode(t, _side(), codes_ref, dec_ref, part_own_ref, part_oth_ref, t)


def _forward_low(codes, dec):
    return pl.pallas_call(
        _forward_low_kernel,
        in_specs=[WHOLE, WHOLE],
        out_specs=[WHOLE, WHOLE],
        out_shape=[jax.ShapeDtypeStruct((2, HALF, D), BF)] * 2,
        compiler_params=_params(4),
        cost_estimate=pl.CostEstimate(
            flops=2 * 2 * 256 * D * W, bytes_accessed=2 * 256 * D * 2, transcendentals=0
        ),
        name="forward_low",
    )(codes, dec)


def _join_kernel(own_low_ref, own_ref, got_low_ref, got_ref, out_ref):
    for t in range(2):
        out_ref[t] = (own_low_ref[t].astype(F32) + got_low_ref[t].astype(F32)).astype(BF)
        out_ref[2 + t] = (own_ref[t].astype(F32) + got_ref[t].astype(F32)).astype(BF)


def _join(*parts):
    return pl.pallas_call(
        _join_kernel,
        in_specs=[WHOLE] * 4,
        out_specs=WHOLE,
        out_shape=jax.ShapeDtypeStruct((LAYERS, HALF, D), BF),
        compiler_params=_params(4),
        cost_estimate=pl.CostEstimate(
            flops=4 * HALF * D, bytes_accessed=3 * 4 * HALF * D * 2, transcendentals=0
        ),
        name="join",
    )(*parts)


def _settle_kernel(pieces_ref, *rest):
    target_refs, errors_ref, recon_refs, rows_ref, turn_ref = (
        rest[:4], rest[4], rest[5:9], rest[9], rest[10]
    )
    y = lax.axis_index("y")
    for j in range(4):
        turn_ref[lax.rem(y + 4 - j, 4)] = target_refs[j][...].astype(F32)
    for j in range(4):
        rows_ref[2 * j : 2 * j + 2] = turn_ref[j]
    summed = lax.fori_loop(
        0, 64, lambda i, acc: acc + pieces_ref[i].astype(F32), jnp.zeros((8, D), F32), unroll=8
    )
    errors = (summed - rows_ref[...]).astype(BF)
    rows_ref[...] = summed
    for j in range(4):
        turn_ref[j] = rows_ref[2 * j : 2 * j + 2]
    for j in range(4):
        recon_refs[j][...] = turn_ref[lax.rem(y + j, 4)].astype(BF)

    def spread(i, carry):
        errors_ref[i] = errors
        return carry

    lax.fori_loop(0, 64, spread, 0, unroll=8)


def _settle(pieces, targets):
    return pl.pallas_call(
        _settle_kernel,
        in_specs=[WHOLE] * 5,
        out_specs=[WHOLE] * 5,
        out_shape=[jax.ShapeDtypeStruct((64, 8, D), BF)]
        + [jax.ShapeDtypeStruct((2, D), BF)] * 4,
        scratch_shapes=[pltpu.VMEM((8, D), F32), pltpu.VMEM((4, 2, D), F32)],
        compiler_params=_params(4),
        cost_estimate=pl.CostEstimate(
            flops=64 * 8 * D, bytes_accessed=2 * 64 * 8 * D * 2, transcendentals=0
        ),
        name="settle",
    )(pieces, *targets)


def _backward_kernel(
    turned_ref, slope_ref, own_ref, oth_ref, x_own_ref, x_oth_ref, dec_ref, *rest
):
    piece_refs = rest[:4]
    grad_ref, genc_ref, bias_ref, recon_ref, back_ref, pre_ref = rest[4:]
    side, y = _side(), lax.axis_index("y")
    p = pl.program_id(0)

    @pl.when(p == 0)
    def _():
        back_ref[...] = jnp.zeros_like(back_ref)
        for j in range(4):
            recon_ref[lax.rem(y + 4 - j, 4)] = piece_refs[j][...]

    @pl.when(p < PAIRS)
    def _():
        pair = jnp.minimum(p, PAIRS - 1)
        slot = (pair >= LAYERS - side).astype(jnp.int32)
        target = jnp.where(slot > 0, pair - 1, side + pair)
        err = jnp.concatenate([own_ref[target], oth_ref[target]], axis=0)
        back_ref[slot] += lax.dot_general(
            err, dec_ref[pair], (((1,), (1,)), ((), ())), preferred_element_type=F32
        )
        turned = turned_ref[slot]
        for cols in CHUNKS:
            err = jnp.concatenate([own_ref[target, :, cols], oth_ref[target, :, cols]], axis=0)
            grad_ref[0, :, cols] = jnp.dot(turned, err, preferred_element_type=F32).astype(BF)

    @pl.when(p == PAIRS)
    def _():
        for k in range(2):
            pre = (back_ref[k] * slope_ref[k]).astype(BF)
            pre_ref[k] = pre
            bias_ref[k : k + 1] = jnp.sum(pre.astype(F32), axis=0, keepdims=True)

    @pl.when(p >= PAIRS)
    def _():
        k = jnp.maximum(p - PAIRS, 0)
        own, oth = _tokens(x_own_ref, x_oth_ref, k)
        for rows in CHUNKS:
            x = jnp.concatenate([own[:, rows], oth[:, rows]], axis=0)
            genc_ref[0, rows] = lax.dot_general(
                x, pre_ref[k], (((0,), (0,)), ((), ())), preferred_element_type=F32
            ).astype(BF)


def _backward(turned, slope, own, oth, x_own, x_oth, decoder, pieces):
    return pl.pallas_call(
        _backward_kernel,
        grid=(PAIRS + 2,),
        in_specs=[WHOLE] * 11,
        out_specs=[
            pl.BlockSpec((1, W, D), lambda p: (jnp.minimum(p, PAIRS - 1), 0, 0)),
            pl.BlockSpec((1, D, W), lambda p: (jnp.maximum(p - PAIRS, 0), 0, 0)),
            pl.BlockSpec((2, W), lambda p: (0, 0)),
            pl.BlockSpec((4, 2, D), lambda p: (0, 0, 0)),
        ],
        scratch_shapes=[pltpu.VMEM((2, 2 * HALF, W), F32), pltpu.VMEM((2, 2 * HALF, W), BF)],
        out_shape=[
            jax.ShapeDtypeStruct((PAIRS, W, D), BF),
            jax.ShapeDtypeStruct((2, D, W), BF),
            jax.ShapeDtypeStruct((2, W), F32),
            jax.ShapeDtypeStruct((4, 2, D), BF),
        ],
        compiler_params=_params(12),
        cost_estimate=pl.CostEstimate(
            flops=4 * PAIRS * 256 * D * W + 4 * 256 * D * W,
            bytes_accessed=PAIRS * W * D * 2 + 2 * D * W * 2,
            transcendentals=0,
        ),
        name="backward",
    )(turned, slope, own, oth, x_own, x_oth, decoder, *pieces)


def _around_y(pieces):
    return [pieces[0]] + [
        lax.ppermute(pieces[j], "y", [(i, (i + j) % 4) for i in range(4)]) for j in (1, 2, 3)
    ]


def per_device(resid_in, resid_out, encoder, enc_bias, decoder, active):
    spread, *targets = _prepare(resid_in, resid_out)
    own = lax.all_to_all(spread, DP, 0, 0)
    oth = lax.ppermute(own, "core", SWAP)
    targets[1:], own = lax.optimization_barrier((targets[1:], own))
    targets = _around_y(targets)
    part_own, part_oth, codes, turned, slope, dec = _forward(
        own, oth, encoder, decoder, enc_bias, active
    )
    got = lax.ppermute(part_oth, "core", SWAP)
    low_own, low_oth = _forward_low(codes, dec)
    got_low = lax.ppermute(low_oth, "core", SWAP)
    part = _join(low_own, part_own, got_low, got)
    part, targets = lax.optimization_barrier((part, targets))
    pieces = lax.all_to_all(part.reshape(64, 8, D), GRID_AXES, 0, 0)
    errors, *recon = _settle(pieces, targets)
    err_own = lax.all_to_all(errors, GRID_AXES, 0, 0).reshape(LAYERS, HALF, D)
    err_oth = lax.ppermute(err_own, "core", SWAP)
    recon, err_own = lax.optimization_barrier((recon, err_own))
    recon = _around_y(recon)
    grad_decoder, grad_encoder, grad_bias, recon = _backward(
        turned, slope, err_own, err_oth, own, oth, dec, recon
    )
    return recon, grad_encoder, grad_bias, grad_decoder


def solution(mesh):
    fine = Mesh(mesh.devices.reshape(4, 2, 2, 2, 4), ALL)
    in_specs = (
        P(None, DP, None),
        P(None, ALL, None),
        P(None, None, ALL),
        P(None, ALL),
        P(None, ALL, None),
        P(),
    )
    out_specs = (P(None, ALL, None), P(None, None, ALL), P(None, ALL), P(None, ALL, None))
    return jax.shard_map(
        per_device, mesh=fine, in_specs=in_specs, out_specs=out_specs, check_vma=False
    )
```

```python
import jax
import jax.numpy as jnp
from jax import lax
from jax.experimental import pallas as pl
from jax.experimental.pallas import tpu as pltpu
from jax.sharding import Mesh
from jax.sharding import PartitionSpec as P

FEAT = 16384
BLOCK = 128
LAYERS = 4
D = 3584
W = 256
HALF = 128
TILES = 8
HROW = 16
PAIRS = 5
GRID_AXES = ("y", "x", "zl", "zh")
DP = ("zh", "y")
ALL = ("x", "zl", "core", "zh", "y")
BF = jnp.bfloat16
F32 = jnp.float32
SWAP = [(0, 1), (1, 0)]

VMEM = pltpu.MemorySpace.VMEM
HBM = pltpu.MemorySpace.HBM
WHOLE = pl.BlockSpec(memory_space=VMEM)
CHUNK = 512
CHUNKS = [slice(c, c + CHUNK) for c in range(0, D, CHUNK)]


def _hbm(x):
    return pltpu.with_memory_space_constraint(x, HBM)


def _vmem(x):
    return pltpu.with_memory_space_constraint(x, VMEM)


def _params(mib):
    return pltpu.CompilerParams(vmem_limit_bytes=mib << 20)


def _tokens(own_ref, oth_ref, k):
    return own_ref[:, k].reshape(HALF, D), oth_ref[:, k].reshape(HALF, D)


def _side():
    return lax.axis_index("x") // 2


def _prepare_kernel(in_hbm, out_hbm, spread_ref, *rest):
    piece_refs, sem = rest[:4], rest[4]
    side, core, y = _side(), lax.axis_index("core"), lax.axis_index("y")
    copies = []
    for k, layer in enumerate((side, LAYERS - 1 - side)):
        for i in range(TILES):
            copies.append(
                pltpu.make_async_copy(
                    in_hbm.at[layer, pl.ds(pl.multiple_of(core * HROW, HROW), HROW)],
                    spread_ref.at[i, k],
                    sem.at[k * TILES + i],
                )
            )
    for j in range(4):
        copies.append(
            pltpu.make_async_copy(
                out_hbm.at[lax.rem(y + j, 4)], piece_refs[j], sem.at[2 * TILES + j]
            )
        )
    for copy in copies:
        copy.start()
    for copy in copies:
        copy.wait()


def _prepare(resid_in, resid_out):
    return pl.pallas_call(
        _prepare_kernel,
        in_specs=[pl.BlockSpec(memory_space=HBM)] * 2,
        out_specs=[WHOLE] * 5,
        out_shape=[jax.ShapeDtypeStruct((TILES, 2, HROW, D), BF)]
        + [jax.ShapeDtypeStruct((2, D), BF)] * 4,
        scratch_shapes=[pltpu.SemaphoreType.DMA((2 * TILES + 4,))],
        compiler_params=_params(2),
        name="prepare",
    )(_hbm(resid_in), _hbm(resid_out))


def _decode(t, side, codes_ref, dec_ref, own_ref, oth_ref, at):
    has_first = t >= side
    has_second = t + 1 >= LAYERS - side
    one = jnp.maximum(t - side, 0)

    def sweep(part):
        for cols in CHUNKS:
            value = part(cols).astype(BF)
            own_ref[at, :, cols] = value[:HALF]
            oth_ref[at, :, cols] = value[HALF:]

    def first(cols):
        return jnp.dot(codes_ref[0], dec_ref[one, :, cols], preferred_element_type=F32)

    def both(cols):
        return first(cols) + jnp.dot(
            codes_ref[1], dec_ref[t + 1, :, cols], preferred_element_type=F32
        )

    @pl.when(has_second)
    def _():
        sweep(both)

    @pl.when(jnp.logical_and(has_first, jnp.logical_not(has_second)))
    def _():
        sweep(first)

    @pl.when(jnp.logical_not(has_first))
    def _():
        own_ref[at] = jnp.zeros((HALF, D), BF)
        oth_ref[at] = jnp.zeros((HALF, D), BF)


def _forward_kernel(
    own_ref, oth_ref, enc_ref, dec_ref, bias_ref, active_ref,
    part_own_ref, part_oth_ref, codes_ref, turned_ref, slope_ref,
):
    x, zl, core = lax.axis_index("x"), lax.axis_index("zl"), lax.axis_index("core")
    zh, y = lax.axis_index("zh"), lax.axis_index("y")
    side = _side()
    rank = (((x * 2 + zl) * 2 + core) * 2 + zh) * 4 + y
    block = rank * (W // BLOCK) - side * (FEAT // BLOCK)
    for k, layer in enumerate((side, LAYERS - 1 - side)):
        rows = jnp.concatenate(_tokens(own_ref, oth_ref, k), axis=0)
        listed = active_ref[layer]
        keep = [
            jnp.broadcast_to(
                jnp.max((listed == block + b).astype(F32), axis=1, keepdims=True), (TILES, BLOCK)
            )
            for b in range(W // BLOCK)
        ]
        keep = jnp.concatenate(keep, axis=1)
        keep = jnp.broadcast_to(keep[:, None, :], (TILES, HROW, W)).reshape(HALF, W)
        keep = jnp.concatenate([keep, keep], axis=0)
        pre = jnp.dot(rows, enc_ref[k], preferred_element_type=F32) + bias_ref[k : k + 1]
        positive = jnp.maximum(pre, 0.0)
        kept = keep * positive
        codes = kept * positive
        codes_ref[k] = codes.astype(BF)
        turned_ref[k] = codes.T.astype(BF)
        slope_ref[k] = 2.0 * kept
    _decode(3, side, codes_ref, dec_ref, part_own_ref, part_oth_ref, 1)
    _decode(2, side, codes_ref, dec_ref, part_own_ref, part_oth_ref, 0)


def _forward(own, oth, encoder, decoder, bias, active):
    return pl.pallas_call(
        _forward_kernel,
        in_specs=[WHOLE] * 6,
        out_specs=[WHOLE] * 5,
        out_shape=[
            jax.ShapeDtypeStruct((2, HALF, D), BF),
            jax.ShapeDtypeStruct((2, HALF, D), BF),
            jax.ShapeDtypeStruct((2, 2 * HALF, W), BF),
            jax.ShapeDtypeStruct((2, W, 2 * HALF), BF),
            jax.ShapeDtypeStruct((2, 2 * HALF, W), F32),
        ],
        compiler_params=_params(6),
        cost_estimate=pl.CostEstimate(
            flops=2 * 5 * 256 * D * W, bytes_accessed=2 * 256 * D * 2, transcendentals=0
        ),
        name="forward",
    )(own, oth, encoder, decoder, bias, active)


def _forward_low_kernel(codes_ref, dec_ref, part_own_ref, part_oth_ref):
    for t in (1, 0):
        _decode(t, _side(), codes_ref, dec_ref, part_own_ref, part_oth_ref, t)


def _forward_low(codes, dec):
    return pl.pallas_call(
        _forward_low_kernel,
        in_specs=[WHOLE, WHOLE],
        out_specs=[WHOLE, WHOLE],
        out_shape=[jax.ShapeDtypeStruct((2, HALF, D), BF)] * 2,
        compiler_params=_params(4),
        cost_estimate=pl.CostEstimate(
            flops=2 * 2 * 256 * D * W, bytes_accessed=2 * 256 * D * 2, transcendentals=0
        ),
        name="forward_low",
    )(codes, dec)


def _join_kernel(own_low_ref, own_ref, got_low_ref, got_ref, out_ref):
    for t in range(2):
        out_ref[t] = (own_low_ref[t].astype(F32) + got_low_ref[t].astype(F32)).astype(BF)
        out_ref[2 + t] = (own_ref[t].astype(F32) + got_ref[t].astype(F32)).astype(BF)


def _join(*parts):
    return pl.pallas_call(
        _join_kernel,
        in_specs=[WHOLE] * 4,
        out_specs=WHOLE,
        out_shape=jax.ShapeDtypeStruct((LAYERS, HALF, D), BF),
        compiler_params=_params(4),
        cost_estimate=pl.CostEstimate(
            flops=4 * HALF * D, bytes_accessed=3 * 4 * HALF * D * 2, transcendentals=0
        ),
        name="join",
    )(*parts)


def _settle_kernel(pieces_ref, *rest):
    target_refs, errors_ref, recon_refs, rows_ref, turn_ref = (
        rest[:4], rest[4], rest[5:9], rest[9], rest[10]
    )
    y = lax.axis_index("y")
    for j in range(4):
        turn_ref[lax.rem(y + 4 - j, 4)] = target_refs[j][...].astype(F32)
    for j in range(4):
        rows_ref[2 * j : 2 * j + 2] = turn_ref[j]
    summed = lax.fori_loop(
        0, 64, lambda i, acc: acc + pieces_ref[i].astype(F32), jnp.zeros((8, D), F32), unroll=8
    )
    errors = (summed - rows_ref[...]).astype(BF)
    rows_ref[...] = summed
    for j in range(4):
        turn_ref[j] = rows_ref[2 * j : 2 * j + 2]
    for j in range(4):
        recon_refs[j][...] = turn_ref[lax.rem(y + j, 4)].astype(BF)

    def spread(i, carry):
        errors_ref[i] = errors
        return carry

    lax.fori_loop(0, 64, spread, 0, unroll=8)


def _settle(pieces, targets):
    return pl.pallas_call(
        _settle_kernel,
        in_specs=[WHOLE] * 5,
        out_specs=[WHOLE] * 5,
        out_shape=[jax.ShapeDtypeStruct((64, 8, D), BF)]
        + [jax.ShapeDtypeStruct((2, D), BF)] * 4,
        scratch_shapes=[pltpu.VMEM((8, D), F32), pltpu.VMEM((4, 2, D), F32)],
        compiler_params=_params(4),
        cost_estimate=pl.CostEstimate(
            flops=64 * 8 * D, bytes_accessed=2 * 64 * 8 * D * 2, transcendentals=0
        ),
        name="settle",
    )(pieces, *targets)


def _backward_kernel(
    turned_ref, slope_ref, own_ref, oth_ref, x_own_ref, x_oth_ref, dec_ref, *rest
):
    piece_refs = rest[:4]
    grad_ref, genc_ref, bias_ref, recon_ref, back_ref, pre_ref = rest[4:]
    side, y = _side(), lax.axis_index("y")
    p = pl.program_id(0)

    @pl.when(p == 0)
    def _():
        back_ref[...] = jnp.zeros_like(back_ref)
        for j in range(4):
            recon_ref[lax.rem(y + 4 - j, 4)] = piece_refs[j][...]

    @pl.when(p < PAIRS)
    def _():
        pair = jnp.minimum(p, PAIRS - 1)
        slot = (pair >= LAYERS - side).astype(jnp.int32)
        target = jnp.where(slot > 0, pair - 1, side + pair)
        err = jnp.concatenate([own_ref[target], oth_ref[target]], axis=0)
        back_ref[slot] += lax.dot_general(
            err, dec_ref[pair], (((1,), (1,)), ((), ())), preferred_element_type=F32
        )
        turned = turned_ref[slot]
        for cols in CHUNKS:
            err = jnp.concatenate([own_ref[target, :, cols], oth_ref[target, :, cols]], axis=0)
            grad_ref[0, :, cols] = jnp.dot(turned, err, preferred_element_type=F32).astype(BF)

    @pl.when(p == PAIRS)
    def _():
        for k in range(2):
            pre = (back_ref[k] * slope_ref[k]).astype(BF)
            pre_ref[k] = pre
            bias_ref[k : k + 1] = jnp.sum(pre.astype(F32), axis=0, keepdims=True)

    @pl.when(p >= PAIRS)
    def _():
        k = jnp.maximum(p - PAIRS, 0)
        own, oth = _tokens(x_own_ref, x_oth_ref, k)
        for rows in CHUNKS:
            x = jnp.concatenate([own[:, rows], oth[:, rows]], axis=0)
            genc_ref[0, rows] = lax.dot_general(
                x, pre_ref[k], (((0,), (0,)), ((), ())), preferred_element_type=F32
            ).astype(BF)


def _backward(turned, slope, own, oth, x_own, x_oth, decoder, pieces):
    return pl.pallas_call(
        _backward_kernel,
        grid=(PAIRS + 2,),
        in_specs=[WHOLE] * 11,
        out_specs=[
            pl.BlockSpec((1, W, D), lambda p: (jnp.minimum(p, PAIRS - 1), 0, 0)),
            pl.BlockSpec((1, D, W), lambda p: (jnp.maximum(p - PAIRS, 0), 0, 0)),
            pl.BlockSpec((2, W), lambda p: (0, 0)),
            pl.BlockSpec((4, 2, D), lambda p: (0, 0, 0)),
        ],
        scratch_shapes=[pltpu.VMEM((2, 2 * HALF, W), F32), pltpu.VMEM((2, 2 * HALF, W), BF)],
        out_shape=[
            jax.ShapeDtypeStruct((PAIRS, W, D), BF),
            jax.ShapeDtypeStruct((2, D, W), BF),
            jax.ShapeDtypeStruct((2, W), F32),
            jax.ShapeDtypeStruct((4, 2, D), BF),
        ],
        compiler_params=_params(12),
        cost_estimate=pl.CostEstimate(
            flops=4 * PAIRS * 256 * D * W + 4 * 256 * D * W,
            bytes_accessed=PAIRS * W * D * 2 + 2 * D * W * 2,
            transcendentals=0,
        ),
        name="backward",
    )(turned, slope, own, oth, x_own, x_oth, decoder, *pieces)


def _around_y(pieces):
    return [pieces[0]] + [
        lax.ppermute(pieces[j], "y", [(i, (i + j) % 4) for i in range(4)]) for j in (1, 2, 3)
    ]


def per_device(resid_in, resid_out, encoder, enc_bias, decoder, active):
    enc, dec = (lax.ppermute(w, "core", [(0, 0), (1, 1)]) for w in (encoder, decoder))
    spread, *targets = _prepare(resid_in, resid_out)
    own = lax.all_to_all(spread, DP, 0, 0)
    oth = lax.ppermute(own, "core", SWAP)
    targets[1:], own = lax.optimization_barrier((targets[1:], own))
    targets = _around_y(targets)
    oth, targets, enc, dec = lax.optimization_barrier((oth, targets, enc, dec))
    part_own, part_oth, codes, turned, slope = _forward(own, oth, enc, dec, enc_bias, active)
    got = lax.ppermute(part_oth, "core", SWAP)
    low_own, low_oth = _forward_low(codes, dec)
    got_low = lax.ppermute(low_oth, "core", SWAP)
    part = _join(low_own, part_own, got_low, got)
    part, targets = lax.optimization_barrier((part, targets))
    pieces = lax.all_to_all(part.reshape(64, 8, D), GRID_AXES, 0, 0)
    errors, *recon = _settle(pieces, targets)
    err_own = lax.all_to_all(errors, GRID_AXES, 0, 0).reshape(LAYERS, HALF, D)
    err_oth = lax.ppermute(err_own, "core", SWAP)
    recon, err_own = lax.optimization_barrier((recon, err_own))
    recon = _around_y(recon)
    grad_decoder, grad_encoder, grad_bias, recon = _backward(
        turned, slope, err_own, err_oth, own, oth, dec, recon
    )
    return recon, grad_encoder, grad_bias, grad_decoder


def solution(mesh):
    fine = Mesh(mesh.devices.reshape(4, 2, 2, 2, 4), ALL)
    in_specs = (
        P(None, DP, None),
        P(None, ALL, None),
        P(None, None, ALL),
        P(None, ALL),
        P(None, ALL, None),
        P(),
    )
    out_specs = (P(None, ALL, None), P(None, None, ALL), P(None, ALL), P(None, ALL, None))
    return jax.shard_map(
        per_device, mesh=fine, in_specs=in_specs, out_specs=out_specs, check_vma=False
    )
```

```python
import functools

import jax
import jax.numpy as jnp
from jax import lax
from jax.experimental import pallas as pl
from jax.experimental.pallas import tpu as pltpu
from jax.sharding import Mesh
from jax.sharding import PartitionSpec as P

FEAT = 16384
BLOCK = 128
LAYERS = 4
D = 3584
W = 256
HALF = 128
TILES = 8
HROW = 16
PAIRS = 5
DP = ("zh", "y")
ALL = ("x", "zl", "core", "zh", "y")
BF = jnp.bfloat16
F32 = jnp.float32
SWAP = [(0, 1), (1, 0)]
QUARTER = 128
BOX = 32


def _rank(x, zl, core, zh, y):
    return (((x * 2 + zl) * 2 + core) * 2 + zh) * 4 + y


def _pairs(move):
    return [
        (_rank(x, zl, core, zh, y), _rank(*move(x, zl, core, zh, y)))
        for x in range(4)
        for zl in range(2)
        for core in range(2)
        for zh in range(2)
        for y in range(4)
    ]


def _ring(flip):
    return _pairs(
        lambda x, zl, core, zh, y: (x ^ (flip * core), zl, core, zh, y ^ (flip * (1 - core)))
    )


RING = {flip: _ring(flip) for flip in (1, 3)}
ALONG_Y = {
    flip: _pairs(lambda x, zl, core, zh, y, flip=flip: (x, zl, core, zh, y ^ flip)) for flip in (1, 3)
}
ACROSS = _pairs(lambda x, zl, core, zh, y: (x, zl, core, zh ^ 1, y))
GROUPS = [
    [_rank(x, zl, 0, zh, y) for x in range(4) for zl in range(2) for zh in range(2)] for y in range(4)
] + [
    [_rank(x, zl, 1, zh, y) for y in range(4) for zl in range(2) for zh in range(2)] for x in range(4)
]

VMEM = pltpu.MemorySpace.VMEM
HBM = pltpu.MemorySpace.HBM
WHOLE = pl.BlockSpec(memory_space=VMEM)
CHUNK = 512
CHUNKS = [slice(c, c + CHUNK) for c in range(0, D, CHUNK)]


def _hbm(x):
    return pltpu.with_memory_space_constraint(x, HBM)


def _vmem(x):
    return pltpu.with_memory_space_constraint(x, VMEM)


def _params(mib):
    return pltpu.CompilerParams(vmem_limit_bytes=mib << 20)


def _tokens(own_ref, oth_ref, k):
    return own_ref[:, k].reshape(HALF, D), oth_ref[:, k].reshape(HALF, D)


def _side():
    return lax.axis_index("x") // 2


def _prepare_kernel(in_hbm, out_hbm, mine_ref, *rest):
    piece_refs, sem = rest[:4], rest[4]
    side, core, y = _side(), lax.axis_index("core"), lax.axis_index("y")
    rows = pl.ds(pl.multiple_of(core * HROW, HROW), HROW)
    copies = [
        pltpu.make_async_copy(in_hbm.at[layer, rows], mine_ref.at[k], sem.at[k])
        for k, layer in enumerate((side, LAYERS - 1 - side))
    ] + [
        pltpu.make_async_copy(out_hbm.at[lax.rem(y + j, 4)], piece_refs[j], sem.at[2 + j])
        for j in range(4)
    ]
    for copy in copies:
        copy.start()
    for copy in copies:
        copy.wait()


def _prepare(resid_in, resid_out):
    return pl.pallas_call(
        _prepare_kernel,
        in_specs=[pl.BlockSpec(memory_space=HBM)] * 2,
        out_specs=[WHOLE] * 5,
        out_shape=[jax.ShapeDtypeStruct((2, HROW, D), BF)] + [jax.ShapeDtypeStruct((2, D), BF)] * 4,
        scratch_shapes=[pltpu.SemaphoreType.DMA((6,))],
        compiler_params=_params(2),
        name="prepare",
    )(_hbm(resid_in), _hbm(resid_out))


def _plain(kernel, out_shape, name, *operands, scratch=(), alias=None):
    return pl.pallas_call(
        kernel,
        in_specs=[WHOLE] * len(operands),
        out_specs=jax.tree.map(lambda _: WHOLE, out_shape),
        out_shape=out_shape,
        scratch_shapes=scratch,
        input_output_aliases=alias or {},
        compiler_params=_params(4),
        name=name,
    )(*operands)


TILE_FROM = ((0, 0), (0, 1), (0, 3), (0, 2), (1, 0), (1, 1), (1, 3), (1, 2))


def _arrange_kernel(*refs):
    zh, y = lax.axis_index("zh"), lax.axis_index("y")
    for piece_ref, (across, flip) in zip(refs[:TILES], TILE_FROM):
        tile = lax.rem(zh + across, 2) * 4 + lax.bitwise_xor(y, flip)
        refs[TILES][tile] = piece_ref[...]


def _gather_inputs(mine):
    far = lax.ppermute(mine, ALL, ACROSS)
    mine_1, mine_3 = (lax.ppermute(mine, ALL, ALONG_Y[flip]) for flip in (1, 3))
    far_3, far_1 = (lax.ppermute(far, ALL, ALONG_Y[flip]) for flip in (3, 1))
    mine_2 = lax.ppermute(mine_1, ALL, ALONG_Y[3])
    far_2 = lax.ppermute(far_3, ALL, ALONG_Y[1])
    return _plain(
        _arrange_kernel,
        jax.ShapeDtypeStruct((TILES, 2, HROW, D), BF),
        "arrange",
        mine, mine_1, mine_3, mine_2, far, far_1, far_3, far_2,
    )


def _place(quarter, i):
    core = lax.axis_index("core")
    return jnp.where(core == 0, quarter, i), jnp.where(core == 0, i, quarter)


def _me():
    return jnp.where(lax.axis_index("core") == 0, lax.axis_index("y"), lax.axis_index("x"))


def _decode(t, side, codes_ref, dec_ref, own_ref, oth_ref, at):
    has_first = t >= side
    has_second = t + 1 >= LAYERS - side
    one = jnp.maximum(t - side, 0)

    def sweep(part):
        for cols in CHUNKS:
            value = part(cols).astype(BF)
            own_ref[at, :, cols] = value[:HALF]
            oth_ref[at, :, cols] = value[HALF:]

    def first(cols):
        return jnp.dot(codes_ref[0], dec_ref[one, :, cols], preferred_element_type=F32)

    def both(cols):
        return first(cols) + jnp.dot(
            codes_ref[1], dec_ref[t + 1, :, cols], preferred_element_type=F32
        )

    @pl.when(has_second)
    def _():
        sweep(both)

    @pl.when(jnp.logical_and(has_first, jnp.logical_not(has_second)))
    def _():
        sweep(first)

    @pl.when(jnp.logical_not(has_first))
    def _():
        own_ref[at] = jnp.zeros((HALF, D), BF)
        oth_ref[at] = jnp.zeros((HALF, D), BF)


def _forward_kernel(
    own_ref, oth_ref, enc_hbm, dec_hbm, bias_ref, active_ref,
    part_own_ref, part_oth_ref, codes_ref, turned_ref, slope_ref, dec_ref, enc_ref, enc_sem, dec_sem,
):
    enc_copies = [
        pltpu.make_async_copy(enc_hbm.at[k], enc_ref.at[k], enc_sem.at[k]) for k in range(2)
    ]
    dec_copies = [
        pltpu.make_async_copy(dec_hbm.at[p], dec_ref.at[p], dec_sem.at[p]) for p in range(PAIRS)
    ]
    for copy in enc_copies + dec_copies[::-1]:
        copy.start()
    x, zl, core = lax.axis_index("x"), lax.axis_index("zl"), lax.axis_index("core")
    zh, y = lax.axis_index("zh"), lax.axis_index("y")
    side = _side()
    rank = (((x * 2 + zl) * 2 + core) * 2 + zh) * 4 + y
    block = rank * (W // BLOCK) - side * (FEAT // BLOCK)
    for k, layer in enumerate((side, LAYERS - 1 - side)):
        rows = jnp.concatenate(_tokens(own_ref, oth_ref, k), axis=0)
        listed = active_ref[layer]
        keep = [
            jnp.broadcast_to(
                jnp.max((listed == block + b).astype(F32), axis=1, keepdims=True), (TILES, BLOCK)
            )
            for b in range(W // BLOCK)
        ]
        keep = jnp.concatenate(keep, axis=1)
        keep = jnp.broadcast_to(keep[:, None, :], (TILES, HROW, W)).reshape(HALF, W)
        keep = jnp.concatenate([keep, keep], axis=0)
        enc_copies[k].wait()
        pre = jnp.dot(rows, enc_ref[k], preferred_element_type=F32) + bias_ref[k : k + 1]
        positive = jnp.maximum(pre, 0.0)
        kept = keep * positive
        codes = kept * positive
        codes_ref[k] = codes.astype(BF)
        turned_ref[k] = codes.T.astype(BF)
        slope_ref[k] = 2.0 * kept
    for p in (4, 3, 2):
        dec_copies[p].wait()
    _decode(3, side, codes_ref, dec_ref, part_own_ref, part_oth_ref, 1)
    dec_copies[1].wait()
    _decode(2, side, codes_ref, dec_ref, part_own_ref, part_oth_ref, 0)
    dec_copies[0].wait()


def _forward(own, oth, encoder, decoder, bias, active):
    hbm = pl.BlockSpec(memory_space=HBM)
    return pl.pallas_call(
        _forward_kernel,
        in_specs=[WHOLE, WHOLE, hbm, hbm, WHOLE, WHOLE],
        out_specs=[WHOLE] * 6,
        out_shape=[
            jax.ShapeDtypeStruct((2, HALF, D), BF),
            jax.ShapeDtypeStruct((2, HALF, D), BF),
            jax.ShapeDtypeStruct((2, 2 * HALF, W), BF),
            jax.ShapeDtypeStruct((2, W, 2 * HALF), BF),
            jax.ShapeDtypeStruct((2, 2 * HALF, W), F32),
            jax.ShapeDtypeStruct((PAIRS, W, D), BF),
        ],
        scratch_shapes=[
            pltpu.VMEM((2, D, W), BF),
            pltpu.SemaphoreType.DMA((2,)),
            pltpu.SemaphoreType.DMA((PAIRS,)),
        ],
        compiler_params=_params(10),
        cost_estimate=pl.CostEstimate(
            flops=2 * 5 * 256 * D * W,
            bytes_accessed=(2 * D * W + PAIRS * W * D) * 2,
            transcendentals=0,
        ),
        name="forward",
    )(own, oth, _hbm(encoder), _hbm(decoder), bias, active)


def _forward_low_kernel(codes_ref, dec_ref, part_own_ref, part_oth_ref):
    for t in (1, 0):
        _decode(t, _side(), codes_ref, dec_ref, part_own_ref, part_oth_ref, t)


def _forward_low(codes, dec):
    return pl.pallas_call(
        _forward_low_kernel,
        in_specs=[WHOLE, WHOLE],
        out_specs=[WHOLE, WHOLE],
        out_shape=[jax.ShapeDtypeStruct((2, HALF, D), BF)] * 2,
        compiler_params=_params(4),
        cost_estimate=pl.CostEstimate(
            flops=2 * 2 * 256 * D * W, bytes_accessed=2 * 256 * D * 2, transcendentals=0
        ),
        name="forward_low",
    )(codes, dec)


def _join_kernel(
    own_low_ref, own_ref, got_low_ref, got_ref, mine_ref, to1_ref, to3_ref, far1_ref, far3_ref
):
    outs = {0: (mine_ref, mine_ref), 1: (to1_ref, to1_ref), 3: (to3_ref, to3_ref), 2: (far1_ref, far3_ref)}
    for flip, (first_ref, second_ref) in outs.items():
        for i in range(4):
            t, x = _place(lax.bitwise_xor(_me(), flip), i)
            rows = pl.ds(pl.multiple_of(x * BOX, BOX), BOX)
            out_ref = first_ref if i < 2 else second_ref
            at = (i % 2 if flip == 2 else i) * BOX

            def add(one_ref, two_ref, index, out_ref=out_ref, at=at, rows=rows):
                value = one_ref[index, rows].astype(F32) + two_ref[index, rows].astype(F32)
                out_ref[at : at + BOX] = value.astype(out_ref.dtype)

            @pl.when(t < 2)
            def _(add=add, t=t):
                add(own_low_ref, got_low_ref, jnp.minimum(t, 1))

            @pl.when(t >= 2)
            def _(add=add, t=t):
                add(own_ref, got_ref, jnp.maximum(t - 2, 0))


def _fold_kernel(at, quarter_ref, got_ref, out_ref):
    rows = slice(at, at + QUARTER // 2)
    out_ref[rows] = (quarter_ref[rows].astype(F32) + got_ref[...].astype(F32)).astype(BF)


def _total_kernel(mine_ref, one_ref, three_ref, out_ref):
    out_ref[...] = (
        mine_ref[...] + one_ref[...].astype(F32) + three_ref[...].astype(F32)
    ).astype(BF)


def _reduce_ring(parts):
    quarter = jax.ShapeDtypeStruct((QUARTER, D), BF)
    half = jax.ShapeDtypeStruct((QUARTER // 2, D), BF)
    mine, to1, to3, far1, far3 = _plain(
        _join_kernel,
        [jax.ShapeDtypeStruct((QUARTER, D), F32), quarter, quarter, half, half],
        "join",
        *parts,
    )
    got1 = lax.ppermute(far1, ALL, RING[1])
    got3 = lax.ppermute(far3, ALL, RING[3])
    to3 = _plain(functools.partial(_fold_kernel, 0), quarter, "fold_low", to3, got1, alias={0: 0})
    from3 = lax.ppermute(to3, ALL, RING[3])
    to1 = _plain(
        functools.partial(_fold_kernel, QUARTER // 2), quarter, "fold_high", to1, got3, alias={0: 0}
    )
    from1 = lax.ppermute(to1, ALL, RING[1])
    return _plain(_total_kernel, quarter, "total", mine, from1, from3)


def _half_kernel(at, quarter_ref, out_ref):
    out_ref[...] = quarter_ref[at : at + QUARTER // 2]


def _assemble_kernel(mine_ref, one_ref, three_ref, far1_ref, far3_ref, out_ref):
    refs = {0: (mine_ref, mine_ref), 1: (one_ref, one_ref), 3: (three_ref, three_ref), 2: (far1_ref, far3_ref)}
    for flip, (first_ref, second_ref) in refs.items():
        for i in range(4):
            t, x = _place(lax.bitwise_xor(_me(), flip), i)
            in_ref = first_ref if i < 2 else second_ref
            at = (i % 2 if flip == 2 else i) * BOX
            out_ref[t, pl.ds(pl.multiple_of(x * BOX, BOX), BOX)] = in_ref[at : at + BOX]


def _gather_ring(quarter):
    half = jax.ShapeDtypeStruct((QUARTER // 2, D), BF)
    one = lax.ppermute(quarter, ALL, RING[1])
    three = lax.ppermute(quarter, ALL, RING[3])
    pass3 = _plain(functools.partial(_half_kernel, 0), half, "half_low", one)
    far1 = lax.ppermute(pass3, ALL, RING[3])
    pass1 = _plain(functools.partial(_half_kernel, QUARTER // 2), half, "half_high", three)
    far3 = lax.ppermute(pass1, ALL, RING[1])
    return _plain(
        _assemble_kernel,
        jax.ShapeDtypeStruct((LAYERS, HALF, D), BF),
        "assemble",
        quarter, one, three, far1, far3,
    )


def _settle_kernel(pieces_ref, *rest):
    target_refs, errors_ref, recon_refs, rows_ref, turn_ref = (
        rest[:4], rest[4], rest[5:9], rest[9], rest[10]
    )
    y = lax.axis_index("y")
    for j in range(4):
        turn_ref[lax.rem(y + 4 - j, 4)] = target_refs[j][...].astype(F32)
    for j in range(4):
        rows_ref[2 * j : 2 * j + 2] = turn_ref[j]
    summed = lax.fori_loop(
        0, 16, lambda i, acc: acc + pieces_ref[i].astype(F32), jnp.zeros((8, D), F32), unroll=8
    )
    errors = (summed - rows_ref[...]).astype(BF)
    rows_ref[...] = summed
    for j in range(4):
        turn_ref[j] = rows_ref[2 * j : 2 * j + 2]
    for j in range(4):
        recon_refs[j][...] = turn_ref[lax.rem(y + j, 4)].astype(BF)

    def spread(i, carry):
        errors_ref[i] = errors
        return carry

    lax.fori_loop(0, 16, spread, 0, unroll=8)


def _settle(pieces, targets):
    return pl.pallas_call(
        _settle_kernel,
        in_specs=[WHOLE] * 5,
        out_specs=[WHOLE] * 5,
        out_shape=[jax.ShapeDtypeStruct((16, 8, D), BF)]
        + [jax.ShapeDtypeStruct((2, D), BF)] * 4,
        scratch_shapes=[pltpu.VMEM((8, D), F32), pltpu.VMEM((4, 2, D), F32)],
        compiler_params=_params(4),
        cost_estimate=pl.CostEstimate(
            flops=16 * 8 * D, bytes_accessed=2 * 16 * 8 * D * 2, transcendentals=0
        ),
        name="settle",
    )(pieces, *targets)


def _backward_kernel(
    turned_ref, slope_ref, own_ref, oth_ref, x_own_ref, x_oth_ref, dec_ref, *rest
):
    piece_refs = rest[:4]
    grad_ref, genc_ref, bias_ref, recon_ref, back_ref, pre_ref = rest[4:]
    side, y = _side(), lax.axis_index("y")
    p = pl.program_id(0)

    @pl.when(p == 0)
    def _():
        back_ref[...] = jnp.zeros_like(back_ref)
        for j in range(4):
            recon_ref[lax.rem(y + 4 - j, 4)] = piece_refs[j][...]

    @pl.when(p < PAIRS)
    def _():
        pair = jnp.minimum(p, PAIRS - 1)
        slot = (pair >= LAYERS - side).astype(jnp.int32)
        target = jnp.where(slot > 0, pair - 1, side + pair)
        err = jnp.concatenate([own_ref[target], oth_ref[target]], axis=0)
        back_ref[slot] += lax.dot_general(
            err, dec_ref[pair], (((1,), (1,)), ((), ())), preferred_element_type=F32
        )
        turned = turned_ref[slot]
        for cols in CHUNKS:
            err = jnp.concatenate([own_ref[target, :, cols], oth_ref[target, :, cols]], axis=0)
            grad_ref[0, :, cols] = jnp.dot(turned, err, preferred_element_type=F32).astype(BF)

    @pl.when(p == PAIRS)
    def _():
        for k in range(2):
            pre = (back_ref[k] * slope_ref[k]).astype(BF)
            pre_ref[k] = pre
            bias_ref[k : k + 1] = jnp.sum(pre.astype(F32), axis=0, keepdims=True)

    @pl.when(p >= PAIRS)
    def _():
        k = jnp.maximum(p - PAIRS, 0)
        own, oth = _tokens(x_own_ref, x_oth_ref, k)
        for rows in CHUNKS:
            x = jnp.concatenate([own[:, rows], oth[:, rows]], axis=0)
            genc_ref[0, rows] = lax.dot_general(
                x, pre_ref[k], (((0,), (0,)), ((), ())), preferred_element_type=F32
            ).astype(BF)


def _backward(turned, slope, own, oth, x_own, x_oth, decoder, pieces):
    return pl.pallas_call(
        _backward_kernel,
        grid=(PAIRS + 2,),
        in_specs=[WHOLE] * 11,
        out_specs=[
            pl.BlockSpec((1, W, D), lambda p: (jnp.minimum(p, PAIRS - 1), 0, 0)),
            pl.BlockSpec((1, D, W), lambda p: (jnp.maximum(p - PAIRS, 0), 0, 0)),
            pl.BlockSpec((2, W), lambda p: (0, 0)),
            pl.BlockSpec((4, 2, D), lambda p: (0, 0, 0)),
        ],
        scratch_shapes=[pltpu.VMEM((2, 2 * HALF, W), F32), pltpu.VMEM((2, 2 * HALF, W), BF)],
        out_shape=[
            jax.ShapeDtypeStruct((PAIRS, W, D), BF),
            jax.ShapeDtypeStruct((2, D, W), BF),
            jax.ShapeDtypeStruct((2, W), F32),
            jax.ShapeDtypeStruct((4, 2, D), BF),
        ],
        compiler_params=_params(12),
        cost_estimate=pl.CostEstimate(
            flops=4 * PAIRS * 256 * D * W + 4 * 256 * D * W,
            bytes_accessed=PAIRS * W * D * 2 + 2 * D * W * 2,
            transcendentals=0,
        ),
        name="backward",
    )(turned, slope, own, oth, x_own, x_oth, decoder, *pieces)


def _around_y(pieces):
    return [pieces[0]] + [
        lax.ppermute(pieces[j], "y", [(i, (i + j) % 4) for i in range(4)]) for j in (1, 2, 3)
    ]


def per_device(resid_in, resid_out, encoder, enc_bias, decoder, active):
    mine, *targets = _prepare(resid_in, resid_out)
    own = _gather_inputs(mine)
    oth = lax.ppermute(own, "core", SWAP)
    targets[1:], own = lax.optimization_barrier((targets[1:], own))
    targets = _around_y(targets)
    part_own, part_oth, codes, turned, slope, dec = _forward(
        own, oth, encoder, decoder, enc_bias, active
    )
    got = lax.ppermute(part_oth, "core", SWAP)
    low_own, low_oth = _forward_low(codes, dec)
    got_low = lax.ppermute(low_oth, "core", SWAP)
    quarter = _reduce_ring((low_own, part_own, got_low, got))
    quarter, targets = lax.optimization_barrier((quarter, targets))
    pieces = lax.all_to_all(quarter.reshape(16, 8, D), ALL, 0, 0, axis_index_groups=GROUPS)
    errors, *recon = _settle(pieces, targets)
    quarter = lax.all_to_all(errors, ALL, 0, 0, axis_index_groups=GROUPS).reshape(QUARTER, D)
    quarter, recon = lax.optimization_barrier((quarter, recon))
    err_own = _gather_ring(quarter)
    err_oth = lax.ppermute(err_own, "core", SWAP)
    recon, err_own = lax.optimization_barrier((recon, err_own))
    recon = _around_y(recon)
    grad_decoder, grad_encoder, grad_bias, recon = _backward(
        turned, slope, err_own, err_oth, own, oth, dec, recon
    )
    return recon, grad_encoder, grad_bias, grad_decoder


def solution(mesh):
    fine = Mesh(mesh.devices.reshape(4, 2, 2, 2, 4), ALL)
    in_specs = (
        P(None, DP, None),
        P(None, ALL, None),
        P(None, None, ALL),
        P(None, ALL),
        P(None, ALL, None),
        P(),
    )
    out_specs = (P(None, ALL, None), P(None, None, ALL), P(None, ALL), P(None, ALL, None))
    return jax.shard_map(
        per_device, mesh=fine, in_specs=in_specs, out_specs=out_specs, check_vma=False
    )
```

```python
import functools

import jax
import jax.numpy as jnp
from jax import lax
from jax.experimental import pallas as pl
from jax.experimental.pallas import tpu as pltpu
from jax.sharding import Mesh
from jax.sharding import PartitionSpec as P

FEAT = 16384
BLOCK = 128
LAYERS = 4
D = 3584
W = 256
HALF = 128
TILES = 8
HROW = 16
PAIRS = 5
DP = ("zh", "y")
ALL = ("x", "zl", "core", "zh", "y")
BF = jnp.bfloat16
F32 = jnp.float32
SWAP = [(0, 1), (1, 0)]
QUARTER = 128
BOX = 32


def _rank(x, zl, core, zh, y):
    return (((x * 2 + zl) * 2 + core) * 2 + zh) * 4 + y


def _pairs(move):
    return [
        (_rank(x, zl, core, zh, y), _rank(*move(x, zl, core, zh, y)))
        for x in range(4)
        for zl in range(2)
        for core in range(2)
        for zh in range(2)
        for y in range(4)
    ]


def _ring(flip):
    return _pairs(
        lambda x, zl, core, zh, y: (x ^ (flip * core), zl, core, zh, y ^ (flip * (1 - core)))
    )


RING = {flip: _ring(flip) for flip in (1, 3)}
ALONG_Y = {
    flip: _pairs(lambda x, zl, core, zh, y, flip=flip: (x, zl, core, zh, y ^ flip)) for flip in (1, 3)
}
ACROSS = _pairs(lambda x, zl, core, zh, y: (x, zl, core, zh ^ 1, y))
GROUPS = [
    [_rank(x, zl, 0, zh, y) for x in range(4) for zl in range(2) for zh in range(2)] for y in range(4)
] + [
    [_rank(x, zl, 1, zh, y) for y in range(4) for zl in range(2) for zh in range(2)] for x in range(4)
]

VMEM = pltpu.MemorySpace.VMEM
HBM = pltpu.MemorySpace.HBM
WHOLE = pl.BlockSpec(memory_space=VMEM)
CHUNK = 512
CHUNKS = [slice(c, c + CHUNK) for c in range(0, D, CHUNK)]


def _hbm(x):
    return pltpu.with_memory_space_constraint(x, HBM)


def _vmem(x):
    return pltpu.with_memory_space_constraint(x, VMEM)


def _params(mib):
    return pltpu.CompilerParams(vmem_limit_bytes=mib << 20)


def _tokens(own_ref, oth_ref, k):
    return own_ref[:, k].reshape(HALF, D), oth_ref[:, k].reshape(HALF, D)


def _side():
    return lax.axis_index("x") // 2


def _prepare_kernel(in_hbm, out_hbm, mine_ref, *rest):
    piece_refs, sem = rest[:4], rest[4]
    side, core, y = _side(), lax.axis_index("core"), lax.axis_index("y")
    rows = pl.ds(pl.multiple_of(core * HROW, HROW), HROW)
    copies = [
        pltpu.make_async_copy(in_hbm.at[layer, rows], mine_ref.at[k], sem.at[k])
        for k, layer in enumerate((side, LAYERS - 1 - side))
    ] + [
        pltpu.make_async_copy(out_hbm.at[lax.rem(y + j, 4)], piece_refs[j], sem.at[2 + j])
        for j in range(4)
    ]
    for copy in copies:
        copy.start()
    for copy in copies:
        copy.wait()


def _prepare(resid_in, resid_out):
    return pl.pallas_call(
        _prepare_kernel,
        in_specs=[pl.BlockSpec(memory_space=HBM)] * 2,
        out_specs=[WHOLE] * 5,
        out_shape=[jax.ShapeDtypeStruct((2, HROW, D), BF)] + [jax.ShapeDtypeStruct((2, D), BF)] * 4,
        scratch_shapes=[pltpu.SemaphoreType.DMA((6,))],
        compiler_params=_params(2),
        name="prepare",
    )(_hbm(resid_in), _hbm(resid_out))


def _plain(kernel, out_shape, name, *operands, scratch=(), alias=None):
    return pl.pallas_call(
        kernel,
        in_specs=[WHOLE] * len(operands),
        out_specs=jax.tree.map(lambda _: WHOLE, out_shape),
        out_shape=out_shape,
        scratch_shapes=scratch,
        input_output_aliases=alias or {},
        compiler_params=_params(4),
        name=name,
    )(*operands)


TILE_FROM = ((0, 0), (0, 1), (0, 3), (0, 2), (1, 0), (1, 1), (1, 3), (1, 2))


def _arrange_kernel(*refs):
    zh, y = lax.axis_index("zh"), lax.axis_index("y")
    for piece_ref, (across, flip) in zip(refs[:TILES], TILE_FROM):
        tile = lax.rem(zh + across, 2) * 4 + lax.bitwise_xor(y, flip)
        refs[TILES][tile] = piece_ref[...]


def _gather_inputs(mine, staged):
    far = lax.ppermute(mine, ALL, ACROSS)
    mine_1, mine_3 = (lax.ppermute(mine, ALL, ALONG_Y[flip]) for flip in (1, 3))
    far, staged = lax.optimization_barrier((far, staged))
    far_3, far_1 = (lax.ppermute(far, ALL, ALONG_Y[flip]) for flip in (3, 1))
    mine_2 = lax.ppermute(mine_1, ALL, ALONG_Y[3])
    far_2 = lax.ppermute(far_3, ALL, ALONG_Y[1])
    own = _plain(
        _arrange_kernel,
        jax.ShapeDtypeStruct((TILES, 2, HROW, D), BF),
        "arrange",
        mine, mine_1, mine_3, mine_2, far, far_1, far_3, far_2,
    )
    return own, staged


def _place(core, quarter, i):
    return jnp.where(core == 0, quarter, i), jnp.where(core == 0, i, quarter)


def _me(core):
    return jnp.where(core == 0, lax.axis_index("y"), lax.axis_index("x"))


def _decode(t, side, codes_ref, dec_ref, own_ref, oth_ref, at):
    has_first = t >= side
    has_second = t + 1 >= LAYERS - side
    one = jnp.maximum(t - side, 0)

    def sweep(part):
        for cols in CHUNKS:
            value = part(cols).astype(BF)
            own_ref[at, :, cols] = value[:HALF]
            oth_ref[at, :, cols] = value[HALF:]

    def first(cols):
        return jnp.dot(codes_ref[0], dec_ref[one, :, cols], preferred_element_type=F32)

    def both(cols):
        return first(cols) + jnp.dot(
            codes_ref[1], dec_ref[t + 1, :, cols], preferred_element_type=F32
        )

    @pl.when(has_second)
    def _():
        sweep(both)

    @pl.when(jnp.logical_and(has_first, jnp.logical_not(has_second)))
    def _():
        sweep(first)

    @pl.when(jnp.logical_not(has_first))
    def _():
        own_ref[at] = jnp.zeros((HALF, D), BF)
        oth_ref[at] = jnp.zeros((HALF, D), BF)


def _stage_kernel(enc_hbm, dec_hbm, enc_ref, dec_ref, sem):
    copies = [
        pltpu.make_async_copy(enc_hbm, enc_ref, sem.at[0]),
        pltpu.make_async_copy(dec_hbm, dec_ref, sem.at[1]),
    ]
    for copy in copies:
        copy.start()
    for copy in copies:
        copy.wait()


def _stage(encoder, decoder):
    return pl.pallas_call(
        _stage_kernel,
        in_specs=[pl.BlockSpec(memory_space=HBM)] * 2,
        out_specs=[WHOLE, WHOLE],
        out_shape=[
            jax.ShapeDtypeStruct((2, D, W), BF),
            jax.ShapeDtypeStruct((PAIRS, W, D), BF),
        ],
        scratch_shapes=[pltpu.SemaphoreType.DMA((2,))],
        compiler_params=_params(1),
        cost_estimate=pl.CostEstimate(
            flops=0, bytes_accessed=2 * (2 * D * W + PAIRS * W * D) * 2, transcendentals=0
        ),
        name="stage",
    )(_hbm(encoder), _hbm(decoder))


def _forward_kernel(
    own_ref, oth_ref, enc_ref, dec_ref, bias_ref, active_ref,
    part_own_ref, part_oth_ref, codes_ref, turned_ref, slope_ref,
):
    x, zl, core = lax.axis_index("x"), lax.axis_index("zl"), lax.axis_index("core")
    zh, y = lax.axis_index("zh"), lax.axis_index("y")
    side = _side()
    rank = (((x * 2 + zl) * 2 + core) * 2 + zh) * 4 + y
    block = rank * (W // BLOCK) - side * (FEAT // BLOCK)
    for k, layer in enumerate((side, LAYERS - 1 - side)):
        rows = jnp.concatenate(_tokens(own_ref, oth_ref, k), axis=0)
        listed = active_ref[layer]
        keep = [
            jnp.broadcast_to(
                jnp.max((listed == block + b).astype(F32), axis=1, keepdims=True), (TILES, BLOCK)
            )
            for b in range(W // BLOCK)
        ]
        keep = jnp.concatenate(keep, axis=1)
        keep = jnp.broadcast_to(keep[:, None, :], (TILES, HROW, W)).reshape(HALF, W)
        keep = jnp.concatenate([keep, keep], axis=0)
        pre = jnp.dot(rows, enc_ref[k], preferred_element_type=F32) + bias_ref[k : k + 1]
        positive = jnp.maximum(pre, 0.0)
        kept = keep * positive
        codes = kept * positive
        codes_ref[k] = codes.astype(BF)
        turned_ref[k] = codes.T.astype(BF)
        slope_ref[k] = 2.0 * kept
    for t in (0, 1):
        _decode(t, side, codes_ref, dec_ref, part_own_ref, part_oth_ref, t)


def _forward(own, oth, encoder, decoder, bias, active):
    return pl.pallas_call(
        _forward_kernel,
        in_specs=[WHOLE] * 6,
        out_specs=[WHOLE] * 5,
        out_shape=[
            jax.ShapeDtypeStruct((2, HALF, D), BF),
            jax.ShapeDtypeStruct((2, HALF, D), BF),
            jax.ShapeDtypeStruct((2, 2 * HALF, W), BF),
            jax.ShapeDtypeStruct((2, W, 2 * HALF), BF),
            jax.ShapeDtypeStruct((2, 2 * HALF, W), F32),
        ],
        compiler_params=_params(6),
        cost_estimate=pl.CostEstimate(
            flops=2 * 4 * 256 * D * W, bytes_accessed=2 * 256 * D * 2, transcendentals=0
        ),
        name="forward",
    )(own, oth, encoder, decoder, bias, active)


def _forward_high_kernel(codes_ref, dec_ref, part_own_ref, part_oth_ref):
    for t in (2, 3):
        _decode(t, _side(), codes_ref, dec_ref, part_own_ref, part_oth_ref, t - 2)


def _forward_high(codes, dec):
    return pl.pallas_call(
        _forward_high_kernel,
        in_specs=[WHOLE, WHOLE],
        out_specs=[WHOLE, WHOLE],
        out_shape=[jax.ShapeDtypeStruct((2, HALF, D), BF)] * 2,
        compiler_params=_params(4),
        cost_estimate=pl.CostEstimate(
            flops=2 * 3 * 256 * D * W, bytes_accessed=2 * 256 * D * 2, transcendentals=0
        ),
        name="forward_high",
    )(codes, dec)


def _join_kernel(
    own_low_ref, own_ref, got_low_ref, got_ref, mine_ref, to1_ref, to3_ref, far1_ref, far3_ref
):
    outs = {0: (mine_ref, mine_ref), 1: (to1_ref, to1_ref), 3: (to3_ref, to3_ref), 2: (far1_ref, far3_ref)}
    core = lax.axis_index("core")
    for flip, (first_ref, second_ref) in outs.items():
        for i in range(4):
            t, x = _place(core, lax.bitwise_xor(_me(core), flip), i)
            rows = pl.ds(pl.multiple_of(x * BOX, BOX), BOX)
            out_ref = first_ref if i < 2 else second_ref
            at = (i % 2 if flip == 2 else i) * BOX

            def add(one_ref, two_ref, index, out_ref=out_ref, at=at, rows=rows):
                value = one_ref[index, rows].astype(F32) + two_ref[index, rows].astype(F32)
                out_ref[at : at + BOX] = value.astype(out_ref.dtype)

            @pl.when(t < 2)
            def _(add=add, t=t):
                add(own_low_ref, got_low_ref, jnp.minimum(t, 1))

            @pl.when(t >= 2)
            def _(add=add, t=t):
                add(own_ref, got_ref, jnp.maximum(t - 2, 0))


def _fold_kernel(at, quarter_ref, got_ref, out_ref):
    rows = slice(at, at + QUARTER // 2)
    out_ref[rows] = (quarter_ref[rows].astype(F32) + got_ref[...].astype(F32)).astype(BF)


def _total_kernel(mine_ref, one_ref, three_ref, out_ref):
    out_ref[...] = (
        mine_ref[...] + one_ref[...].astype(F32) + three_ref[...].astype(F32)
    ).astype(BF)


def _reduce_ring(parts):
    quarter = jax.ShapeDtypeStruct((QUARTER, D), BF)
    half = jax.ShapeDtypeStruct((QUARTER // 2, D), BF)
    mine, to1, to3, far1, far3 = _plain(
        _join_kernel,
        [jax.ShapeDtypeStruct((QUARTER, D), F32), quarter, quarter, half, half],
        "join",
        *parts,
    )
    got1 = lax.ppermute(far1, ALL, RING[1])
    got3 = lax.ppermute(far3, ALL, RING[3])
    to3 = _plain(functools.partial(_fold_kernel, 0), quarter, "fold_low", to3, got1, alias={0: 0})
    from3 = lax.ppermute(to3, ALL, RING[3])
    to1 = _plain(
        functools.partial(_fold_kernel, QUARTER // 2), quarter, "fold_high", to1, got3, alias={0: 0}
    )
    from1 = lax.ppermute(to1, ALL, RING[1])
    return _plain(_total_kernel, quarter, "total", mine, from1, from3)


def _half_kernel(at, quarter_ref, out_ref):
    out_ref[...] = quarter_ref[at : at + QUARTER // 2]


def _assemble_kernel(other, mine_ref, one_ref, three_ref, far1_ref, far3_ref, out_ref):
    refs = {0: (mine_ref, mine_ref), 1: (one_ref, one_ref), 3: (three_ref, three_ref), 2: (far1_ref, far3_ref)}
    core = lax.axis_index("core")
    core = 1 - core if other else core
    for flip, (first_ref, second_ref) in refs.items():
        for i in range(4):
            t, x = _place(core, lax.bitwise_xor(_me(core), flip), i)
            in_ref = first_ref if i < 2 else second_ref
            at = (i % 2 if flip == 2 else i) * BOX
            out_ref[t, pl.ds(pl.multiple_of(x * BOX, BOX), BOX)] = in_ref[at : at + BOX]


def _gather_ring(quarter):
    half = jax.ShapeDtypeStruct((QUARTER // 2, D), BF)
    one = lax.ppermute(quarter, ALL, RING[1])
    three = lax.ppermute(quarter, ALL, RING[3])
    pass3 = _plain(functools.partial(_half_kernel, 0), half, "half_low", one)
    far1 = lax.ppermute(pass3, ALL, RING[3])
    pass1 = _plain(functools.partial(_half_kernel, QUARTER // 2), half, "half_high", three)
    far3 = lax.ppermute(pass1, ALL, RING[1])
    pieces = (quarter, one, three, far1, far3)
    others = [lax.ppermute(piece, "core", SWAP) for piece in pieces]
    whole = jax.ShapeDtypeStruct((LAYERS, HALF, D), BF)
    own = _plain(functools.partial(_assemble_kernel, False), whole, "assemble_own", *pieces)
    oth = _plain(functools.partial(_assemble_kernel, True), whole, "assemble_oth", *others)
    return own, oth


def _settle_kernel(pieces_ref, *rest):
    target_refs, errors_ref, recon_refs, rows_ref, turn_ref = (
        rest[:4], rest[4], rest[5:9], rest[9], rest[10]
    )
    y = lax.axis_index("y")
    for j in range(4):
        turn_ref[lax.rem(y + 4 - j, 4)] = target_refs[j][...].astype(F32)
    for j in range(4):
        rows_ref[2 * j : 2 * j + 2] = turn_ref[j]
    summed = lax.fori_loop(
        0, 16, lambda i, acc: acc + pieces_ref[i].astype(F32), jnp.zeros((8, D), F32), unroll=8
    )
    errors = (summed - rows_ref[...]).astype(BF)
    rows_ref[...] = summed
    for j in range(4):
        turn_ref[j] = rows_ref[2 * j : 2 * j + 2]
    for j in range(4):
        recon_refs[j][...] = turn_ref[lax.rem(y + j, 4)].astype(BF)

    def spread(i, carry):
        errors_ref[i] = errors
        return carry

    lax.fori_loop(0, 16, spread, 0, unroll=8)


def _settle(pieces, targets):
    return pl.pallas_call(
        _settle_kernel,
        in_specs=[WHOLE] * 5,
        out_specs=[WHOLE] * 5,
        out_shape=[jax.ShapeDtypeStruct((16, 8, D), BF)]
        + [jax.ShapeDtypeStruct((2, D), BF)] * 4,
        scratch_shapes=[pltpu.VMEM((8, D), F32), pltpu.VMEM((4, 2, D), F32)],
        compiler_params=_params(4),
        cost_estimate=pl.CostEstimate(
            flops=16 * 8 * D, bytes_accessed=2 * 16 * 8 * D * 2, transcendentals=0
        ),
        name="settle",
    )(pieces, *targets)


def _backward_kernel(
    turned_ref, slope_ref, own_ref, oth_ref, x_own_ref, x_oth_ref, dec_ref, *rest
):
    piece_refs = rest[:4]
    grad_ref, genc_ref, bias_ref, recon_ref, back_ref, pre_ref = rest[4:]
    side, y = _side(), lax.axis_index("y")
    p = pl.program_id(0)

    @pl.when(p == 0)
    def _():
        back_ref[...] = jnp.zeros_like(back_ref)
        for j in range(4):
            recon_ref[lax.rem(y + 4 - j, 4)] = piece_refs[j][...]

    @pl.when(p < PAIRS)
    def _():
        pair = jnp.minimum(p, PAIRS - 1)
        slot = (pair >= LAYERS - side).astype(jnp.int32)
        target = jnp.where(slot > 0, pair - 1, side + pair)
        err = jnp.concatenate([own_ref[target], oth_ref[target]], axis=0)
        back_ref[slot] += lax.dot_general(
            err, dec_ref[pair], (((1,), (1,)), ((), ())), preferred_element_type=F32
        )
        turned = turned_ref[slot]
        for cols in CHUNKS:
            err = jnp.concatenate([own_ref[target, :, cols], oth_ref[target, :, cols]], axis=0)
            grad_ref[0, :, cols] = jnp.dot(turned, err, preferred_element_type=F32).astype(BF)

    @pl.when(p == PAIRS)
    def _():
        for k in range(2):
            pre = (back_ref[k] * slope_ref[k]).astype(BF)
            pre_ref[k] = pre
            bias_ref[k : k + 1] = jnp.sum(pre.astype(F32), axis=0, keepdims=True)

    @pl.when(p >= PAIRS)
    def _():
        k = jnp.maximum(p - PAIRS, 0)
        own, oth = _tokens(x_own_ref, x_oth_ref, k)
        for rows in CHUNKS:
            x = jnp.concatenate([own[:, rows], oth[:, rows]], axis=0)
            genc_ref[0, rows] = lax.dot_general(
                x, pre_ref[k], (((0,), (0,)), ((), ())), preferred_element_type=F32
            ).astype(BF)


def _backward(turned, slope, own, oth, x_own, x_oth, decoder, pieces):
    return pl.pallas_call(
        _backward_kernel,
        grid=(PAIRS + 2,),
        in_specs=[WHOLE] * 11,
        out_specs=[
            pl.BlockSpec((1, W, D), lambda p: (jnp.minimum(p, PAIRS - 1), 0, 0)),
            pl.BlockSpec((1, D, W), lambda p: (jnp.maximum(p - PAIRS, 0), 0, 0)),
            pl.BlockSpec((2, W), lambda p: (0, 0)),
            pl.BlockSpec((4, 2, D), lambda p: (0, 0, 0)),
        ],
        scratch_shapes=[pltpu.VMEM((2, 2 * HALF, W), F32), pltpu.VMEM((2, 2 * HALF, W), BF)],
        out_shape=[
            jax.ShapeDtypeStruct((PAIRS, W, D), BF),
            jax.ShapeDtypeStruct((2, D, W), BF),
            jax.ShapeDtypeStruct((2, W), F32),
            jax.ShapeDtypeStruct((4, 2, D), BF),
        ],
        compiler_params=_params(12),
        cost_estimate=pl.CostEstimate(
            flops=4 * PAIRS * 256 * D * W + 4 * 256 * D * W,
            bytes_accessed=PAIRS * W * D * 2 + 2 * D * W * 2,
            transcendentals=0,
        ),
        name="backward",
    )(turned, slope, own, oth, x_own, x_oth, decoder, *pieces)


def _around_y(pieces):
    return [pieces[0]] + [
        lax.ppermute(pieces[j], "y", [(i, (i + j) % 4) for i in range(4)]) for j in (1, 2, 3)
    ]


def per_device(resid_in, resid_out, encoder, enc_bias, decoder, active):
    mine, *targets = _prepare(resid_in, resid_out)
    encoder, decoder, mine = lax.optimization_barrier((encoder, decoder, mine))
    own, (enc, dec) = _gather_inputs(mine, _stage(encoder, decoder))
    targets[1:], own = lax.optimization_barrier((targets[1:], own))
    oth = lax.ppermute(own, "core", SWAP)
    targets = _around_y(targets)
    low_own, low_oth, codes, turned, slope = _forward(own, oth, enc, dec, enc_bias, active)
    got_low = lax.ppermute(low_oth, "core", SWAP)
    part_own, part_oth = _forward_high(codes, dec)
    got = lax.ppermute(part_oth, "core", SWAP)
    quarter = _reduce_ring((low_own, part_own, got_low, got))
    quarter, targets = lax.optimization_barrier((quarter, targets))
    pieces = lax.all_to_all(quarter.reshape(16, 8, D), ALL, 0, 0, axis_index_groups=GROUPS)
    errors, *recon = _settle(pieces, targets)
    quarter = lax.all_to_all(errors, ALL, 0, 0, axis_index_groups=GROUPS).reshape(QUARTER, D)
    quarter, recon = lax.optimization_barrier((quarter, recon))
    err_own, err_oth = _gather_ring(quarter)
    recon = _around_y(recon)
    grad_decoder, grad_encoder, grad_bias, recon = _backward(
        turned, slope, err_own, err_oth, own, oth, dec, recon
    )
    return recon, grad_encoder, grad_bias, grad_decoder


def solution(mesh):
    fine = Mesh(mesh.devices.reshape(4, 2, 2, 2, 4), ALL)
    in_specs = (
        P(None, DP, None),
        P(None, ALL, None),
        P(None, None, ALL),
        P(None, ALL),
        P(None, ALL, None),
        P(),
    )
    out_specs = (P(None, ALL, None), P(None, None, ALL), P(None, ALL), P(None, ALL, None))
    return jax.shard_map(
        per_device, mesh=fine, in_specs=in_specs, out_specs=out_specs, check_vma=False
    )
```

```python
import functools

import jax
import jax.numpy as jnp
from jax import lax
from jax.experimental import pallas as pl
from jax.experimental.pallas import tpu as pltpu
from jax.sharding import Mesh
from jax.sharding import PartitionSpec as P

FEAT = 16384
BLOCK = 128
LAYERS = 4
D = 3584
W = 256
HALF = 128
TILES = 8
HROW = 16
PAIRS = 5
DP = ("zh", "y")
ALL = ("x", "zl", "core", "zh", "y")
BF = jnp.bfloat16
F32 = jnp.float32
SWAP = [(0, 1), (1, 0)]
QUARTER = 128
BOX = 32


def _rank(x, zl, core, zh, y):
    return (((x * 2 + zl) * 2 + core) * 2 + zh) * 4 + y


def _pairs(move):
    return [
        (_rank(x, zl, core, zh, y), _rank(*move(x, zl, core, zh, y)))
        for x in range(4)
        for zl in range(2)
        for core in range(2)
        for zh in range(2)
        for y in range(4)
    ]


def _ring(flip):
    return _pairs(
        lambda x, zl, core, zh, y: (x ^ (flip * core), zl, core, zh, y ^ (flip * (1 - core)))
    )


RING = {flip: _ring(flip) for flip in (1, 3)}
ALONG_Y = {
    flip: _pairs(lambda x, zl, core, zh, y, flip=flip: (x, zl, core, zh, y ^ flip)) for flip in (1, 3)
}
ACROSS = _pairs(lambda x, zl, core, zh, y: (x, zl, core, zh ^ 1, y))
GROUPS = [
    [_rank(x, zl, 0, zh, y) for x in range(4) for zl in range(2) for zh in range(2)] for y in range(4)
] + [
    [_rank(x, zl, 1, zh, y) for y in range(4) for zl in range(2) for zh in range(2)] for x in range(4)
]

VMEM = pltpu.MemorySpace.VMEM
HBM = pltpu.MemorySpace.HBM
WHOLE = pl.BlockSpec(memory_space=VMEM)
CHUNK = 512
CHUNKS = [slice(c, c + CHUNK) for c in range(0, D, CHUNK)]


def _hbm(x):
    return pltpu.with_memory_space_constraint(x, HBM)


def _vmem(x):
    return pltpu.with_memory_space_constraint(x, VMEM)


def _params(mib):
    return pltpu.CompilerParams(vmem_limit_bytes=mib << 20)


def _tokens(own_ref, oth_ref, k):
    return own_ref[:, k].reshape(HALF, D), oth_ref[:, k].reshape(HALF, D)


def _side():
    return lax.axis_index("x") // 2


def _prepare_kernel(in_hbm, out_hbm, mine_ref, *rest):
    piece_refs, sem = rest[:4], rest[4]
    side, core, y = _side(), lax.axis_index("core"), lax.axis_index("y")
    rows = pl.ds(pl.multiple_of(core * HROW, HROW), HROW)
    copies = [
        pltpu.make_async_copy(in_hbm.at[layer, rows], mine_ref.at[k], sem.at[k])
        for k, layer in enumerate((side, LAYERS - 1 - side))
    ] + [
        pltpu.make_async_copy(out_hbm.at[lax.rem(y + j, 4)], piece_refs[j], sem.at[2 + j])
        for j in range(4)
    ]
    for copy in copies:
        copy.start()
    for copy in copies:
        copy.wait()


def _prepare(resid_in, resid_out):
    return pl.pallas_call(
        _prepare_kernel,
        in_specs=[pl.BlockSpec(memory_space=HBM)] * 2,
        out_specs=[WHOLE] * 5,
        out_shape=[jax.ShapeDtypeStruct((2, HROW, D), BF)] + [jax.ShapeDtypeStruct((2, D), BF)] * 4,
        scratch_shapes=[pltpu.SemaphoreType.DMA((6,))],
        compiler_params=_params(2),
        name="prepare",
    )(_hbm(resid_in), _hbm(resid_out))


def _plain(kernel, out_shape, name, *operands, scratch=(), alias=None):
    return pl.pallas_call(
        kernel,
        in_specs=[WHOLE] * len(operands),
        out_specs=jax.tree.map(lambda _: WHOLE, out_shape),
        out_shape=out_shape,
        scratch_shapes=scratch,
        input_output_aliases=alias or {},
        compiler_params=_params(4),
        name=name,
    )(*operands)


TILE_FROM = ((0, 0), (0, 1), (0, 3), (0, 2), (1, 0), (1, 1), (1, 3), (1, 2))


def _arrange_kernel(*refs):
    zh, y = lax.axis_index("zh"), lax.axis_index("y")
    for piece_ref, (across, flip) in zip(refs[:TILES], TILE_FROM):
        tile = lax.rem(zh + across, 2) * 4 + lax.bitwise_xor(y, flip)
        refs[TILES][tile] = piece_ref[...]


def _gather_inputs(mine, staged):
    far = lax.ppermute(mine, ALL, ACROSS)
    mine_1, mine_3 = (lax.ppermute(mine, ALL, ALONG_Y[flip]) for flip in (1, 3))
    far, staged = lax.optimization_barrier((far, staged))
    far_3, far_1 = (lax.ppermute(far, ALL, ALONG_Y[flip]) for flip in (3, 1))
    mine_2 = lax.ppermute(mine_1, ALL, ALONG_Y[3])
    far_2 = lax.ppermute(far_3, ALL, ALONG_Y[1])
    own = _plain(
        _arrange_kernel,
        jax.ShapeDtypeStruct((TILES, 2, HROW, D), BF),
        "arrange",
        mine, mine_1, mine_3, mine_2, far, far_1, far_3, far_2,
    )
    return own, staged


def _place(core, quarter, i):
    return jnp.where(core == 0, quarter, i), jnp.where(core == 0, i, quarter)


def _me(core):
    return jnp.where(core == 0, lax.axis_index("y"), lax.axis_index("x"))


def _decode(t, side, codes_ref, dec_ref, own_ref, oth_ref, at):
    has_first = t >= side
    has_second = t + 1 >= LAYERS - side
    one = jnp.maximum(t - side, 0)

    def sweep(part):
        for cols in CHUNKS:
            value = part(cols).astype(BF)
            own_ref[at, :, cols] = value[:HALF]
            oth_ref[at, :, cols] = value[HALF:]

    def first(cols):
        return jnp.dot(codes_ref[0], dec_ref[one, :, cols], preferred_element_type=F32)

    def both(cols):
        return first(cols) + jnp.dot(
            codes_ref[1], dec_ref[t + 1, :, cols], preferred_element_type=F32
        )

    @pl.when(has_second)
    def _():
        sweep(both)

    @pl.when(jnp.logical_and(has_first, jnp.logical_not(has_second)))
    def _():
        sweep(first)

    @pl.when(jnp.logical_not(has_first))
    def _():
        own_ref[at] = jnp.zeros((HALF, D), BF)
        oth_ref[at] = jnp.zeros((HALF, D), BF)


def _stage_kernel(enc_hbm, dec_hbm, enc_ref, dec_ref, sem):
    copies = [
        pltpu.make_async_copy(enc_hbm, enc_ref, sem.at[0]),
        pltpu.make_async_copy(dec_hbm, dec_ref, sem.at[1]),
    ]
    for copy in copies:
        copy.start()
    for copy in copies:
        copy.wait()


def _stage(encoder, decoder):
    return pl.pallas_call(
        _stage_kernel,
        in_specs=[pl.BlockSpec(memory_space=HBM)] * 2,
        out_specs=[WHOLE, WHOLE],
        out_shape=[
            jax.ShapeDtypeStruct((2, D, W), BF),
            jax.ShapeDtypeStruct((PAIRS, W, D), BF),
        ],
        scratch_shapes=[pltpu.SemaphoreType.DMA((2,))],
        compiler_params=_params(1),
        cost_estimate=pl.CostEstimate(
            flops=0, bytes_accessed=2 * (2 * D * W + PAIRS * W * D) * 2, transcendentals=0
        ),
        name="stage",
    )(_hbm(encoder), _hbm(decoder))


def _forward_kernel(
    own_ref, oth_ref, enc_ref, dec_ref, bias_ref, active_ref,
    part_own_ref, part_oth_ref, codes_ref, turned_ref, slope_ref,
):
    x, zl, core = lax.axis_index("x"), lax.axis_index("zl"), lax.axis_index("core")
    zh, y = lax.axis_index("zh"), lax.axis_index("y")
    side = _side()
    rank = (((x * 2 + zl) * 2 + core) * 2 + zh) * 4 + y
    block = rank * (W // BLOCK) - side * (FEAT // BLOCK)
    for k, layer in enumerate((side, LAYERS - 1 - side)):
        rows = jnp.concatenate(_tokens(own_ref, oth_ref, k), axis=0)
        listed = active_ref[layer]
        keep = [
            jnp.broadcast_to(
                jnp.max((listed == block + b).astype(F32), axis=1, keepdims=True), (TILES, BLOCK)
            )
            for b in range(W // BLOCK)
        ]
        keep = jnp.concatenate(keep, axis=1)
        keep = jnp.broadcast_to(keep[:, None, :], (TILES, HROW, W)).reshape(HALF, W)
        keep = jnp.concatenate([keep, keep], axis=0)
        pre = jnp.dot(rows, enc_ref[k], preferred_element_type=F32) + bias_ref[k : k + 1]
        positive = jnp.maximum(pre, 0.0)
        kept = keep * positive
        codes = kept * positive
        codes_ref[k] = codes.astype(BF)
        turned_ref[k] = codes.T.astype(BF)
        slope_ref[k] = 2.0 * kept
    for t in (0, 1):
        _decode(t, side, codes_ref, dec_ref, part_own_ref, part_oth_ref, t)


def _forward(own, oth, encoder, decoder, bias, active):
    return pl.pallas_call(
        _forward_kernel,
        in_specs=[WHOLE] * 6,
        out_specs=[WHOLE] * 5,
        out_shape=[
            jax.ShapeDtypeStruct((2, HALF, D), BF),
            jax.ShapeDtypeStruct((2, HALF, D), BF),
            jax.ShapeDtypeStruct((2, 2 * HALF, W), BF),
            jax.ShapeDtypeStruct((2, W, 2 * HALF), BF),
            jax.ShapeDtypeStruct((2, 2 * HALF, W), F32),
        ],
        compiler_params=_params(6),
        cost_estimate=pl.CostEstimate(
            flops=2 * 4 * 256 * D * W, bytes_accessed=2 * 256 * D * 2, transcendentals=0
        ),
        name="forward",
    )(own, oth, encoder, decoder, bias, active)


def _forward_high_kernel(codes_ref, dec_ref, part_own_ref, part_oth_ref):
    for t in (2, 3):
        _decode(t, _side(), codes_ref, dec_ref, part_own_ref, part_oth_ref, t - 2)


def _forward_high(codes, dec):
    return pl.pallas_call(
        _forward_high_kernel,
        in_specs=[WHOLE, WHOLE],
        out_specs=[WHOLE, WHOLE],
        out_shape=[jax.ShapeDtypeStruct((2, HALF, D), BF)] * 2,
        compiler_params=_params(4),
        cost_estimate=pl.CostEstimate(
            flops=2 * 3 * 256 * D * W, bytes_accessed=2 * 256 * D * 2, transcendentals=0
        ),
        name="forward_high",
    )(codes, dec)


def _join_kernel(
    own_low_ref, own_ref, got_low_ref, got_ref, mine_ref, to1_ref, to3_ref, far1_ref, far3_ref
):
    outs = {0: (mine_ref, mine_ref), 1: (to1_ref, to1_ref), 3: (to3_ref, to3_ref), 2: (far1_ref, far3_ref)}
    core = lax.axis_index("core")
    for flip, (first_ref, second_ref) in outs.items():
        for i in range(4):
            t, x = _place(core, lax.bitwise_xor(_me(core), flip), i)
            rows = pl.ds(pl.multiple_of(x * BOX, BOX), BOX)
            out_ref = first_ref if i < 2 else second_ref
            at = (i % 2 if flip == 2 else i) * BOX

            def add(one_ref, two_ref, index, out_ref=out_ref, at=at, rows=rows):
                value = one_ref[index, rows].astype(F32) + two_ref[index, rows].astype(F32)
                out_ref[at : at + BOX] = value.astype(out_ref.dtype)

            @pl.when(t < 2)
            def _(add=add, t=t):
                add(own_low_ref, got_low_ref, jnp.minimum(t, 1))

            @pl.when(t >= 2)
            def _(add=add, t=t):
                add(own_ref, got_ref, jnp.maximum(t - 2, 0))


def _fold_kernel(at, quarter_ref, got_ref, out_ref):
    rows = slice(at, at + QUARTER // 2)
    out_ref[rows] = (quarter_ref[rows].astype(F32) + got_ref[...].astype(F32)).astype(BF)


def _total_kernel(mine_ref, one_ref, three_ref, out_ref):
    out_ref[...] = (
        mine_ref[...] + one_ref[...].astype(F32) + three_ref[...].astype(F32)
    ).astype(BF)


def _reduce_ring(parts):
    quarter = jax.ShapeDtypeStruct((QUARTER, D), BF)
    half = jax.ShapeDtypeStruct((QUARTER // 2, D), BF)
    mine, to1, to3, far1, far3 = _plain(
        _join_kernel,
        [jax.ShapeDtypeStruct((QUARTER, D), F32), quarter, quarter, half, half],
        "join",
        *parts,
    )
    got1 = lax.ppermute(far1, ALL, RING[1])
    got3 = lax.ppermute(far3, ALL, RING[3])
    to3 = _plain(functools.partial(_fold_kernel, 0), quarter, "fold_low", to3, got1, alias={0: 0})
    from3 = lax.ppermute(to3, ALL, RING[3])
    to1 = _plain(
        functools.partial(_fold_kernel, QUARTER // 2), quarter, "fold_high", to1, got3, alias={0: 0}
    )
    from1 = lax.ppermute(to1, ALL, RING[1])
    return _plain(_total_kernel, quarter, "total", mine, from1, from3)


def _half_kernel(at, quarter_ref, out_ref):
    out_ref[...] = quarter_ref[at : at + QUARTER // 2]


def _assemble_kernel(other, mine_ref, one_ref, three_ref, far1_ref, far3_ref, out_ref):
    refs = {0: (mine_ref, mine_ref), 1: (one_ref, one_ref), 3: (three_ref, three_ref), 2: (far1_ref, far3_ref)}
    core = lax.axis_index("core")
    core = 1 - core if other else core
    for flip, (first_ref, second_ref) in refs.items():
        for i in range(4):
            t, x = _place(core, lax.bitwise_xor(_me(core), flip), i)
            in_ref = first_ref if i < 2 else second_ref
            at = (i % 2 if flip == 2 else i) * BOX
            out_ref[t, pl.ds(pl.multiple_of(x * BOX, BOX), BOX)] = in_ref[at : at + BOX]


def _gather_ring(quarter, recon):
    half = jax.ShapeDtypeStruct((QUARTER // 2, D), BF)
    one = lax.ppermute(quarter, ALL, RING[1])
    three = lax.ppermute(quarter, ALL, RING[3])
    one, three, recon = lax.optimization_barrier((one, three, _around_y(recon)))
    pass3 = _plain(functools.partial(_half_kernel, 0), half, "half_low", one)
    far1 = lax.ppermute(pass3, ALL, RING[3])
    pass1 = _plain(functools.partial(_half_kernel, QUARTER // 2), half, "half_high", three)
    far3 = lax.ppermute(pass1, ALL, RING[1])
    pieces = (quarter, one, three, far1, far3)
    others = [lax.ppermute(piece, "core", SWAP) for piece in pieces]
    whole = jax.ShapeDtypeStruct((LAYERS, HALF, D), BF)
    own = _plain(functools.partial(_assemble_kernel, False), whole, "assemble_own", *pieces)
    oth = _plain(functools.partial(_assemble_kernel, True), whole, "assemble_oth", *others)
    return own, oth, recon


def _settle_kernel(pieces_ref, *rest):
    target_refs, errors_ref, recon_refs, rows_ref, turn_ref = (
        rest[:4], rest[4], rest[5:9], rest[9], rest[10]
    )
    y = lax.axis_index("y")
    for j in range(4):
        turn_ref[lax.rem(y + 4 - j, 4)] = target_refs[j][...].astype(F32)
    for j in range(4):
        rows_ref[2 * j : 2 * j + 2] = turn_ref[j]
    summed = lax.fori_loop(
        0, 16, lambda i, acc: acc + pieces_ref[i].astype(F32), jnp.zeros((8, D), F32), unroll=8
    )
    errors = (summed - rows_ref[...]).astype(BF)
    rows_ref[...] = summed
    for j in range(4):
        turn_ref[j] = rows_ref[2 * j : 2 * j + 2]
    for j in range(4):
        recon_refs[j][...] = turn_ref[lax.rem(y + j, 4)].astype(BF)

    def spread(i, carry):
        errors_ref[i] = errors
        return carry

    lax.fori_loop(0, 16, spread, 0, unroll=8)


def _settle(pieces, targets):
    return pl.pallas_call(
        _settle_kernel,
        in_specs=[WHOLE] * 5,
        out_specs=[WHOLE] * 5,
        out_shape=[jax.ShapeDtypeStruct((16, 8, D), BF)]
        + [jax.ShapeDtypeStruct((2, D), BF)] * 4,
        scratch_shapes=[pltpu.VMEM((8, D), F32), pltpu.VMEM((4, 2, D), F32)],
        compiler_params=_params(4),
        cost_estimate=pl.CostEstimate(
            flops=16 * 8 * D, bytes_accessed=2 * 16 * 8 * D * 2, transcendentals=0
        ),
        name="settle",
    )(pieces, *targets)


def _backward_kernel(
    turned_ref, slope_ref, own_ref, oth_ref, x_own_ref, x_oth_ref, dec_ref, *rest
):
    piece_refs = rest[:4]
    grad_ref, genc_ref, bias_ref, recon_ref, back_ref, pre_ref = rest[4:]
    side, y = _side(), lax.axis_index("y")
    p = pl.program_id(0)

    @pl.when(p == 0)
    def _():
        back_ref[...] = jnp.zeros_like(back_ref)
        for j in range(4):
            recon_ref[lax.rem(y + 4 - j, 4)] = piece_refs[j][...]

    @pl.when(p < PAIRS)
    def _():
        pair = jnp.minimum(p, PAIRS - 1)
        slot = (pair >= LAYERS - side).astype(jnp.int32)
        target = jnp.where(slot > 0, pair - 1, side + pair)
        err = jnp.concatenate([own_ref[target], oth_ref[target]], axis=0)
        back_ref[slot] += lax.dot_general(
            err, dec_ref[pair], (((1,), (1,)), ((), ())), preferred_element_type=F32
        )
        turned = turned_ref[slot]
        for cols in CHUNKS:
            err = jnp.concatenate([own_ref[target, :, cols], oth_ref[target, :, cols]], axis=0)
            grad_ref[0, :, cols] = jnp.dot(turned, err, preferred_element_type=F32).astype(BF)

    @pl.when(p == PAIRS)
    def _():
        for k in range(2):
            pre = (back_ref[k] * slope_ref[k]).astype(BF)
            pre_ref[k] = pre
            bias_ref[k : k + 1] = jnp.sum(pre.astype(F32), axis=0, keepdims=True)

    @pl.when(p >= PAIRS)
    def _():
        k = jnp.maximum(p - PAIRS, 0)
        own, oth = _tokens(x_own_ref, x_oth_ref, k)
        for rows in CHUNKS:
            x = jnp.concatenate([own[:, rows], oth[:, rows]], axis=0)
            genc_ref[0, rows] = lax.dot_general(
                x, pre_ref[k], (((0,), (0,)), ((), ())), preferred_element_type=F32
            ).astype(BF)


def _backward(turned, slope, own, oth, x_own, x_oth, decoder, pieces):
    return pl.pallas_call(
        _backward_kernel,
        grid=(PAIRS + 2,),
        in_specs=[WHOLE] * 11,
        out_specs=[
            pl.BlockSpec((1, W, D), lambda p: (jnp.minimum(p, PAIRS - 1), 0, 0)),
            pl.BlockSpec((1, D, W), lambda p: (jnp.maximum(p - PAIRS, 0), 0, 0)),
            pl.BlockSpec((2, W), lambda p: (0, 0)),
            pl.BlockSpec((4, 2, D), lambda p: (0, 0, 0)),
        ],
        scratch_shapes=[pltpu.VMEM((2, 2 * HALF, W), F32), pltpu.VMEM((2, 2 * HALF, W), BF)],
        out_shape=[
            jax.ShapeDtypeStruct((PAIRS, W, D), BF),
            jax.ShapeDtypeStruct((2, D, W), BF),
            jax.ShapeDtypeStruct((2, W), F32),
            jax.ShapeDtypeStruct((4, 2, D), BF),
        ],
        compiler_params=_params(12),
        cost_estimate=pl.CostEstimate(
            flops=4 * PAIRS * 256 * D * W + 4 * 256 * D * W,
            bytes_accessed=PAIRS * W * D * 2 + 2 * D * W * 2,
            transcendentals=0,
        ),
        name="backward",
    )(turned, slope, own, oth, x_own, x_oth, decoder, *pieces)


def _around_y(pieces):
    return [pieces[0]] + [
        lax.ppermute(pieces[j], "y", [(i, (i + j) % 4) for i in range(4)]) for j in (1, 2, 3)
    ]


def per_device(resid_in, resid_out, encoder, enc_bias, decoder, active):
    mine, *targets = _prepare(resid_in, resid_out)
    encoder, decoder, mine = lax.optimization_barrier((encoder, decoder, mine))
    own, (enc, dec) = _gather_inputs(mine, _stage(encoder, decoder))
    targets[1:], own = lax.optimization_barrier((targets[1:], own))
    oth = lax.ppermute(own, "core", SWAP)
    targets = _around_y(targets)
    low_own, low_oth, codes, turned, slope = _forward(own, oth, enc, dec, enc_bias, active)
    got_low = lax.ppermute(low_oth, "core", SWAP)
    part_own, part_oth = _forward_high(codes, dec)
    got = lax.ppermute(part_oth, "core", SWAP)
    quarter = _reduce_ring((low_own, part_own, got_low, got))
    quarter, targets = lax.optimization_barrier((quarter, targets))
    pieces = lax.all_to_all(quarter.reshape(16, 8, D), ALL, 0, 0, axis_index_groups=GROUPS)
    errors, *recon = _settle(pieces, targets)
    quarter = lax.all_to_all(errors, ALL, 0, 0, axis_index_groups=GROUPS).reshape(QUARTER, D)
    quarter, recon = lax.optimization_barrier((quarter, recon))
    err_own, err_oth, recon = _gather_ring(quarter, recon)
    grad_decoder, grad_encoder, grad_bias, recon = _backward(
        turned, slope, err_own, err_oth, own, oth, dec, recon
    )
    return recon, grad_encoder, grad_bias, grad_decoder


def solution(mesh):
    fine = Mesh(mesh.devices.reshape(4, 2, 2, 2, 4), ALL)
    in_specs = (
        P(None, DP, None),
        P(None, ALL, None),
        P(None, None, ALL),
        P(None, ALL),
        P(None, ALL, None),
        P(),
    )
    out_specs = (P(None, ALL, None), P(None, None, ALL), P(None, ALL), P(None, ALL, None))
    return jax.shard_map(
        per_device, mesh=fine, in_specs=in_specs, out_specs=out_specs, check_vma=False
    )
```

```python
import functools

import jax
import jax.numpy as jnp
from jax import lax
from jax.experimental import pallas as pl
from jax.experimental.pallas import tpu as pltpu
from jax.sharding import Mesh
from jax.sharding import PartitionSpec as P

FEAT = 16384
BLOCK = 128
LAYERS = 4
D = 3584
W = 256
HALF = 128
TILES = 8
HROW = 16
PAIRS = 5
DP = ("zh", "y")
ALL = ("x", "zl", "core", "zh", "y")
BF = jnp.bfloat16
F32 = jnp.float32
SWAP = [(0, 1), (1, 0)]
QUARTER = 128
BOX = 32


def _rank(x, zl, core, zh, y):
    return (((x * 2 + zl) * 2 + core) * 2 + zh) * 4 + y


def _pairs(move):
    return [
        (_rank(x, zl, core, zh, y), _rank(*move(x, zl, core, zh, y)))
        for x in range(4)
        for zl in range(2)
        for core in range(2)
        for zh in range(2)
        for y in range(4)
    ]


def _ring(flip):
    return _pairs(
        lambda x, zl, core, zh, y: (x ^ (flip * core), zl, core, zh, y ^ (flip * (1 - core)))
    )


RING = {flip: _ring(flip) for flip in (1, 3)}
ALONG_Y = {
    flip: _pairs(lambda x, zl, core, zh, y, flip=flip: (x, zl, core, zh, y ^ flip)) for flip in (1, 3)
}
ACROSS = _pairs(lambda x, zl, core, zh, y: (x, zl ^ 1, core, zh ^ 1, y))
GROUPS = [
    [_rank(x, zl, 0, zh, y) for x in range(4) for zl in range(2) for zh in range(2)] for y in range(4)
] + [
    [_rank(x, zl, 1, zh, y) for y in range(4) for zl in range(2) for zh in range(2)] for x in range(4)
]

VMEM = pltpu.MemorySpace.VMEM
HBM = pltpu.MemorySpace.HBM
WHOLE = pl.BlockSpec(memory_space=VMEM)
CHUNK = 512
CHUNKS = [slice(c, c + CHUNK) for c in range(0, D, CHUNK)]


def _hbm(x):
    return pltpu.with_memory_space_constraint(x, HBM)


def _vmem(x):
    return pltpu.with_memory_space_constraint(x, VMEM)


def _params(mib):
    return pltpu.CompilerParams(vmem_limit_bytes=mib << 20)


def _tokens(own_ref, oth_ref, k):
    return own_ref[:, k].reshape(HALF, D), oth_ref[:, k].reshape(HALF, D)


def _side():
    return lax.axis_index("x") // 2


def _prepare_kernel(in_hbm, out_hbm, mine_ref, *rest):
    piece_refs, sem = rest[:4], rest[4]
    side, core, y = _side(), lax.axis_index("core"), lax.axis_index("y")
    rows = pl.ds(pl.multiple_of(core * HROW, HROW), HROW)
    copies = [
        pltpu.make_async_copy(in_hbm.at[layer, rows], mine_ref.at[k], sem.at[k])
        for k, layer in enumerate((side, LAYERS - 1 - side))
    ] + [
        pltpu.make_async_copy(out_hbm.at[lax.rem(y + j, 4)], piece_refs[j], sem.at[2 + j])
        for j in range(4)
    ]
    for copy in copies:
        copy.start()
    for copy in copies:
        copy.wait()


def _prepare(resid_in, resid_out):
    return pl.pallas_call(
        _prepare_kernel,
        in_specs=[pl.BlockSpec(memory_space=HBM)] * 2,
        out_specs=[WHOLE] * 5,
        out_shape=[jax.ShapeDtypeStruct((2, HROW, D), BF)] + [jax.ShapeDtypeStruct((2, D), BF)] * 4,
        scratch_shapes=[pltpu.SemaphoreType.DMA((6,))],
        compiler_params=_params(2),
        name="prepare",
    )(_hbm(resid_in), _hbm(resid_out))


def _plain(kernel, out_shape, name, *operands, scratch=(), alias=None):
    return pl.pallas_call(
        kernel,
        in_specs=[WHOLE] * len(operands),
        out_specs=jax.tree.map(lambda _: WHOLE, out_shape),
        out_shape=out_shape,
        scratch_shapes=scratch,
        input_output_aliases=alias or {},
        compiler_params=_params(4),
        name=name,
    )(*operands)


TILE_FROM = ((0, 0), (0, 1), (0, 3), (0, 2), (1, 0), (1, 1), (1, 3), (1, 2))


def _arrange_kernel(*refs):
    zh, y = lax.axis_index("zh"), lax.axis_index("y")
    for piece_ref, (across, flip) in zip(refs[:TILES], TILE_FROM):
        tile = lax.rem(zh + across, 2) * 4 + lax.bitwise_xor(y, flip)
        refs[TILES][tile] = piece_ref[...]


def _gather_inputs(mine, staged):
    far = lax.ppermute(mine, ALL, ACROSS)
    mine_1, mine_3 = (lax.ppermute(mine, ALL, ALONG_Y[flip]) for flip in (1, 3))
    far, mine_1, mine_3, staged = lax.optimization_barrier((far, mine_1, mine_3, staged))
    far_3, far_1 = (lax.ppermute(far, ALL, ALONG_Y[flip]) for flip in (3, 1))
    mine_2 = lax.ppermute(mine_1, ALL, ALONG_Y[3])
    far_2 = lax.ppermute(far_3, ALL, ALONG_Y[1])
    own = _plain(
        _arrange_kernel,
        jax.ShapeDtypeStruct((TILES, 2, HROW, D), BF),
        "arrange",
        mine, mine_1, mine_3, mine_2, far, far_1, far_3, far_2,
    )
    return own, staged


def _place(core, quarter, i):
    return jnp.where(core == 0, quarter, i), jnp.where(core == 0, i, quarter)


def _me(core):
    return jnp.where(core == 0, lax.axis_index("y"), lax.axis_index("x"))


def _decode(t, side, codes_ref, dec_ref, own_ref, oth_ref, at):
    has_first = t >= side
    has_second = t + 1 >= LAYERS - side
    one = jnp.maximum(t - side, 0)

    def sweep(part):
        for cols in CHUNKS:
            value = part(cols).astype(BF)
            own_ref[at, :, cols] = value[:HALF]
            oth_ref[at, :, cols] = value[HALF:]

    def first(cols):
        return jnp.dot(codes_ref[0], dec_ref[one, :, cols], preferred_element_type=F32)

    def both(cols):
        return first(cols) + jnp.dot(
            codes_ref[1], dec_ref[t + 1, :, cols], preferred_element_type=F32
        )

    @pl.when(has_second)
    def _():
        sweep(both)

    @pl.when(jnp.logical_and(has_first, jnp.logical_not(has_second)))
    def _():
        sweep(first)

    @pl.when(jnp.logical_not(has_first))
    def _():
        own_ref[at] = jnp.zeros((HALF, D), BF)
        oth_ref[at] = jnp.zeros((HALF, D), BF)


def _stage_kernel(enc_hbm, dec_hbm, enc_ref, dec_ref, sem):
    copies = [
        pltpu.make_async_copy(enc_hbm, enc_ref, sem.at[0]),
        pltpu.make_async_copy(dec_hbm, dec_ref, sem.at[1]),
    ]
    for copy in copies:
        copy.start()
    for copy in copies:
        copy.wait()


def _stage(encoder, decoder):
    return pl.pallas_call(
        _stage_kernel,
        in_specs=[pl.BlockSpec(memory_space=HBM)] * 2,
        out_specs=[WHOLE, WHOLE],
        out_shape=[
            jax.ShapeDtypeStruct((2, D, W), BF),
            jax.ShapeDtypeStruct((PAIRS, W, D), BF),
        ],
        scratch_shapes=[pltpu.SemaphoreType.DMA((2,))],
        compiler_params=_params(1),
        cost_estimate=pl.CostEstimate(
            flops=0, bytes_accessed=2 * (2 * D * W + PAIRS * W * D) * 2, transcendentals=0
        ),
        name="stage",
    )(_hbm(encoder), _hbm(decoder))


def _forward_kernel(
    own_ref, oth_ref, enc_ref, dec_ref, bias_ref, active_ref,
    part_own_ref, part_oth_ref, codes_ref, turned_ref, slope_ref,
):
    x, zl, core = lax.axis_index("x"), lax.axis_index("zl"), lax.axis_index("core")
    zh, y = lax.axis_index("zh"), lax.axis_index("y")
    side = _side()
    rank = (((x * 2 + zl) * 2 + core) * 2 + zh) * 4 + y
    block = rank * (W // BLOCK) - side * (FEAT // BLOCK)
    for k, layer in enumerate((side, LAYERS - 1 - side)):
        rows = jnp.concatenate(_tokens(own_ref, oth_ref, k), axis=0)
        listed = active_ref[layer]
        keep = [
            jnp.broadcast_to(
                jnp.max((listed == block + b).astype(F32), axis=1, keepdims=True), (TILES, BLOCK)
            )
            for b in range(W // BLOCK)
        ]
        keep = jnp.concatenate(keep, axis=1)
        keep = jnp.broadcast_to(keep[:, None, :], (TILES, HROW, W)).reshape(HALF, W)
        keep = jnp.concatenate([keep, keep], axis=0)
        pre = jnp.dot(rows, enc_ref[k], preferred_element_type=F32) + bias_ref[k : k + 1]
        positive = jnp.maximum(pre, 0.0)
        kept = keep * positive
        codes = kept * positive
        codes_ref[k] = codes.astype(BF)
        turned_ref[k] = codes.T.astype(BF)
        slope_ref[k] = 2.0 * kept
    for t in (0, 1):
        _decode(t, side, codes_ref, dec_ref, part_own_ref, part_oth_ref, t)


def _forward(own, oth, encoder, decoder, bias, active):
    return pl.pallas_call(
        _forward_kernel,
        in_specs=[WHOLE] * 6,
        out_specs=[WHOLE] * 5,
        out_shape=[
            jax.ShapeDtypeStruct((2, HALF, D), BF),
            jax.ShapeDtypeStruct((2, HALF, D), BF),
            jax.ShapeDtypeStruct((2, 2 * HALF, W), BF),
            jax.ShapeDtypeStruct((2, W, 2 * HALF), BF),
            jax.ShapeDtypeStruct((2, 2 * HALF, W), F32),
        ],
        compiler_params=_params(6),
        cost_estimate=pl.CostEstimate(
            flops=2 * 4 * 256 * D * W, bytes_accessed=2 * 256 * D * 2, transcendentals=0
        ),
        name="forward",
    )(own, oth, encoder, decoder, bias, active)


def _forward_high_kernel(codes_ref, dec_ref, part_own_ref, part_oth_ref):
    for t in (2, 3):
        _decode(t, _side(), codes_ref, dec_ref, part_own_ref, part_oth_ref, t - 2)


def _forward_high(codes, dec):
    return pl.pallas_call(
        _forward_high_kernel,
        in_specs=[WHOLE, WHOLE],
        out_specs=[WHOLE, WHOLE],
        out_shape=[jax.ShapeDtypeStruct((2, HALF, D), BF)] * 2,
        compiler_params=_params(4),
        cost_estimate=pl.CostEstimate(
            flops=2 * 3 * 256 * D * W, bytes_accessed=2 * 256 * D * 2, transcendentals=0
        ),
        name="forward_high",
    )(codes, dec)


def _join_kernel(flips, own_low_ref, own_ref, got_low_ref, got_ref, *out_refs):
    if flips == (2,):
        outs = {2: out_refs}
    else:
        outs = {flip: (out_ref, out_ref) for flip, out_ref in zip(flips, out_refs)}
    core = lax.axis_index("core")
    for flip, (first_ref, second_ref) in outs.items():
        for i in range(4):
            t, x = _place(core, lax.bitwise_xor(_me(core), flip), i)
            rows = pl.ds(pl.multiple_of(x * BOX, BOX), BOX)
            out_ref = first_ref if i < 2 else second_ref
            at = (i % 2 if flip == 2 else i) * BOX

            def add(one_ref, two_ref, index, out_ref=out_ref, at=at, rows=rows):
                value = one_ref[index, rows].astype(F32) + two_ref[index, rows].astype(F32)
                out_ref[at : at + BOX] = value.astype(out_ref.dtype)

            @pl.when(t < 2)
            def _(add=add, t=t):
                add(own_low_ref, got_low_ref, jnp.minimum(t, 1))

            @pl.when(t >= 2)
            def _(add=add, t=t):
                add(own_ref, got_ref, jnp.maximum(t - 2, 0))


def _fold_kernel(at, quarter_ref, got_ref, out_ref):
    rows = slice(at, at + QUARTER // 2)
    out_ref[rows] = (quarter_ref[rows].astype(F32) + got_ref[...].astype(F32)).astype(BF)


def _total_kernel(mine_ref, one_ref, three_ref, out_ref):
    out_ref[...] = (
        mine_ref[...] + one_ref[...].astype(F32) + three_ref[...].astype(F32)
    ).astype(BF)


def _reduce_ring(parts):
    quarter = jax.ShapeDtypeStruct((QUARTER, D), BF)
    half = jax.ShapeDtypeStruct((QUARTER // 2, D), BF)
    far1, far3 = _plain(functools.partial(_join_kernel, (2,)), [half, half], "join_far", *parts)
    mine, to1, to3 = _plain(
        functools.partial(_join_kernel, (0, 1, 3)),
        [jax.ShapeDtypeStruct((QUARTER, D), F32), quarter, quarter],
        "join",
        *parts,
    )
    got1 = lax.ppermute(far1, ALL, RING[1])
    got3 = lax.ppermute(far3, ALL, RING[3])
    to3 = _plain(functools.partial(_fold_kernel, 0), quarter, "fold_low", to3, got1, alias={0: 0})
    from3 = lax.ppermute(to3, ALL, RING[3])
    to1 = _plain(
        functools.partial(_fold_kernel, QUARTER // 2), quarter, "fold_high", to1, got3, alias={0: 0}
    )
    from1 = lax.ppermute(to1, ALL, RING[1])
    return _plain(_total_kernel, quarter, "total", mine, from1, from3)


def _half_kernel(at, quarter_ref, out_ref):
    out_ref[...] = quarter_ref[at : at + QUARTER // 2]


def _assemble_kernel(other, mine_ref, one_ref, three_ref, far1_ref, far3_ref, out_ref):
    refs = {0: (mine_ref, mine_ref), 1: (one_ref, one_ref), 3: (three_ref, three_ref), 2: (far1_ref, far3_ref)}
    core = lax.axis_index("core")
    core = 1 - core if other else core
    for flip, (first_ref, second_ref) in refs.items():
        for i in range(4):
            t, x = _place(core, lax.bitwise_xor(_me(core), flip), i)
            in_ref = first_ref if i < 2 else second_ref
            at = (i % 2 if flip == 2 else i) * BOX
            out_ref[t, pl.ds(pl.multiple_of(x * BOX, BOX), BOX)] = in_ref[at : at + BOX]


def _gather_ring(quarter, recon):
    half = jax.ShapeDtypeStruct((QUARTER // 2, D), BF)
    one = lax.ppermute(quarter, ALL, RING[1])
    three = lax.ppermute(quarter, ALL, RING[3])
    one, three, recon = lax.optimization_barrier((one, three, _around_y(recon)))
    pass3 = _plain(functools.partial(_half_kernel, 0), half, "half_low", one)
    far1 = lax.ppermute(pass3, ALL, RING[3])
    pass1 = _plain(functools.partial(_half_kernel, QUARTER // 2), half, "half_high", three)
    far3 = lax.ppermute(pass1, ALL, RING[1])
    pieces = (quarter, one, three, far1, far3)
    others = [lax.ppermute(piece, "core", SWAP) for piece in pieces]
    whole = jax.ShapeDtypeStruct((LAYERS, HALF, D), BF)
    own = _plain(functools.partial(_assemble_kernel, False), whole, "assemble_own", *pieces)
    oth = _plain(functools.partial(_assemble_kernel, True), whole, "assemble_oth", *others)
    return own, oth, recon


def _settle_kernel(pieces_ref, *rest):
    target_refs, errors_ref, recon_refs, rows_ref, turn_ref = (
        rest[:4], rest[4], rest[5:9], rest[9], rest[10]
    )
    y = lax.axis_index("y")
    for j in range(4):
        turn_ref[lax.rem(y + 4 - j, 4)] = target_refs[j][...].astype(F32)
    for j in range(4):
        rows_ref[2 * j : 2 * j + 2] = turn_ref[j]
    summed = lax.fori_loop(
        0, 16, lambda i, acc: acc + pieces_ref[i].astype(F32), jnp.zeros((8, D), F32), unroll=8
    )
    errors = (summed - rows_ref[...]).astype(BF)
    rows_ref[...] = summed
    for j in range(4):
        turn_ref[j] = rows_ref[2 * j : 2 * j + 2]
    for j in range(4):
        recon_refs[j][...] = turn_ref[lax.rem(y + j, 4)].astype(BF)

    def spread(i, carry):
        errors_ref[i] = errors
        return carry

    lax.fori_loop(0, 16, spread, 0, unroll=8)


def _settle(pieces, targets):
    return pl.pallas_call(
        _settle_kernel,
        in_specs=[WHOLE] * 5,
        out_specs=[WHOLE] * 5,
        out_shape=[jax.ShapeDtypeStruct((16, 8, D), BF)]
        + [jax.ShapeDtypeStruct((2, D), BF)] * 4,
        scratch_shapes=[pltpu.VMEM((8, D), F32), pltpu.VMEM((4, 2, D), F32)],
        compiler_params=_params(4),
        cost_estimate=pl.CostEstimate(
            flops=16 * 8 * D, bytes_accessed=2 * 16 * 8 * D * 2, transcendentals=0
        ),
        name="settle",
    )(pieces, *targets)


def _backward_kernel(
    turned_ref, slope_ref, own_ref, oth_ref, x_own_ref, x_oth_ref, dec_ref, *rest
):
    piece_refs = rest[:4]
    grad_ref, genc_ref, bias_ref, recon_ref, back_ref, pre_ref = rest[4:]
    side, y = _side(), lax.axis_index("y")
    p = pl.program_id(0)

    @pl.when(p == 0)
    def _():
        back_ref[...] = jnp.zeros_like(back_ref)
        for j in range(4):
            recon_ref[lax.rem(y + 4 - j, 4)] = piece_refs[j][...]

    @pl.when(p < PAIRS)
    def _():
        pair = jnp.minimum(p, PAIRS - 1)
        slot = (pair >= LAYERS - side).astype(jnp.int32)
        target = jnp.where(slot > 0, pair - 1, side + pair)
        err = jnp.concatenate([own_ref[target], oth_ref[target]], axis=0)
        back_ref[slot] += lax.dot_general(
            err, dec_ref[pair], (((1,), (1,)), ((), ())), preferred_element_type=F32
        )
        turned = turned_ref[slot]
        for cols in CHUNKS:
            err = jnp.concatenate([own_ref[target, :, cols], oth_ref[target, :, cols]], axis=0)
            grad_ref[0, :, cols] = jnp.dot(turned, err, preferred_element_type=F32).astype(BF)

    @pl.when(p == PAIRS)
    def _():
        for k in range(2):
            pre = (back_ref[k] * slope_ref[k]).astype(BF)
            pre_ref[k] = pre
            bias_ref[k : k + 1] = jnp.sum(pre.astype(F32), axis=0, keepdims=True)

    @pl.when(p >= PAIRS)
    def _():
        k = jnp.maximum(p - PAIRS, 0)
        own, oth = _tokens(x_own_ref, x_oth_ref, k)
        for rows in CHUNKS:
            x = jnp.concatenate([own[:, rows], oth[:, rows]], axis=0)
            genc_ref[0, rows] = lax.dot_general(
                x, pre_ref[k], (((0,), (0,)), ((), ())), preferred_element_type=F32
            ).astype(BF)


def _backward(turned, slope, own, oth, x_own, x_oth, decoder, pieces):
    return pl.pallas_call(
        _backward_kernel,
        grid=(PAIRS + 2,),
        in_specs=[WHOLE] * 11,
        out_specs=[
            pl.BlockSpec((1, W, D), lambda p: (jnp.minimum(p, PAIRS - 1), 0, 0)),
            pl.BlockSpec((1, D, W), lambda p: (jnp.maximum(p - PAIRS, 0), 0, 0)),
            pl.BlockSpec((2, W), lambda p: (0, 0)),
            pl.BlockSpec((4, 2, D), lambda p: (0, 0, 0)),
        ],
        scratch_shapes=[pltpu.VMEM((2, 2 * HALF, W), F32), pltpu.VMEM((2, 2 * HALF, W), BF)],
        out_shape=[
            jax.ShapeDtypeStruct((PAIRS, W, D), BF),
            jax.ShapeDtypeStruct((2, D, W), BF),
            jax.ShapeDtypeStruct((2, W), F32),
            jax.ShapeDtypeStruct((4, 2, D), BF),
        ],
        compiler_params=_params(12),
        cost_estimate=pl.CostEstimate(
            flops=4 * PAIRS * 256 * D * W + 4 * 256 * D * W,
            bytes_accessed=PAIRS * W * D * 2 + 2 * D * W * 2,
            transcendentals=0,
        ),
        name="backward",
    )(turned, slope, own, oth, x_own, x_oth, decoder, *pieces)


def _around_y(pieces):
    return [pieces[0]] + [
        lax.ppermute(pieces[j], "y", [(i, (i + j) % 4) for i in range(4)]) for j in (1, 2, 3)
    ]


def per_device(resid_in, resid_out, encoder, enc_bias, decoder, active):
    mine, *targets = _prepare(resid_in, resid_out)
    encoder, decoder, mine = lax.optimization_barrier((encoder, decoder, mine))
    own, (enc, dec) = _gather_inputs(mine, _stage(encoder, decoder))
    targets[1:], own = lax.optimization_barrier((targets[1:], own))
    oth = lax.ppermute(own, "core", SWAP)
    targets = _around_y(targets)
    low_own, low_oth, codes, turned, slope = _forward(own, oth, enc, dec, enc_bias, active)
    got_low = lax.ppermute(low_oth, "core", SWAP)
    part_own, part_oth = _forward_high(codes, dec)
    got = lax.ppermute(part_oth, "core", SWAP)
    quarter = _reduce_ring((low_own, part_own, got_low, got))
    quarter, targets = lax.optimization_barrier((quarter, targets))
    pieces = lax.all_to_all(quarter.reshape(16, 8, D), ALL, 0, 0, axis_index_groups=GROUPS)
    errors, *recon = _settle(pieces, targets)
    quarter = lax.all_to_all(errors, ALL, 0, 0, axis_index_groups=GROUPS).reshape(QUARTER, D)
    quarter, recon = lax.optimization_barrier((quarter, recon))
    err_own, err_oth, recon = _gather_ring(quarter, recon)
    grad_decoder, grad_encoder, grad_bias, recon = _backward(
        turned, slope, err_own, err_oth, own, oth, dec, recon
    )
    return recon, grad_encoder, grad_bias, grad_decoder


def solution(mesh):
    fine = Mesh(mesh.devices.reshape(4, 2, 2, 2, 4), ALL)
    in_specs = (
        P(None, DP, None),
        P(None, ALL, None),
        P(None, None, ALL),
        P(None, ALL),
        P(None, ALL, None),
        P(),
    )
    out_specs = (P(None, ALL, None), P(None, None, ALL), P(None, ALL), P(None, ALL, None))
    return jax.shard_map(
        per_device, mesh=fine, in_specs=in_specs, out_specs=out_specs, check_vma=False
    )
```

```python
import functools

import jax
import jax.numpy as jnp
from jax import lax
from jax.experimental import pallas as pl
from jax.experimental.pallas import tpu as pltpu
from jax.sharding import Mesh
from jax.sharding import PartitionSpec as P

FEAT = 16384
BLOCK = 128
LAYERS = 4
D = 3584
W = 256
HALF = 128
TILES = 8
HROW = 16
PAIRS = 5
DP = ("zh", "y")
ALL = ("x", "zl", "core", "zh", "y")
BF = jnp.bfloat16
F32 = jnp.float32
SWAP = [(0, 1), (1, 0)]
QUARTER = 128
BOX = 32


def _rank(x, zl, core, zh, y):
    return (((x * 2 + zl) * 2 + core) * 2 + zh) * 4 + y


def _pairs(move):
    return [
        (_rank(x, zl, core, zh, y), _rank(*move(x, zl, core, zh, y)))
        for x in range(4)
        for zl in range(2)
        for core in range(2)
        for zh in range(2)
        for y in range(4)
    ]


def _ring(flip):
    return _pairs(
        lambda x, zl, core, zh, y: (x ^ (flip * core), zl, core, zh, y ^ (flip * (1 - core)))
    )


RING = {flip: _ring(flip) for flip in (1, 3)}
ALONG_Y = {
    flip: _pairs(
        lambda x, zl, core, zh, y, flip=flip: (x, zl, core, zh, y ^ (4 - flip if core else flip))
    )
    for flip in (1, 3)
}
ACROSS = _pairs(lambda x, zl, core, zh, y: (x, zl ^ 1, core, zh ^ 1, y))
GROUPS = [
    [_rank(x, zl, 0, zh, y) for x in range(4) for zl in range(2) for zh in range(2)] for y in range(4)
] + [
    [_rank(x, zl, 1, zh, y) for y in range(4) for zl in range(2) for zh in range(2)] for x in range(4)
]

VMEM = pltpu.MemorySpace.VMEM
HBM = pltpu.MemorySpace.HBM
WHOLE = pl.BlockSpec(memory_space=VMEM)
CHUNK = 512
CHUNKS = [slice(c, c + CHUNK) for c in range(0, D, CHUNK)]


def _hbm(x):
    return pltpu.with_memory_space_constraint(x, HBM)


def _vmem(x):
    return pltpu.with_memory_space_constraint(x, VMEM)


def _params(mib):
    return pltpu.CompilerParams(vmem_limit_bytes=mib << 20)


def _tokens(own_ref, oth_ref, k):
    return own_ref[:, k].reshape(HALF, D), oth_ref[:, k].reshape(HALF, D)


def _side():
    return lax.axis_index("x") // 2


def _prepare_kernel(in_hbm, out_hbm, mine_ref, *rest):
    piece_refs, sem = rest[:4], rest[4]
    side, core, y = _side(), lax.axis_index("core"), lax.axis_index("y")
    rows = pl.ds(pl.multiple_of(core * HROW, HROW), HROW)
    copies = [
        pltpu.make_async_copy(in_hbm.at[layer, rows], mine_ref.at[k], sem.at[k])
        for k, layer in enumerate((side, LAYERS - 1 - side))
    ] + [
        pltpu.make_async_copy(out_hbm.at[lax.rem(y + j, 4)], piece_refs[j], sem.at[2 + j])
        for j in range(4)
    ]
    for copy in copies:
        copy.start()
    for copy in copies:
        copy.wait()


def _prepare(resid_in, resid_out):
    return pl.pallas_call(
        _prepare_kernel,
        in_specs=[pl.BlockSpec(memory_space=HBM)] * 2,
        out_specs=[WHOLE] * 5,
        out_shape=[jax.ShapeDtypeStruct((2, HROW, D), BF)] + [jax.ShapeDtypeStruct((2, D), BF)] * 4,
        scratch_shapes=[pltpu.SemaphoreType.DMA((6,))],
        compiler_params=_params(2),
        name="prepare",
    )(_hbm(resid_in), _hbm(resid_out))


def _plain(kernel, out_shape, name, *operands, scratch=(), alias=None):
    return pl.pallas_call(
        kernel,
        in_specs=[WHOLE] * len(operands),
        out_specs=jax.tree.map(lambda _: WHOLE, out_shape),
        out_shape=out_shape,
        scratch_shapes=scratch,
        input_output_aliases=alias or {},
        compiler_params=_params(4),
        name=name,
    )(*operands)


TILE_FROM = ((0, 0), (0, 1), (0, 3), (0, 2), (1, 0), (1, 1), (1, 3), (1, 2))


def _arrange_kernel(*refs):
    zh, y = lax.axis_index("zh"), lax.axis_index("y")
    core = lax.axis_index("core")
    for piece_ref, (across, flip) in zip(refs[:TILES], TILE_FROM):
        flip = jnp.where(core == 0, flip, (4 - flip) % 4)
        tile = lax.rem(zh + across, 2) * 4 + lax.bitwise_xor(y, flip)
        refs[TILES][tile] = piece_ref[...]


def _gather_inputs(mine, staged):
    far = lax.ppermute(mine, ALL, ACROSS)
    mine_1, mine_3 = (lax.ppermute(mine, ALL, ALONG_Y[flip]) for flip in (1, 3))
    far, mine_1, mine_3, staged = lax.optimization_barrier((far, mine_1, mine_3, staged))
    far_3, far_1 = (lax.ppermute(far, ALL, ALONG_Y[flip]) for flip in (3, 1))
    mine_2 = lax.ppermute(mine_1, ALL, ALONG_Y[3])
    far_2 = lax.ppermute(far_3, ALL, ALONG_Y[1])
    own = _plain(
        _arrange_kernel,
        jax.ShapeDtypeStruct((TILES, 2, HROW, D), BF),
        "arrange",
        mine, mine_1, mine_3, mine_2, far, far_1, far_3, far_2,
    )
    return own, staged


def _place(core, quarter, i):
    return jnp.where(core == 0, quarter, i), jnp.where(core == 0, i, quarter)


def _me(core):
    return jnp.where(core == 0, lax.axis_index("y"), lax.axis_index("x"))


def _decode(t, side, codes_ref, dec_ref, own_ref, oth_ref, at):
    has_first = t >= side
    has_second = t + 1 >= LAYERS - side
    one = jnp.maximum(t - side, 0)

    def sweep(part):
        for cols in CHUNKS:
            value = part(cols).astype(BF)
            own_ref[at, :, cols] = value[:HALF]
            oth_ref[at, :, cols] = value[HALF:]

    def first(cols):
        return jnp.dot(codes_ref[0], dec_ref[one, :, cols], preferred_element_type=F32)

    def both(cols):
        return first(cols) + jnp.dot(
            codes_ref[1], dec_ref[t + 1, :, cols], preferred_element_type=F32
        )

    @pl.when(has_second)
    def _():
        sweep(both)

    @pl.when(jnp.logical_and(has_first, jnp.logical_not(has_second)))
    def _():
        sweep(first)

    @pl.when(jnp.logical_not(has_first))
    def _():
        own_ref[at] = jnp.zeros((HALF, D), BF)
        oth_ref[at] = jnp.zeros((HALF, D), BF)


def _stage_kernel(enc_hbm, dec_hbm, enc_ref, dec_ref, sem):
    copies = [
        pltpu.make_async_copy(enc_hbm, enc_ref, sem.at[0]),
        pltpu.make_async_copy(dec_hbm, dec_ref, sem.at[1]),
    ]
    for copy in copies:
        copy.start()
    for copy in copies:
        copy.wait()


def _stage(encoder, decoder):
    return pl.pallas_call(
        _stage_kernel,
        in_specs=[pl.BlockSpec(memory_space=HBM)] * 2,
        out_specs=[WHOLE, WHOLE],
        out_shape=[
            jax.ShapeDtypeStruct((2, D, W), BF),
            jax.ShapeDtypeStruct((PAIRS, W, D), BF),
        ],
        scratch_shapes=[pltpu.SemaphoreType.DMA((2,))],
        compiler_params=_params(1),
        cost_estimate=pl.CostEstimate(
            flops=0, bytes_accessed=2 * (2 * D * W + PAIRS * W * D) * 2, transcendentals=0
        ),
        name="stage",
    )(_hbm(encoder), _hbm(decoder))


def _forward_kernel(
    own_ref, oth_ref, enc_ref, dec_ref, bias_ref, active_ref,
    part_own_ref, part_oth_ref, codes_ref, turned_ref, slope_ref,
):
    x, zl, core = lax.axis_index("x"), lax.axis_index("zl"), lax.axis_index("core")
    zh, y = lax.axis_index("zh"), lax.axis_index("y")
    side = _side()
    rank = (((x * 2 + zl) * 2 + core) * 2 + zh) * 4 + y
    block = rank * (W // BLOCK) - side * (FEAT // BLOCK)
    for k, layer in enumerate((side, LAYERS - 1 - side)):
        rows = jnp.concatenate(_tokens(own_ref, oth_ref, k), axis=0)
        listed = active_ref[layer]
        keep = [
            jnp.broadcast_to(
                jnp.max((listed == block + b).astype(F32), axis=1, keepdims=True), (TILES, BLOCK)
            )
            for b in range(W // BLOCK)
        ]
        keep = jnp.concatenate(keep, axis=1)
        keep = jnp.broadcast_to(keep[:, None, :], (TILES, HROW, W)).reshape(HALF, W)
        keep = jnp.concatenate([keep, keep], axis=0)
        pre = jnp.dot(rows, enc_ref[k], preferred_element_type=F32) + bias_ref[k : k + 1]
        positive = jnp.maximum(pre, 0.0)
        kept = keep * positive
        codes = kept * positive
        codes_ref[k] = codes.astype(BF)
        turned_ref[k] = codes.T.astype(BF)
        slope_ref[k] = 2.0 * kept
    for t in (0, 1):
        _decode(t, side, codes_ref, dec_ref, part_own_ref, part_oth_ref, t)


def _forward(own, oth, encoder, decoder, bias, active):
    return pl.pallas_call(
        _forward_kernel,
        in_specs=[WHOLE] * 6,
        out_specs=[WHOLE] * 5,
        out_shape=[
            jax.ShapeDtypeStruct((2, HALF, D), BF),
            jax.ShapeDtypeStruct((2, HALF, D), BF),
            jax.ShapeDtypeStruct((2, 2 * HALF, W), BF),
            jax.ShapeDtypeStruct((2, W, 2 * HALF), BF),
            jax.ShapeDtypeStruct((2, 2 * HALF, W), F32),
        ],
        compiler_params=_params(6),
        cost_estimate=pl.CostEstimate(
            flops=2 * 4 * 256 * D * W, bytes_accessed=2 * 256 * D * 2, transcendentals=0
        ),
        name="forward",
    )(own, oth, encoder, decoder, bias, active)


def _forward_high_kernel(codes_ref, dec_ref, part_own_ref, part_oth_ref):
    for t in (2, 3):
        _decode(t, _side(), codes_ref, dec_ref, part_own_ref, part_oth_ref, t - 2)


def _forward_high(codes, dec):
    return pl.pallas_call(
        _forward_high_kernel,
        in_specs=[WHOLE, WHOLE],
        out_specs=[WHOLE, WHOLE],
        out_shape=[jax.ShapeDtypeStruct((2, HALF, D), BF)] * 2,
        compiler_params=_params(4),
        cost_estimate=pl.CostEstimate(
            flops=2 * 3 * 256 * D * W, bytes_accessed=2 * 256 * D * 2, transcendentals=0
        ),
        name="forward_high",
    )(codes, dec)


def _join_kernel(flips, own_low_ref, own_ref, got_low_ref, got_ref, *out_refs):
    if flips == (2,):
        outs = {2: out_refs}
    else:
        outs = {flip: (out_ref, out_ref) for flip, out_ref in zip(flips, out_refs)}
    core = lax.axis_index("core")
    for flip, (first_ref, second_ref) in outs.items():
        for i in range(4):
            t, x = _place(core, lax.bitwise_xor(_me(core), flip), i)
            rows = pl.ds(pl.multiple_of(x * BOX, BOX), BOX)
            out_ref = first_ref if i < 2 else second_ref
            at = (i % 2 if flip == 2 else i) * BOX

            def add(one_ref, two_ref, index, out_ref=out_ref, at=at, rows=rows):
                value = one_ref[index, rows].astype(F32) + two_ref[index, rows].astype(F32)
                out_ref[at : at + BOX] = value.astype(out_ref.dtype)

            @pl.when(t < 2)
            def _(add=add, t=t):
                add(own_low_ref, got_low_ref, jnp.minimum(t, 1))

            @pl.when(t >= 2)
            def _(add=add, t=t):
                add(own_ref, got_ref, jnp.maximum(t - 2, 0))


def _fold_kernel(at, quarter_ref, got_ref, out_ref):
    rows = slice(at, at + QUARTER // 2)
    out_ref[rows] = (quarter_ref[rows].astype(F32) + got_ref[...].astype(F32)).astype(BF)


def _total_kernel(mine_ref, one_ref, three_ref, out_ref):
    out_ref[...] = (
        mine_ref[...] + one_ref[...].astype(F32) + three_ref[...].astype(F32)
    ).astype(BF)


def _reduce_ring(parts):
    quarter = jax.ShapeDtypeStruct((QUARTER, D), BF)
    half = jax.ShapeDtypeStruct((QUARTER // 2, D), BF)
    far1, far3 = _plain(functools.partial(_join_kernel, (2,)), [half, half], "join_far", *parts)
    mine, to1, to3 = _plain(
        functools.partial(_join_kernel, (0, 1, 3)),
        [jax.ShapeDtypeStruct((QUARTER, D), F32), quarter, quarter],
        "join",
        *parts,
    )
    got1 = lax.ppermute(far1, ALL, RING[1])
    got3 = lax.ppermute(far3, ALL, RING[3])
    to3 = _plain(functools.partial(_fold_kernel, 0), quarter, "fold_low", to3, got1, alias={0: 0})
    from3 = lax.ppermute(to3, ALL, RING[3])
    to1 = _plain(
        functools.partial(_fold_kernel, QUARTER // 2), quarter, "fold_high", to1, got3, alias={0: 0}
    )
    from1 = lax.ppermute(to1, ALL, RING[1])
    return _plain(_total_kernel, quarter, "total", mine, from1, from3)


def _half_kernel(at, quarter_ref, out_ref):
    out_ref[...] = quarter_ref[at : at + QUARTER // 2]


def _assemble_kernel(other, mine_ref, one_ref, three_ref, far1_ref, far3_ref, out_ref):
    refs = {0: (mine_ref, mine_ref), 1: (one_ref, one_ref), 3: (three_ref, three_ref), 2: (far1_ref, far3_ref)}
    core = lax.axis_index("core")
    core = 1 - core if other else core
    for flip, (first_ref, second_ref) in refs.items():
        for i in range(4):
            t, x = _place(core, lax.bitwise_xor(_me(core), flip), i)
            in_ref = first_ref if i < 2 else second_ref
            at = (i % 2 if flip == 2 else i) * BOX
            out_ref[t, pl.ds(pl.multiple_of(x * BOX, BOX), BOX)] = in_ref[at : at + BOX]


def _gather_ring(quarter, recon):
    half = jax.ShapeDtypeStruct((QUARTER // 2, D), BF)
    one = lax.ppermute(quarter, ALL, RING[1])
    three = lax.ppermute(quarter, ALL, RING[3])
    one, three, recon = lax.optimization_barrier((one, three, _around_y(recon)))
    pass3 = _plain(functools.partial(_half_kernel, 0), half, "half_low", one)
    far1 = lax.ppermute(pass3, ALL, RING[3])
    pass1 = _plain(functools.partial(_half_kernel, QUARTER // 2), half, "half_high", three)
    far3 = lax.ppermute(pass1, ALL, RING[1])
    pieces = (quarter, one, three, far1, far3)
    others = [lax.ppermute(piece, "core", SWAP) for piece in pieces]
    whole = jax.ShapeDtypeStruct((LAYERS, HALF, D), BF)
    own = _plain(functools.partial(_assemble_kernel, False), whole, "assemble_own", *pieces)
    oth = _plain(functools.partial(_assemble_kernel, True), whole, "assemble_oth", *others)
    return own, oth, recon


def _settle_kernel(pieces_ref, *rest):
    target_refs, errors_ref, recon_refs, rows_ref, turn_ref = (
        rest[:4], rest[4], rest[5:9], rest[9], rest[10]
    )
    y = lax.axis_index("y")
    for j in range(4):
        turn_ref[lax.rem(y + 4 - j, 4)] = target_refs[j][...].astype(F32)
    for j in range(4):
        rows_ref[2 * j : 2 * j + 2] = turn_ref[j]
    summed = lax.fori_loop(
        0, 16, lambda i, acc: acc + pieces_ref[i].astype(F32), jnp.zeros((8, D), F32), unroll=8
    )
    errors = (summed - rows_ref[...]).astype(BF)
    rows_ref[...] = summed
    for j in range(4):
        turn_ref[j] = rows_ref[2 * j : 2 * j + 2]
    for j in range(4):
        recon_refs[j][...] = turn_ref[lax.rem(y + j, 4)].astype(BF)

    def spread(i, carry):
        errors_ref[i] = errors
        return carry

    lax.fori_loop(0, 16, spread, 0, unroll=8)


def _settle(pieces, targets):
    return pl.pallas_call(
        _settle_kernel,
        in_specs=[WHOLE] * 5,
        out_specs=[WHOLE] * 5,
        out_shape=[jax.ShapeDtypeStruct((16, 8, D), BF)]
        + [jax.ShapeDtypeStruct((2, D), BF)] * 4,
        scratch_shapes=[pltpu.VMEM((8, D), F32), pltpu.VMEM((4, 2, D), F32)],
        compiler_params=_params(4),
        cost_estimate=pl.CostEstimate(
            flops=16 * 8 * D, bytes_accessed=2 * 16 * 8 * D * 2, transcendentals=0
        ),
        name="settle",
    )(pieces, *targets)


def _backward_kernel(
    turned_ref, slope_ref, own_ref, oth_ref, x_own_ref, x_oth_ref, dec_ref, *rest
):
    piece_refs = rest[:4]
    grad_ref, genc_ref, bias_ref, recon_ref, back_ref, pre_ref = rest[4:]
    side, y = _side(), lax.axis_index("y")
    p = pl.program_id(0)

    @pl.when(p == 0)
    def _():
        back_ref[...] = jnp.zeros_like(back_ref)
        for j in range(4):
            recon_ref[lax.rem(y + 4 - j, 4)] = piece_refs[j][...]

    @pl.when(p < PAIRS)
    def _():
        pair = jnp.minimum(p, PAIRS - 1)
        slot = (pair >= LAYERS - side).astype(jnp.int32)
        target = jnp.where(slot > 0, pair - 1, side + pair)
        err = jnp.concatenate([own_ref[target], oth_ref[target]], axis=0)
        back_ref[slot] += lax.dot_general(
            err, dec_ref[pair], (((1,), (1,)), ((), ())), preferred_element_type=F32
        )
        turned = turned_ref[slot]
        for cols in CHUNKS:
            err = jnp.concatenate([own_ref[target, :, cols], oth_ref[target, :, cols]], axis=0)
            grad_ref[0, :, cols] = jnp.dot(turned, err, preferred_element_type=F32).astype(BF)

    @pl.when(p == PAIRS)
    def _():
        for k in range(2):
            pre = (back_ref[k] * slope_ref[k]).astype(BF)
            pre_ref[k] = pre
            bias_ref[k : k + 1] = jnp.sum(pre.astype(F32), axis=0, keepdims=True)

    @pl.when(p >= PAIRS)
    def _():
        k = jnp.maximum(p - PAIRS, 0)
        own, oth = _tokens(x_own_ref, x_oth_ref, k)
        for rows in CHUNKS:
            x = jnp.concatenate([own[:, rows], oth[:, rows]], axis=0)
            genc_ref[0, rows] = lax.dot_general(
                x, pre_ref[k], (((0,), (0,)), ((), ())), preferred_element_type=F32
            ).astype(BF)


def _backward(turned, slope, own, oth, x_own, x_oth, decoder, pieces):
    return pl.pallas_call(
        _backward_kernel,
        grid=(PAIRS + 2,),
        in_specs=[WHOLE] * 11,
        out_specs=[
            pl.BlockSpec((1, W, D), lambda p: (jnp.minimum(p, PAIRS - 1), 0, 0)),
            pl.BlockSpec((1, D, W), lambda p: (jnp.maximum(p - PAIRS, 0), 0, 0)),
            pl.BlockSpec((2, W), lambda p: (0, 0)),
            pl.BlockSpec((4, 2, D), lambda p: (0, 0, 0)),
        ],
        scratch_shapes=[pltpu.VMEM((2, 2 * HALF, W), F32), pltpu.VMEM((2, 2 * HALF, W), BF)],
        out_shape=[
            jax.ShapeDtypeStruct((PAIRS, W, D), BF),
            jax.ShapeDtypeStruct((2, D, W), BF),
            jax.ShapeDtypeStruct((2, W), F32),
            jax.ShapeDtypeStruct((4, 2, D), BF),
        ],
        compiler_params=_params(12),
        cost_estimate=pl.CostEstimate(
            flops=4 * PAIRS * 256 * D * W + 4 * 256 * D * W,
            bytes_accessed=PAIRS * W * D * 2 + 2 * D * W * 2,
            transcendentals=0,
        ),
        name="backward",
    )(turned, slope, own, oth, x_own, x_oth, decoder, *pieces)


def _around_y(pieces):
    return [pieces[0]] + [
        lax.ppermute(pieces[j], "y", [(i, (i + j) % 4) for i in range(4)]) for j in (1, 2, 3)
    ]


def per_device(resid_in, resid_out, encoder, enc_bias, decoder, active):
    mine, *targets = _prepare(resid_in, resid_out)
    encoder, decoder, mine = lax.optimization_barrier((encoder, decoder, mine))
    own, (enc, dec) = _gather_inputs(mine, _stage(encoder, decoder))
    targets[1:], own = lax.optimization_barrier((targets[1:], own))
    oth = lax.ppermute(own, "core", SWAP)
    targets = _around_y(targets)
    low_own, low_oth, codes, turned, slope = _forward(own, oth, enc, dec, enc_bias, active)
    got_low = lax.ppermute(low_oth, "core", SWAP)
    part_own, part_oth = _forward_high(codes, dec)
    got = lax.ppermute(part_oth, "core", SWAP)
    quarter = _reduce_ring((low_own, part_own, got_low, got))
    quarter, targets = lax.optimization_barrier((quarter, targets))
    pieces = lax.all_to_all(quarter.reshape(16, 8, D), ALL, 0, 0, axis_index_groups=GROUPS)
    errors, *recon = _settle(pieces, targets)
    quarter = lax.all_to_all(errors, ALL, 0, 0, axis_index_groups=GROUPS).reshape(QUARTER, D)
    quarter, recon = lax.optimization_barrier((quarter, recon))
    err_own, err_oth, recon = _gather_ring(quarter, recon)
    grad_decoder, grad_encoder, grad_bias, recon = _backward(
        turned, slope, err_own, err_oth, own, oth, dec, recon
    )
    return recon, grad_encoder, grad_bias, grad_decoder


def solution(mesh):
    fine = Mesh(mesh.devices.reshape(4, 2, 2, 2, 4), ALL)
    in_specs = (
        P(None, DP, None),
        P(None, ALL, None),
        P(None, None, ALL),
        P(None, ALL),
        P(None, ALL, None),
        P(),
    )
    out_specs = (P(None, ALL, None), P(None, None, ALL), P(None, ALL), P(None, ALL, None))
    return jax.shard_map(
        per_device, mesh=fine, in_specs=in_specs, out_specs=out_specs, check_vma=False
    )
```

```python
import functools

import jax
import jax.numpy as jnp
from jax import lax
from jax.experimental import pallas as pl
from jax.experimental.pallas import tpu as pltpu
from jax.sharding import Mesh
from jax.sharding import PartitionSpec as P

FEAT = 16384
BLOCK = 128
LAYERS = 4
D = 3584
W = 256
HALF = 128
TILES = 8
HROW = 16
PAIRS = 5
DP = ("zh", "y")
ALL = ("x", "zl", "core", "zh", "y")
BF = jnp.bfloat16
F32 = jnp.float32
SWAP = [(0, 1), (1, 0)]
QUARTER = 128
BOX = 32


def _rank(x, zl, core, zh, y):
    return (((x * 2 + zl) * 2 + core) * 2 + zh) * 4 + y


def _pairs(move):
    return [
        (_rank(x, zl, core, zh, y), _rank(*move(x, zl, core, zh, y)))
        for x in range(4)
        for zl in range(2)
        for core in range(2)
        for zh in range(2)
        for y in range(4)
    ]


def _ring(flip):
    return _pairs(
        lambda x, zl, core, zh, y: (x ^ (flip * core), zl, core, zh, y ^ (flip * (1 - core)))
    )


RING = {flip: _ring(flip) for flip in (1, 3)}
ALONG_Y = {
    flip: _pairs(
        lambda x, zl, core, zh, y, flip=flip: (x, zl, core, zh, y ^ (4 - flip if core else flip))
    )
    for flip in (1, 3)
}
ACROSS = _pairs(lambda x, zl, core, zh, y: (x, zl ^ 1, core, zh ^ 1, y))
GROUPS = [
    [_rank(x, zl, 0, zh, y) for x in range(4) for zl in range(2) for zh in range(2)] for y in range(4)
] + [
    [_rank(x, zl, 1, zh, y) for y in range(4) for zl in range(2) for zh in range(2)] for x in range(4)
]

VMEM = pltpu.MemorySpace.VMEM
HBM = pltpu.MemorySpace.HBM
WHOLE = pl.BlockSpec(memory_space=VMEM)
CHUNK = 512
CHUNKS = [slice(c, c + CHUNK) for c in range(0, D, CHUNK)]


def _hbm(x):
    return pltpu.with_memory_space_constraint(x, HBM)


def _vmem(x):
    return pltpu.with_memory_space_constraint(x, VMEM)


def _params(mib):
    return pltpu.CompilerParams(vmem_limit_bytes=mib << 20)


def _tokens(own_ref, oth_ref, k):
    return own_ref[:, k].reshape(HALF, D), oth_ref[:, k].reshape(HALF, D)


def _side():
    return lax.axis_index("x") // 2


def _prepare_kernel(in_hbm, out_hbm, mine_ref, *rest):
    piece_refs, sem = rest[:4], rest[4]
    side, core, y = _side(), lax.axis_index("core"), lax.axis_index("y")
    rows = pl.ds(pl.multiple_of(core * HROW, HROW), HROW)
    copies = [
        pltpu.make_async_copy(in_hbm.at[layer, rows], mine_ref.at[k], sem.at[k])
        for k, layer in enumerate((side, LAYERS - 1 - side))
    ] + [
        pltpu.make_async_copy(out_hbm.at[lax.rem(y + j, 4)], piece_refs[j], sem.at[2 + j])
        for j in range(4)
    ]
    for copy in copies:
        copy.start()
    for copy in copies:
        copy.wait()


def _prepare(resid_in, resid_out):
    return pl.pallas_call(
        _prepare_kernel,
        in_specs=[pl.BlockSpec(memory_space=HBM)] * 2,
        out_specs=[WHOLE] * 5,
        out_shape=[jax.ShapeDtypeStruct((2, HROW, D), BF)] + [jax.ShapeDtypeStruct((2, D), BF)] * 4,
        scratch_shapes=[pltpu.SemaphoreType.DMA((6,))],
        compiler_params=_params(2),
        name="prepare",
    )(_hbm(resid_in), _hbm(resid_out))


def _plain(kernel, out_shape, name, *operands, scratch=(), alias=None):
    return pl.pallas_call(
        kernel,
        in_specs=[WHOLE] * len(operands),
        out_specs=jax.tree.map(lambda _: WHOLE, out_shape),
        out_shape=out_shape,
        scratch_shapes=scratch,
        input_output_aliases=alias or {},
        compiler_params=_params(4),
        name=name,
    )(*operands)


TILE_FROM = ((0, 0), (0, 1), (0, 3), (0, 2), (1, 0), (1, 1), (1, 3), (1, 2))


def _arrange_kernel(*refs):
    zh, y = lax.axis_index("zh"), lax.axis_index("y")
    core = lax.axis_index("core")
    for piece_ref, (across, flip) in zip(refs[:TILES], TILE_FROM):
        flip = jnp.where(core == 0, flip, (4 - flip) % 4)
        tile = lax.rem(zh + across, 2) * 4 + lax.bitwise_xor(y, flip)
        refs[TILES][tile] = piece_ref[...]


def _gather_inputs(mine, staged):
    far = lax.ppermute(mine, ALL, ACROSS)
    mine_1, mine_3 = (lax.ppermute(mine, ALL, ALONG_Y[flip]) for flip in (1, 3))
    far, mine_1, mine_3, staged = lax.optimization_barrier((far, mine_1, mine_3, staged))
    far_3, far_1 = (lax.ppermute(far, ALL, ALONG_Y[flip]) for flip in (3, 1))
    mine_2 = lax.ppermute(mine_1, ALL, ALONG_Y[3])
    far_2 = lax.ppermute(far_3, ALL, ALONG_Y[1])
    own = _plain(
        _arrange_kernel,
        jax.ShapeDtypeStruct((TILES, 2, HROW, D), BF),
        "arrange",
        mine, mine_1, mine_3, mine_2, far, far_1, far_3, far_2,
    )
    return own, staged


def _place(core, quarter, i):
    return jnp.where(core == 0, quarter, i), jnp.where(core == 0, i, quarter)


def _me(core):
    return jnp.where(core == 0, lax.axis_index("y"), lax.axis_index("x"))


def _decode(t, side, codes_ref, dec_ref, own_ref, oth_ref, at):
    has_first = t >= side
    has_second = t + 1 >= LAYERS - side
    one = jnp.maximum(t - side, 0)

    def sweep(part):
        for cols in CHUNKS:
            value = part(cols).astype(BF)
            own_ref[at, :, cols] = value[:HALF]
            oth_ref[at, :, cols] = value[HALF:]

    def first(cols):
        return jnp.dot(codes_ref[0], dec_ref[one, :, cols], preferred_element_type=F32)

    def both(cols):
        return first(cols) + jnp.dot(
            codes_ref[1], dec_ref[t + 1, :, cols], preferred_element_type=F32
        )

    @pl.when(has_second)
    def _():
        sweep(both)

    @pl.when(jnp.logical_and(has_first, jnp.logical_not(has_second)))
    def _():
        sweep(first)

    @pl.when(jnp.logical_not(has_first))
    def _():
        own_ref[at] = jnp.zeros((HALF, D), BF)
        oth_ref[at] = jnp.zeros((HALF, D), BF)


def _stage_kernel(enc_hbm, dec_hbm, enc_ref, dec_ref, sem):
    copies = [
        pltpu.make_async_copy(enc_hbm, enc_ref, sem.at[0]),
        pltpu.make_async_copy(dec_hbm, dec_ref, sem.at[1]),
    ]
    for copy in copies:
        copy.start()
    for copy in copies:
        copy.wait()


def _stage(encoder, decoder):
    return pl.pallas_call(
        _stage_kernel,
        in_specs=[pl.BlockSpec(memory_space=HBM)] * 2,
        out_specs=[WHOLE, WHOLE],
        out_shape=[
            jax.ShapeDtypeStruct((2, D, W), BF),
            jax.ShapeDtypeStruct((PAIRS, W, D), BF),
        ],
        scratch_shapes=[pltpu.SemaphoreType.DMA((2,))],
        compiler_params=_params(1),
        cost_estimate=pl.CostEstimate(
            flops=0, bytes_accessed=2 * (2 * D * W + PAIRS * W * D) * 2, transcendentals=0
        ),
        name="stage",
    )(_hbm(encoder), _hbm(decoder))


def _forward_kernel(
    own_ref, oth_ref, enc_ref, dec_ref, bias_ref, active_ref,
    part_own_ref, part_oth_ref, codes_ref, turned_ref, slope_ref,
):
    x, zl, core = lax.axis_index("x"), lax.axis_index("zl"), lax.axis_index("core")
    zh, y = lax.axis_index("zh"), lax.axis_index("y")
    side = _side()
    rank = (((x * 2 + zl) * 2 + core) * 2 + zh) * 4 + y
    block = rank * (W // BLOCK) - side * (FEAT // BLOCK)
    for k, layer in enumerate((side, LAYERS - 1 - side)):
        rows = jnp.concatenate(_tokens(own_ref, oth_ref, k), axis=0)
        listed = active_ref[layer]
        keep = [
            jnp.broadcast_to(
                jnp.max((listed == block + b).astype(F32), axis=1, keepdims=True), (TILES, BLOCK)
            )
            for b in range(W // BLOCK)
        ]
        keep = jnp.concatenate(keep, axis=1)
        keep = jnp.broadcast_to(keep[:, None, :], (TILES, HROW, W)).reshape(HALF, W)
        keep = jnp.concatenate([keep, keep], axis=0)
        pre = jnp.dot(rows, enc_ref[k], preferred_element_type=F32) + bias_ref[k : k + 1]
        positive = jnp.maximum(pre, 0.0)
        kept = keep * positive
        codes = kept * positive
        codes_ref[k] = codes.astype(BF)
        turned_ref[k] = codes.T.astype(BF)
        slope_ref[k] = 2.0 * kept
    for t in (0, 1):
        _decode(t, side, codes_ref, dec_ref, part_own_ref, part_oth_ref, t)


def _forward(own, oth, encoder, decoder, bias, active):
    return pl.pallas_call(
        _forward_kernel,
        in_specs=[WHOLE] * 6,
        out_specs=[WHOLE] * 5,
        out_shape=[
            jax.ShapeDtypeStruct((2, HALF, D), BF),
            jax.ShapeDtypeStruct((2, HALF, D), BF),
            jax.ShapeDtypeStruct((2, 2 * HALF, W), BF),
            jax.ShapeDtypeStruct((2, W, 2 * HALF), BF),
            jax.ShapeDtypeStruct((2, 2 * HALF, W), F32),
        ],
        compiler_params=_params(6),
        cost_estimate=pl.CostEstimate(
            flops=2 * 4 * 256 * D * W, bytes_accessed=2 * 256 * D * 2, transcendentals=0
        ),
        name="forward",
    )(own, oth, encoder, decoder, bias, active)


def _forward_high_kernel(codes_ref, dec_ref, part_own_ref, part_oth_ref):
    for t in (2, 3):
        _decode(t, _side(), codes_ref, dec_ref, part_own_ref, part_oth_ref, t - 2)


def _forward_high(codes, dec):
    return pl.pallas_call(
        _forward_high_kernel,
        in_specs=[WHOLE, WHOLE],
        out_specs=[WHOLE, WHOLE],
        out_shape=[jax.ShapeDtypeStruct((2, HALF, D), BF)] * 2,
        compiler_params=_params(4),
        cost_estimate=pl.CostEstimate(
            flops=2 * 3 * 256 * D * W, bytes_accessed=2 * 256 * D * 2, transcendentals=0
        ),
        name="forward_high",
    )(codes, dec)


def _join_kernel(flips, own_low_ref, own_ref, got_low_ref, got_ref, *out_refs):
    if flips == (2,):
        outs = {2: out_refs}
    else:
        outs = {flip: (out_ref, out_ref) for flip, out_ref in zip(flips, out_refs)}
    core = lax.axis_index("core")
    for flip, (first_ref, second_ref) in outs.items():
        for i in range(4):
            t, x = _place(core, lax.bitwise_xor(_me(core), flip), i)
            rows = pl.ds(pl.multiple_of(x * BOX, BOX), BOX)
            out_ref = first_ref if i < 2 else second_ref
            at = (i % 2 if flip == 2 else i) * BOX

            def add(one_ref, two_ref, index, out_ref=out_ref, at=at, rows=rows):
                value = one_ref[index, rows].astype(F32) + two_ref[index, rows].astype(F32)
                out_ref[at : at + BOX] = value.astype(out_ref.dtype)

            @pl.when(t < 2)
            def _(add=add, t=t):
                add(own_low_ref, got_low_ref, jnp.minimum(t, 1))

            @pl.when(t >= 2)
            def _(add=add, t=t):
                add(own_ref, got_ref, jnp.maximum(t - 2, 0))


def _fold_kernel(at, quarter_ref, got_ref, out_ref):
    rows = slice(at, at + QUARTER // 2)
    out_ref[rows] = (quarter_ref[rows].astype(F32) + got_ref[...].astype(F32)).astype(BF)


def _total_kernel(mine_ref, one_ref, three_ref, out_ref):
    out_ref[...] = (
        mine_ref[...] + one_ref[...].astype(F32) + three_ref[...].astype(F32)
    ).astype(BF)


def _reduce_ring(parts):
    quarter = jax.ShapeDtypeStruct((QUARTER, D), BF)
    half = jax.ShapeDtypeStruct((QUARTER // 2, D), BF)
    far1, far3 = _plain(functools.partial(_join_kernel, (2,)), [half, half], "join_far", *parts)
    mine, to1, to3 = _plain(
        functools.partial(_join_kernel, (0, 1, 3)),
        [jax.ShapeDtypeStruct((QUARTER, D), F32), quarter, quarter],
        "join",
        *parts,
    )
    got1 = lax.ppermute(far1, ALL, RING[1])
    got3 = lax.ppermute(far3, ALL, RING[3])
    to3 = _plain(functools.partial(_fold_kernel, 0), quarter, "fold_low", to3, got1, alias={0: 0})
    from3 = lax.ppermute(to3, ALL, RING[3])
    to1 = _plain(
        functools.partial(_fold_kernel, QUARTER // 2), quarter, "fold_high", to1, got3, alias={0: 0}
    )
    from1 = lax.ppermute(to1, ALL, RING[1])
    return _plain(_total_kernel, quarter, "total", mine, from1, from3)


def _half_kernel(at, quarter_ref, out_ref):
    out_ref[...] = quarter_ref[at : at + QUARTER // 2]


def _assemble_kernel(other, mine_ref, one_ref, three_ref, far1_ref, far3_ref, out_ref):
    refs = {0: (mine_ref, mine_ref), 1: (one_ref, one_ref), 3: (three_ref, three_ref), 2: (far1_ref, far3_ref)}
    core = lax.axis_index("core")
    core = 1 - core if other else core
    for flip, (first_ref, second_ref) in refs.items():
        for i in range(4):
            t, x = _place(core, lax.bitwise_xor(_me(core), flip), i)
            in_ref = first_ref if i < 2 else second_ref
            at = (i % 2 if flip == 2 else i) * BOX
            out_ref[t, pl.ds(pl.multiple_of(x * BOX, BOX), BOX)] = in_ref[at : at + BOX]


def _gather_ring(quarter, recon):
    half = jax.ShapeDtypeStruct((QUARTER // 2, D), BF)
    one = lax.ppermute(quarter, ALL, RING[1])
    three = lax.ppermute(quarter, ALL, RING[3])
    one, three, recon = lax.optimization_barrier((one, three, _around_y(recon)))
    pass3 = _plain(functools.partial(_half_kernel, 0), half, "half_low", one)
    far1 = lax.ppermute(pass3, ALL, RING[3])
    pass1 = _plain(functools.partial(_half_kernel, QUARTER // 2), half, "half_high", three)
    far3 = lax.ppermute(pass1, ALL, RING[1])
    pieces = (quarter, one, three, far1, far3)
    others = [lax.ppermute(piece, "core", SWAP) for piece in pieces]
    whole = jax.ShapeDtypeStruct((LAYERS, HALF, D), BF)
    own = _plain(functools.partial(_assemble_kernel, False), whole, "assemble_own", *pieces)
    oth = _plain(functools.partial(_assemble_kernel, True), whole, "assemble_oth", *others)
    return own, oth, recon


def _settle_kernel(pieces_ref, *rest):
    target_refs, errors_ref, recon_refs, rows_ref, turn_ref = (
        rest[:4], rest[4], rest[5:9], rest[9], rest[10]
    )
    y = lax.axis_index("y")
    for j in range(4):
        turn_ref[lax.rem(y + 4 - j, 4)] = target_refs[j][...].astype(F32)
    for j in range(4):
        rows_ref[2 * j : 2 * j + 2] = turn_ref[j]
    summed = lax.fori_loop(
        0, 16, lambda i, acc: acc + pieces_ref[i].astype(F32), jnp.zeros((8, D), F32), unroll=8
    )
    errors = (summed - rows_ref[...]).astype(BF)
    rows_ref[...] = summed
    for j in range(4):
        turn_ref[j] = rows_ref[2 * j : 2 * j + 2]
    for j in range(4):
        recon_refs[j][...] = turn_ref[lax.rem(y + j, 4)].astype(BF)

    def spread(i, carry):
        errors_ref[i] = errors
        return carry

    lax.fori_loop(0, 16, spread, 0, unroll=8)


def _settle(pieces, targets):
    return pl.pallas_call(
        _settle_kernel,
        in_specs=[WHOLE] * 5,
        out_specs=[WHOLE] * 5,
        out_shape=[jax.ShapeDtypeStruct((16, 8, D), BF)]
        + [jax.ShapeDtypeStruct((2, D), BF)] * 4,
        scratch_shapes=[pltpu.VMEM((8, D), F32), pltpu.VMEM((4, 2, D), F32)],
        compiler_params=_params(4),
        cost_estimate=pl.CostEstimate(
            flops=16 * 8 * D, bytes_accessed=2 * 16 * 8 * D * 2, transcendentals=0
        ),
        name="settle",
    )(pieces, *targets)


def _backward_kernel(
    turned_ref, slope_ref, own_ref, oth_ref, x_own_ref, x_oth_ref, dec_ref, *rest
):
    piece_refs = rest[:4]
    grad_ref, genc_ref, bias_ref, recon_ref, back_ref, pre_ref = rest[4:]
    side, y = _side(), lax.axis_index("y")
    p = pl.program_id(0)

    @pl.when(p == 0)
    def _():
        back_ref[...] = jnp.zeros_like(back_ref)
        for j in range(4):
            recon_ref[lax.rem(y + 4 - j, 4)] = piece_refs[j][...]

    @pl.when(p < PAIRS)
    def _():
        pair = jnp.minimum(p, PAIRS - 1)
        slot = (pair >= LAYERS - side).astype(jnp.int32)
        target = jnp.where(slot > 0, pair - 1, side + pair)
        err = jnp.concatenate([own_ref[target], oth_ref[target]], axis=0)
        back_ref[slot] += lax.dot_general(
            err, dec_ref[pair], (((1,), (1,)), ((), ())), preferred_element_type=F32
        )
        turned = turned_ref[slot]
        for cols in CHUNKS:
            err = jnp.concatenate([own_ref[target, :, cols], oth_ref[target, :, cols]], axis=0)
            grad_ref[0, :, cols] = jnp.dot(turned, err, preferred_element_type=F32).astype(BF)

    @pl.when(p == PAIRS)
    def _():
        for k in range(2):
            pre = (back_ref[k] * slope_ref[k]).astype(BF)
            pre_ref[k] = pre
            bias_ref[k : k + 1] = jnp.sum(pre.astype(F32), axis=0, keepdims=True)

    for late in range(2):

        @pl.when(jnp.logical_and(p >= PAIRS, lax.rem(jnp.maximum(p - PAIRS, 0), 2) == late))
        def _(late=late):
            k = jnp.maximum(p - PAIRS, 0) // 2
            own, oth = _tokens(x_own_ref, x_oth_ref, k)
            for at in range(0, D // 2, W):
                rows = slice(late * (D // 2) + at, late * (D // 2) + at + W)
                x = jnp.concatenate([own[:, rows], oth[:, rows]], axis=0)
                genc_ref[0, at : at + W] = lax.dot_general(
                    x, pre_ref[k], (((0,), (0,)), ((), ())), preferred_element_type=F32
                ).astype(BF)


def _backward(turned, slope, own, oth, x_own, x_oth, decoder, pieces):
    return pl.pallas_call(
        _backward_kernel,
        grid=(PAIRS + 4,),
        in_specs=[WHOLE] * 11,
        out_specs=[
            pl.BlockSpec((1, W, D), lambda p: (jnp.minimum(p, PAIRS - 1), 0, 0)),
            pl.BlockSpec(
                (1, D // 2, W),
                lambda p: (jnp.maximum(p - PAIRS, 0) // 2, lax.rem(jnp.maximum(p - PAIRS, 0), 2), 0),
            ),
            pl.BlockSpec((2, W), lambda p: (0, 0)),
            pl.BlockSpec((4, 2, D), lambda p: (0, 0, 0)),
        ],
        scratch_shapes=[pltpu.VMEM((2, 2 * HALF, W), F32), pltpu.VMEM((2, 2 * HALF, W), BF)],
        out_shape=[
            jax.ShapeDtypeStruct((PAIRS, W, D), BF),
            jax.ShapeDtypeStruct((2, D, W), BF),
            jax.ShapeDtypeStruct((2, W), F32),
            jax.ShapeDtypeStruct((4, 2, D), BF),
        ],
        compiler_params=_params(12),
        cost_estimate=pl.CostEstimate(
            flops=4 * PAIRS * 256 * D * W + 4 * 256 * D * W,
            bytes_accessed=PAIRS * W * D * 2 + 2 * D * W * 2,
            transcendentals=0,
        ),
        name="backward",
    )(turned, slope, own, oth, x_own, x_oth, decoder, *pieces)


def _around_y(pieces):
    return [pieces[0]] + [
        lax.ppermute(pieces[j], "y", [(i, (i + j) % 4) for i in range(4)]) for j in (1, 2, 3)
    ]


def per_device(resid_in, resid_out, encoder, enc_bias, decoder, active):
    mine, *targets = _prepare(resid_in, resid_out)
    encoder, decoder, mine = lax.optimization_barrier((encoder, decoder, mine))
    own, (enc, dec) = _gather_inputs(mine, _stage(encoder, decoder))
    targets[1:], own = lax.optimization_barrier((targets[1:], own))
    oth = lax.ppermute(own, "core", SWAP)
    targets = _around_y(targets)
    low_own, low_oth, codes, turned, slope = _forward(own, oth, enc, dec, enc_bias, active)
    got_low = lax.ppermute(low_oth, "core", SWAP)
    part_own, part_oth = _forward_high(codes, dec)
    got = lax.ppermute(part_oth, "core", SWAP)
    quarter = _reduce_ring((low_own, part_own, got_low, got))
    quarter, targets = lax.optimization_barrier((quarter, targets))
    pieces = lax.all_to_all(quarter.reshape(16, 8, D), ALL, 0, 0, axis_index_groups=GROUPS)
    errors, *recon = _settle(pieces, targets)
    quarter = lax.all_to_all(errors, ALL, 0, 0, axis_index_groups=GROUPS).reshape(QUARTER, D)
    quarter, recon = lax.optimization_barrier((quarter, recon))
    err_own, err_oth, recon = _gather_ring(quarter, recon)
    grad_decoder, grad_encoder, grad_bias, recon = _backward(
        turned, slope, err_own, err_oth, own, oth, dec, recon
    )
    return recon, grad_encoder, grad_bias, grad_decoder


def solution(mesh):
    fine = Mesh(mesh.devices.reshape(4, 2, 2, 2, 4), ALL)
    in_specs = (
        P(None, DP, None),
        P(None, ALL, None),
        P(None, None, ALL),
        P(None, ALL),
        P(None, ALL, None),
        P(),
    )
    out_specs = (P(None, ALL, None), P(None, None, ALL), P(None, ALL), P(None, ALL, None))
    return jax.shard_map(
        per_device, mesh=fine, in_specs=in_specs, out_specs=out_specs, check_vma=False
    )
```
